32 devices in a mesh: groups: 2 (over y), tx: 4 (over z), ty: 4 (over x, core).
Axes of the slice: x: 2, y: 2, z: 4, core: 2. Of those that a mesh axis runs over, the one named last changes fastest.
Arguments:
- object_field: float32 [4, 256, 512], P('groups', 'tx', 'ty'), parts along dimension 0, may hold values from -4 to 4
- probe_modes: float32 [4, 8, 128, 128], P('groups'), parts along dimension 0, may hold values from -3 to 3
- positions: int32 [192, 2], P(('groups', 'tx', 'ty')), parts along dimension 0, may hold values from 0 to 384, as said below
- counts: int32 [32], P(('groups', 'tx', 'ty')), parts along dimension 0, may hold values from 1 to 6, as said below
- intensity: float32 [192, 128, 128], P(('groups', 'tx', 'ty')), parts along dimension 0, may hold values from 0.5 to 20
Outputs:
- object_out: float32 [4, 256, 512], P('groups', 'tx', 'ty'), parts along dimension 0
- probe_out: float32 [4, 8, 128, 128], P('groups'), parts along dimension 0
The draws below stay inside these ranges and needn't reach their ends.
There are 2 independent parts, one for each index of `groups`. The reference program is written for one: setup_inputs(seed, part) draws one part's arguments, and reference() takes and returns one part's arrays. A program takes and returns all parts, laid end to end along the dimension named above; each array names one. Nothing has to cross between parts.
Inputs may be any that keep to these rules, and one draw needn't show every extreme that they name: `positions`: slot s belongs to tile t = s // 6, which covers object rows from (t // 4) * 64 on (64 rows) and columns from (t % 4) * 128 on (128 columns). The window of slot s, rows row to row + 127 and columns col to col + 127, lies inside the object and inside its tile widened by 64 pixels on every side. Tile t's live slots are its first counts[t] slots; the other slots are unused and their positions and intensity carry no meaning. Some tile has all 6 slots live.
All inputs are finite; a program needn't handle non-finite values.
Results may differ from the reference program's by a relative error of at most 0.0001.
Values sent between devices are 32-bit elements; how exact they have to be, the bound alone decides.
A program may use at most 64 MiB of HBM per device.

```python
import math
import jax
import jax.numpy as jnp
from jax import lax

P_SIZE = 128
MODES = 8
TH = 64
TW = 128
CAP = 6
ITERS = 2
NH = 256
NW = 512
TILES = 16
SLOTS = 96


def draw_positions(key, part):
    slot_ids = jnp.arange(SLOTS, dtype=jnp.int32)
    tile_of = slot_ids // CAP
    tiles_across = NW // TW
    row_low = tile_of // tiles_across * TH
    col_low = tile_of % tiles_across * TW
    row_center = row_low + jax.random.randint(jax.random.fold_in(key, 11), (SLOTS,), 0, TH, dtype=jnp.int32)
    col_center = col_low + jax.random.randint(jax.random.fold_in(key, 12), (SLOTS,), 0, TW, dtype=jnp.int32)
    margin = P_SIZE // 2
    row_start = jnp.clip(row_center - margin, 0, NH - P_SIZE)
    col_start = jnp.clip(col_center - margin, 0, NW - P_SIZE)
    return jnp.stack([row_start, col_start], axis=1).astype(jnp.int32)


def draw_counts(key, part):
    baseline = jax.random.randint(jax.random.fold_in(key, 21), (TILES,), 1, CAP // 2 + 1, dtype=jnp.int32)
    filled = jax.random.randint(jax.random.fold_in(key, 22), (TILES,), 0, 8, dtype=jnp.int32) == 0
    chosen = jnp.arange(TILES, dtype=jnp.int32) == jax.random.randint(jax.random.fold_in(key, 23), (), 0, TILES, dtype=jnp.int32)
    return jnp.where(filled | chosen, CAP, baseline).astype(jnp.int32)


def level_of(own_key, dims, split, smallest, largest):
    loudness = 1.0
    for dim, shards_of in split:
        heights = jax.random.uniform(jax.random.fold_in(jax.random.fold_in(own_key, 6), dim), (shards_of,), jnp.float32, smallest / len(split), largest / len(split))
        loudness = loudness * jnp.repeat(jnp.exp(heights), dims[dim] // shards_of).reshape((-1,) + (1,) * (len(dims) - 1 - dim))
    return loudness


def centred(stream_key, dims, deviation, reach, pieces=(), kind=jnp.bfloat16):
    result = deviation * jax.random.normal(stream_key, dims, jnp.float32)
    if pieces:
        result = result * level_of(stream_key, dims, pieces, -0.22, 0.18)
    return jnp.clip(result, -reach, reach).astype(kind)


def setup_inputs(seed: int = 0, part: int = 0) -> dict:
    key_of = jax.random.split(jax.random.key(seed), 6)
    part_splits = jax.random.split(jax.random.fold_in(key_of[5], part), 6)
    object_field = centred(part_splits[0], (2, NH, NW), 0.7, 4.0, ((1, 4), (2, 4)), jnp.float32)
    probe_modes = centred(part_splits[1], (2, MODES, P_SIZE, P_SIZE), 0.5, 3.0, (), jnp.float32)
    positions = draw_positions(jax.random.fold_in(jax.random.fold_in(key_of[5], part), 71), part)
    counts = draw_counts(jax.random.fold_in(jax.random.fold_in(key_of[5], part), 71), part)
    intensity = jnp.clip(jnp.exp(math.log(20.0) - 3.6888795 * jax.random.uniform(part_splits[4], (SLOTS, P_SIZE, P_SIZE), jnp.float32) ** level_of(part_splits[4], (SLOTS, P_SIZE, P_SIZE), ((0, 16),), -0.2, 0.2)), 0.5, 20.0)
    return dict(object_field=object_field, probe_modes=probe_modes, positions=positions, counts=counts, intensity=intensity)


precise = lax.Precision.HIGHEST

def tables(length):
    indices = jnp.arange(length, dtype=jnp.int32)
    phases = indices[:, None] * indices[None, :] % length
    angles = phases.astype(jnp.float32) * (2.0 * jnp.pi / length)
    normal_scale = 1.0 / jnp.sqrt(jnp.float32(length))
    return (jnp.cos(angles) * normal_scale, jnp.sin(angles) * normal_scale)

def transform(real_part, imag_part, cos_table, sin_table):
    left_r = jnp.einsum('ab,mbc->mac', cos_table, real_part, precision=precise) - jnp.einsum('ab,mbc->mac', sin_table, imag_part, precision=precise)
    left_i = jnp.einsum('ab,mbc->mac', cos_table, imag_part, precision=precise) + jnp.einsum('ab,mbc->mac', sin_table, real_part, precision=precise)
    out_r = jnp.einsum('mab,bc->mac', left_r, cos_table, precision=precise) - jnp.einsum('mab,bc->mac', left_i, sin_table, precision=precise)
    out_i = jnp.einsum('mab,bc->mac', left_i, cos_table, precision=precise) + jnp.einsum('mab,bc->mac', left_r, sin_table, precision=precise)
    return (out_r, out_i)

def exit_update(window, probes, measured, cos_table, sin_table):
    obj_r, obj_i = (window[0], window[1])
    probe_r, probe_i = (probes[0], probes[1])
    wave_r = probe_r * obj_r - probe_i * obj_i
    wave_i = probe_r * obj_i + probe_i * obj_r
    far_r, far_i = transform(wave_r, wave_i, cos_table, -sin_table)
    modelled = lax.optimization_barrier(jnp.sum(far_r * far_r + far_i * far_i, axis=0))
    factor = jnp.sqrt(measured / jnp.maximum(modelled, 1.0))
    back_r, back_i = transform(far_r * factor, far_i * factor, cos_table, sin_table)
    return (back_r - wave_r, back_i - wave_i)

def slot_terms(window, probes, lighting, change_r, change_i, weight):
    obj_r, obj_i = (window[0], window[1])
    probe_r, probe_i = (probes[0], probes[1])
    object_terms = jnp.stack([lax.optimization_barrier(jnp.sum(probe_r * change_r + probe_i * change_i, axis=0)), lax.optimization_barrier(jnp.sum(probe_r * change_i - probe_i * change_r, axis=0)), lighting]) * weight
    probe_terms = jnp.stack([obj_r * change_r + obj_i * change_i, obj_r * change_i - obj_i * change_r]) * weight
    coverage = (obj_r * obj_r + obj_i * obj_i) * weight
    return (object_terms, probe_terms, coverage)

def accumulate(object_map, probes, starts, active, intensity, cos_table, sin_table):
    length = probes.shape[-1]
    lighting = lax.optimization_barrier(jnp.sum(probes[0] * probes[0] + probes[1] * probes[1], axis=0))
    anchor_index = jnp.int32(0)

    def visit_slot(carried, element):
        totals, probe_sum, probe_weight = carried
        corner_at, weight, measured = element
        corner = (anchor_index, corner_at[0], corner_at[1])
        window = lax.dynamic_slice(object_map, corner, (2, length, length))
        change_r, change_i = exit_update(window, probes, measured, cos_table, sin_table)
        object_terms, probe_terms, coverage = slot_terms(window, probes, lighting, change_r, change_i, weight)
        region = lax.dynamic_slice(totals, corner, (3, length, length))
        totals = lax.dynamic_update_slice(totals, region + object_terms, corner)
        return ((totals, probe_sum + probe_terms, probe_weight + coverage), None)
    initial = (jnp.zeros((3,) + object_map.shape[1:], jnp.float32), jnp.zeros(probes.shape, jnp.float32), jnp.zeros((length, length), jnp.float32))
    (totals, probe_sum, probe_weight), _ = lax.scan(visit_slot, initial, (starts, active, intensity))
    return (totals, probe_sum, probe_weight)

def mixing(probes, probe_step):
    mix_r = lax.optimization_barrier(jnp.sum(probes[0] * probe_step[0] + probes[1] * probe_step[1], axis=0))
    mix_i = lax.optimization_barrier(jnp.sum(probes[0] * probe_step[1] - probes[1] * probe_step[0], axis=0))
    return (mix_r, mix_i)

def cross_term(object_map, change, starts, active, mix_r, mix_i):
    length = mix_r.shape[-1]
    anchor_index = jnp.int32(0)

    def visit_slot(running, element):
        corner_at, weight = element
        corner = (anchor_index, corner_at[0], corner_at[1])
        object_win = lax.dynamic_slice(object_map, corner, (2, length, length))
        change_win = lax.dynamic_slice(change, corner, (2, length, length))
        aligned = change_win[0] * object_win[0] + change_win[1] * object_win[1]
        rotated = change_win[0] * object_win[1] - change_win[1] * object_win[0]
        return (running + weight * jnp.sum(aligned * mix_r - rotated * mix_i), None)
    running, _ = lax.scan(visit_slot, jnp.zeros((), jnp.float32), (starts, active))
    return running

def solve_steps(object_curve, cross_curve, probe_curve, object_slope, probe_slope):
    object_diag = 1.1 * object_curve + 0.001
    probe_diag = 1.1 * probe_curve + 0.001
    determinant = object_diag * probe_diag - cross_curve * cross_curve
    object_rate = (probe_diag * object_slope - cross_curve * probe_slope) / determinant
    probe_rate = (object_diag * probe_slope - cross_curve * object_slope) / determinant
    return (object_rate, probe_rate)

def reference(object_field, probe_modes, positions, counts, intensity):
    length = probe_modes.shape[-1]
    cos_table, sin_table = tables(length)
    slot_ids = jnp.arange(positions.shape[0], dtype=jnp.int32)
    active = (slot_ids % CAP < counts[slot_ids // CAP]).astype(jnp.float32)
    object_map = object_field
    probes = probe_modes
    for repeat in range(ITERS):
        totals, probe_sum, probe_weight = accumulate(object_map, probes, positions, active, intensity, cos_table, sin_table)
        change = totals[:2] / jnp.maximum(totals[2], 1.0)
        probe_step = probe_sum / (probe_weight + 1e-05)
        object_curve = jnp.sum((change[0] * change[0] + change[1] * change[1]) * totals[2])
        object_slope = jnp.sum(totals[:2] * change)
        probe_curve = jnp.sum((probe_step[0] * probe_step[0] + probe_step[1] * probe_step[1]) * probe_weight)
        probe_slope = jnp.sum(probe_sum * probe_step)
        mix_r, mix_i = mixing(probes, probe_step)
        cross_curve = cross_term(object_map, change, positions, active, mix_r, mix_i)
        object_rate, probe_rate = solve_steps(object_curve, cross_curve, probe_curve, object_slope, probe_slope)
        object_map = object_map + object_rate * change
        probes = probes + probe_rate * probe_step
    return (object_map, probes)
```

```python
import functools

import jax
import jax.numpy as jnp
import ml_dtypes
import numpy as np
from jax import lax
from jax.experimental import pallas as pl
from jax.experimental.pallas import tpu as pltpu
from jax.sharding import PartitionSpec as P

ITERS = 2
memory = pl.BlockSpec(memory_space=pltpu.VMEM)
scalars = pl.BlockSpec(memory_space=pltpu.SMEM)


def with_halo(value, sides, width):
    for axis, dim in sides:
        size, length = (lax.axis_size(axis), value.shape[dim])
        up = [(i, (i + 1) % size) for i in range(size - 1)]
        down = [(j, i) for i, j in up]
        last = lax.slice_in_dim(value, length - width, length, axis=dim)
        first = lax.slice_in_dim(value, 0, width, axis=dim)
        before = lax.ppermute(last, axis, up)
        after = lax.ppermute(first, axis, down)
        value = jnp.concatenate([before, value, after], axis=dim)
    return value


def from_behind(block, axis, distance):
    devices = range(lax.axis_size(axis))
    route = [(i - distance, i) for i in devices if i - distance in devices]
    return lax.ppermute(block, axis, route)


def split_tables(length):
    indices = np.arange(length)
    angles = (indices[:, None] * indices[None, :] % length) * (2.0 * np.pi / length)
    cos_table = np.cos(angles) / np.sqrt(length)
    sin_table = np.sin(angles) / np.sqrt(length)
    forward = np.block([[cos_table, -sin_table], [sin_table, cos_table]])
    inverse = np.block([[cos_table, sin_table], [-sin_table, cos_table]])

    def stacked(table):
        coarse = table.astype(np.float32).astype(ml_dtypes.bfloat16)
        fine = (table - coarse.astype(np.float64)).astype(ml_dtypes.bfloat16)
        return np.concatenate([coarse, coarse, fine], axis=0)

    return np.stack([stacked(forward), stacked(inverse)])


def halves(value, axis):
    coarse = value.astype(jnp.bfloat16)
    fine = (value - coarse.astype(jnp.float32)).astype(jnp.bfloat16)
    return jnp.concatenate([coarse, fine, coarse], axis=axis)


def along_lanes(value, table):
    return jnp.dot(halves(value, 1), table, preferred_element_type=jnp.float32)


def along_rows(value, table):
    dims = (((0,), (0,)), ((), ()))
    return lax.dot_general(halves(value, 0), table, dims, preferred_element_type=jnp.float32)


def regroup(value, length):
    top, bottom = (value[:length], value[length:])
    return jnp.concatenate(
        [
            jnp.concatenate([top[:, :length], bottom[:, :length]], axis=1),
            jnp.concatenate([top[:, length:], bottom[:, length:]], axis=1),
        ],
        axis=0,
    )


def slots_kernel(
    places, counts, object_map, probes, intensity, turns, totals, sums, window, far, power, terms
):
    modes, length = (probes.shape[1], probes.shape[-1])
    breadth = object_map.shape[-1]
    tall = length // 8
    slots = intensity.shape[0]
    live = counts[0]
    sublane = lax.broadcasted_iota(jnp.int32, (tall, 8, length), 1)
    sublane_more = lax.broadcasted_iota(jnp.int32, (tall + 1, 8, length), 1)
    totals[...] = jnp.zeros_like(totals)
    lighting = jnp.zeros((length, length), jnp.float32)
    for mode in range(modes):
        lighting += probes[0, mode] * probes[0, mode] + probes[1, mode] * probes[1, mode]
    terms[0, 2] = lighting
    coverage = jnp.zeros((length, length), jnp.float32)
    for slot in range(slots):
        tile, back, shift, upward = (places[slot, n] for n in range(4))
        for plane in range(2):
            wide = object_map[plane, pl.ds(tile, tall + 1)]
            wide = pltpu.roll(wide, back, 2)[:, :, :length]
            wide = pltpu.roll(wide, upward, 1)
            wide = jnp.where(sublane + shift < 8, wide[:tall], wide[1:])
            window[slot, plane] = wide.reshape(length, length)
        lit = window[slot, 0] * window[slot, 0] + window[slot, 1] * window[slot, 1]
        coverage += jnp.where(slot < live, lit, 0.0)
    sums[2 * modes] = coverage

    for pair in range(modes // 2):
        for slot in range(slots):
            waves = []
            for mode in (2 * pair, 2 * pair + 1):
                probe_r, probe_i = (probes[0, mode], probes[1, mode])
                obj_r, obj_i = (window[slot, 0], window[slot, 1])
                wave_r = probe_r * obj_r - probe_i * obj_i
                wave_i = probe_r * obj_i + probe_i * obj_r
                waves.append(jnp.concatenate([wave_r, wave_i], axis=1))
            half = regroup(along_lanes(jnp.concatenate(waves, axis=0), turns[0]), length)
            spread = along_rows(half, turns[0])
            far[slot, pair] = spread
            square = spread * spread
            square = square[:, :length] + square[:, length:]
            square = square[:length] + square[length:]
            if pair == 0:
                power[slot] = square
            else:
                power[slot] += square
    for slot in range(slots):
        ratio = jnp.sqrt(intensity[slot].T / jnp.maximum(power[slot], 1.0)) - 1.0
        power[slot] = jnp.where(slot < live, ratio, 0.0)
    for pair in range(modes // 2):
        for slot in range(slots):
            factor = power[slot]
            factor = jnp.concatenate([factor, factor], axis=1)
            factor = jnp.concatenate([factor, factor], axis=0)
            half = regroup(along_lanes(far[slot, pair] * factor, turns[1]), length)
            change = along_rows(half, turns[1])
            obj_r, obj_i = (window[slot, 0], window[slot, 1])
            terms_r = jnp.zeros((length, length), jnp.float32)
            terms_i = jnp.zeros((length, length), jnp.float32)
            for which in range(2):
                mode = 2 * pair + which
                rows = slice(which * length, (which + 1) * length)
                change_r, change_i = (change[rows, :length], change[rows, length:])
                probe_r, probe_i = (probes[0, mode], probes[1, mode])
                terms_r += probe_r * change_r + probe_i * change_i
                terms_i += probe_r * change_i - probe_i * change_r
                moved_r = obj_r * change_r + obj_i * change_i
                moved_i = obj_r * change_i - obj_i * change_r
                if slot == 0:
                    sums[mode] = moved_r
                    sums[modes + mode] = moved_i
                else:
                    sums[mode] += moved_r
                    sums[modes + mode] += moved_i
            if pair == 0:
                terms[slot, 0] = terms_r
                terms[slot, 1] = terms_i
            else:
                terms[slot, 0] += terms_r
                terms[slot, 1] += terms_i

    def place_slot(slot, carry):
        tile, back, shift = (places[slot, n] for n in range(3))
        onward = lax.rem(breadth - back, breadth)
        blank = jnp.zeros((1, 8, length), jnp.float32)
        margin = jnp.zeros((tall + 1, 8, breadth - length), jnp.float32)
        for plane in range(3):
            part = terms[slot, plane] if plane < 2 else terms[0, 2]
            part = pltpu.roll(part.reshape(tall, 8, length), lax.rem(shift, 8), 1)
            part = jnp.where(
                sublane_more >= shift,
                jnp.concatenate([part, blank], axis=0),
                jnp.concatenate([blank, part], axis=0),
            )
            wide = pltpu.roll(jnp.concatenate([part, margin], axis=2), onward, 2)
            totals[plane, pl.ds(tile, tall + 1)] += wide
        return carry

    lax.fori_loop(0, live, place_slot, 0)


def accumulate(object_map, probes, places, counts, intensity, turns):
    _, modes, length, _ = probes.shape
    slots = intensity.shape[0]
    return pl.pallas_call(
        slots_kernel,
        out_shape=(
            jax.ShapeDtypeStruct((3,) + object_map.shape[1:], jnp.float32),
            jax.ShapeDtypeStruct((2 * modes + 1, length, length), jnp.float32),
        ),
        in_specs=[scalars, scalars] + [memory] * 4,
        out_specs=(memory, memory),
        scratch_shapes=[
            pltpu.VMEM((slots, 2, length, length), jnp.float32),
            pltpu.VMEM((slots, modes // 2, 2 * length, 2 * length), jnp.float32),
            pltpu.VMEM((slots, length, length), jnp.float32),
            pltpu.VMEM((slots, 3, length, length), jnp.float32),
        ],
        compiler_params=pltpu.CompilerParams(vmem_limit_bytes=36 * 1024 * 1024),
        name="slots",
    )(places, counts, object_map, probes, intensity, turns)


def window_places(starts, rows, lanes, length, lead):
    rows_at = jnp.clip(starts[:, 0], 0, rows - length)
    cols_at = jnp.clip(starts[:, 1], 0, lanes - length)
    tile = jnp.minimum(rows_at // 8, (rows - length) // 8 - 1)
    shift = rows_at - 8 * tile
    back = (lanes + lead - cols_at) % lanes
    return jnp.stack([tile, back, shift, (8 - shift) % 8], axis=1)


def mixing(probes, probe_step):
    mix_r = jnp.sum(probes[0] * probe_step[0] + probes[1] * probe_step[1], axis=0)
    mix_i = jnp.sum(probes[0] * probe_step[1] - probes[1] * probe_step[0], axis=0)
    return (mix_r, mix_i)


def cross_term(object_map, change, starts, active, mix_r, mix_i):
    length = mix_r.shape[-1]
    anchor_index = jnp.int32(0)

    def cross_visit_slot(running, element):
        corner_at, weight = element
        corner = (anchor_index, corner_at[0], corner_at[1])
        object_win = lax.dynamic_slice(object_map, corner, (2, length, length))
        change_win = lax.dynamic_slice(change, corner, (2, length, length))
        aligned = change_win[0] * object_win[0] + change_win[1] * object_win[1]
        rotated = change_win[0] * object_win[1] - change_win[1] * object_win[0]
        return (running + weight * jnp.sum(aligned * mix_r - rotated * mix_i), None)

    running, _ = lax.scan(cross_visit_slot, jnp.zeros((), jnp.float32), (starts, active))
    return running


def solve_steps(object_curve, cross_curve, probe_curve, object_slope, probe_slope):
    object_diag = 1.1 * object_curve + 0.001
    probe_diag = 1.1 * probe_curve + 0.001
    determinant = object_diag * probe_diag - cross_curve * cross_curve
    object_rate = (probe_diag * object_slope - cross_curve * probe_slope) / determinant
    probe_rate = (object_diag * probe_slope - cross_curve * object_slope) / determinant
    return (object_rate, probe_rate)


def widen(planes, margin):
    return with_halo(planes, (("tx", 1), ("ty", 2)), margin)


def fold_rims(totals, margin, height, breadth):
    middle = totals[:, margin : margin + height, :]
    for direction in (1, -1):
        border = totals[:, margin + height :, :] if direction == 1 else totals[:, :margin, :]
        arrived = from_behind(border, "tx", direction)
        if direction == 1:
            middle = jnp.concatenate([middle + arrived, middle[:, margin:, :]], axis=1)
        else:
            middle = jnp.concatenate([middle[:, : height - margin, :], middle + arrived], axis=1)
    interior = middle[:, :, margin : margin + breadth]
    for direction in (1, -1):
        border = middle[:, :, margin + breadth :] if direction == 1 else middle[:, :, :margin]
        arrived = from_behind(border, "ty", direction)
        if direction == 1:
            interior = jnp.concatenate(
                [interior[:, :, :margin] + arrived, interior[:, :, margin:]], axis=2
            )
        else:
            interior = jnp.concatenate(
                [interior[:, :, : breadth - margin], interior[:, :, breadth - margin :] + arrived],
                axis=2,
            )
    return interior


def general(object_field, probe_modes, positions, counts, intensity):
    length = probe_modes.shape[-1]
    margin = length // 2
    height = object_field.shape[1]
    breadth = object_field.shape[2]
    turns = split_tables(length)
    modes = probe_modes.shape[1]
    anchor = jnp.stack(
        [lax.axis_index("tx") * height - margin, lax.axis_index("ty") * breadth - margin]
    )
    starts = positions - anchor[None, :]
    active = (jnp.arange(positions.shape[0], dtype=jnp.int32) < counts[0]).astype(jnp.float32)
    places = window_places(starts, height + 2 * margin, breadth + 2 * margin, length, 0)
    object_map = object_field
    probes = probe_modes
    extended = widen(object_map, margin)
    for repeat in range(ITERS):
        tiled = extended.reshape(2, -1, 8, extended.shape[-1])
        totals, sums = accumulate(tiled, probes, places, counts, intensity, turns)
        totals = totals.reshape((3,) + extended.shape[1:])
        interior = fold_rims(totals, margin, height, breadth)
        change = interior[:2] / jnp.maximum(interior[2], 1.0)
        object_part = jnp.sum((change[0] * change[0] + change[1] * change[1]) * interior[2])
        slope_part = jnp.sum(interior[:2] * change)
        wide_change = widen(change, margin)
        sums = lax.psum(sums, ("tx", "ty"))
        probe_total = sums[: 2 * modes].reshape(probes.shape)
        weight_total = sums[2 * modes]
        probe_step = probe_total / (weight_total + 1e-05)
        mix_r, mix_i = mixing(probes, probe_step)
        cross_part = cross_term(extended, wide_change, starts, active, mix_r, mix_i)
        object_curve, cross_curve, object_slope = lax.psum(
            (object_part, cross_part, slope_part), ("tx", "ty")
        )
        probe_curve = jnp.sum(
            (probe_step[0] * probe_step[0] + probe_step[1] * probe_step[1]) * weight_total
        )
        probe_slope = jnp.sum(probe_total * probe_step)
        object_rate, probe_rate = solve_steps(
            object_curve, cross_curve, probe_curve, object_slope, probe_slope
        )
        object_map = object_map + object_rate * change
        probes = probes + probe_rate * probe_step
        if repeat + 1 < ITERS:
            extended = extended + object_rate * wide_change
    return (object_map, probes)

anywhere = pl.BlockSpec(memory_space=pl.ANY)
OTHERS = [(i, j) for i in range(4) for j in range(4) if i or j]
AROUND = [(i, j) for i in (-1, 0, 1) for j in (-1, 0, 1) if i or j]
SIDES = [(i, j) for i in (-1, 0, 1) for j in (-1, 1)]


def everyone(row, col):
    return [{"tx": (row + i) % 4, "ty": (col + j) % 4} for i, j in OTHERS]


def greet(peers):
    barrier = pltpu.get_barrier_semaphore()
    for peer in peers:
        pl.semaphore_signal(barrier, 1, device_id=peer, device_id_type=pl.DeviceIdType.MESH)
    pl.semaphore_wait(barrier, len(peers))


class Copies:
    def __init__(self, send, arrive):
        self.send, self.arrive, self.count = (send, arrive, 0)
        self.unsent = []

    def slots(self, number):
        self.count += number
        return self.count - number

    def make(self, source, target, index, landing, peer):
        return pltpu.make_async_remote_copy(
            src_ref=source,
            dst_ref=target,
            send_sem=self.send.at[index],
            recv_sem=self.arrive.at[landing],
            device_id=peer,
            device_id_type=pl.DeviceIdType.MESH,
        )

    def start(self, source, target, peer):
        index = self.slots(1)
        copy = self.make(source, target, index, index, peer)
        copy.start()
        self.unsent.append(copy)
        return copy

    def finish(self):
        for copy in self.unsent:
            copy.wait_send()


class Ring:
    def __init__(self, copies, row, col, source, target):
        self.copies, self.row, self.col = (copies, row, col)
        self.source, self.target = (source, target)
        self.base = copies.slots(len(AROUND))

    def each(self, what):
        for k, (i, j) in enumerate(AROUND):
            row, col = (self.row + i, self.col + j)
            inside = (row >= 0) & (row < 4) & (col >= 0) & (col < 4)
            pl.when(inside)(functools.partial(what, k, i, j, {"tx": row, "ty": col}))

    def outgoing(self, k, i, j, peer):
        landing = AROUND.index((-i, -j))
        return self.copies.make(
            self.source(i, j), self.target(-i, -j), self.base + k, self.base + landing, peer
        )

    def blank(self):
        for i, j in AROUND:
            row, col = (self.row + i, self.col + j)
            inside = (row >= 0) & (row < 4) & (col >= 0) & (col < 4)
            target = self.target(i, j)

            @pl.when(jnp.logical_not(inside))
            def _():
                target[...] = jnp.zeros(target.shape, jnp.float32)

    def start(self):
        self.each(lambda k, i, j, peer: self.outgoing(k, i, j, peer).start())

    def receive(self):
        def arrived(k, i, j, peer):
            index = self.base + k
            self.copies.make(self.source(i, j), self.target(i, j), index, index, peer).wait_recv()

        self.each(arrived)

    def finish(self):
        self.each(lambda k, i, j, peer: self.outgoing(k, i, j, peer).wait_send())


def early_lanes(value):
    return lax.broadcasted_iota(jnp.int32, value.shape, value.ndim - 1) < value.shape[-1] // 2


def turned(value):
    return pltpu.roll(value, value.shape[-1] // 2, value.ndim - 1)


def pack_first(block):
    half = block.shape[1] // 2
    top, bottom = (block[:, :half], block[:, half:])
    return jnp.where(early_lanes(top), top, turned(bottom))


def pack_last(block):
    half = block.shape[1] // 2
    top, bottom = (block[:, :half], block[:, half:])
    return jnp.where(early_lanes(top), turned(top), bottom)


def unpack(first, last):
    early = early_lanes(first)
    top = jnp.where(early, first, turned(last))
    bottom = jnp.where(early, turned(first), last)
    return jnp.concatenate([top, bottom], axis=1)


def row_range(i, high):
    return slice((i + 1) * high, (i + 2) * high)


def halo_ring(copies, row, col, own, packed, above, beside):
    def source(i, j):
        return own if j == 0 else packed.at[(j + 1) // 2]

    def target(i, j):
        return above.at[(i + 1) // 2] if j == 0 else beside.at[SIDES.index((i, j))]

    return Ring(copies, row, col, source, target)


def spread_halo(own, above, beside, wide):
    high, broad = (own.shape[1], own.shape[-1])
    for i in (-1, 0, 1):
        rows = row_range(i, high)
        wide[:, rows, :, :broad] = own if i == 0 else above[(i + 1) // 2]
        wide[:, rows, :, broad:] = unpack(
            beside[SIDES.index((i, 1))], beside[SIDES.index((i, -1))]
        )


def widen_kernel(
    own_at, probes_at, turns_at, intensity_at, wide, probes, turns, intensity, own, packed, above,
    beside, local, send, arrive,
):
    row, col = (lax.axis_index("tx"), lax.axis_index("ty"))
    fetches = [
        pltpu.make_async_copy(source, target, local.at[k])
        for k, (source, target) in enumerate(
            ((own_at, own), (probes_at, probes), (turns_at, turns), (intensity_at, intensity))
        )
    ]
    for fetch in fetches:
        fetch.start()
    copies = Copies(send, arrive)
    ring = halo_ring(copies, row, col, own, packed, above, beside)
    ring.blank()
    fetches[0].wait()
    block = own[...]
    packed[0] = pack_first(block)
    packed[1] = pack_last(block)
    greet(everyone(row, col))
    ring.start()
    for fetch in fetches[1:]:
        fetch.wait()
    ring.receive()
    spread_halo(block, above, beside, wide)
    ring.finish()


def halo_scratch(high, broad):
    return [
        pltpu.VMEM((2, 2, high // 2, 8, broad), jnp.float32),
        pltpu.VMEM((2, 2, high, 8, broad), jnp.float32),
        pltpu.VMEM((6, 2, high // 2, 8, broad), jnp.float32),
    ]


def widen_tiles(own, probes, turns, intensity):
    two, high, _, broad = own.shape

    def like(value):
        return jax.ShapeDtypeStruct(value.shape, value.dtype)

    return pl.pallas_call(
        widen_kernel,
        out_shape=(
            jax.ShapeDtypeStruct((two, 3 * high, 8, 2 * broad), jnp.float32),
            like(probes),
            like(turns),
            like(intensity),
        ),
        in_specs=[anywhere] * 4,
        out_specs=(memory,) * 4,
        scratch_shapes=[pltpu.VMEM(own.shape, jnp.float32)]
        + halo_scratch(high, broad)
        + [
            pltpu.SemaphoreType.DMA((4,)),
            pltpu.SemaphoreType.DMA((8,)),
            pltpu.SemaphoreType.DMA((8,)),
        ],
        compiler_params=pltpu.CompilerParams(
            collective_id=0, has_side_effects=True, vmem_limit_bytes=12 * 1024 * 1024
        ),
        name="widen",
    )(own, probes, turns, intensity)


def in_rows(values, lanes):
    at = lax.broadcasted_iota(jnp.int32, (8, lanes), 0)
    result = jnp.zeros((8, lanes), jnp.float32)
    for place, value in enumerate(values):
        result = jnp.where(at == place, value, result)
    return result


def settle_kernel(
    last, places, weights, totals, sums, object_map, probes, *rest
):
    if last:
        got, change_own, rates_out = rest[:3]
        rest = rest[3:]
    else:
        new_map, new_probes, got = rest[:3]
        rest = rest[3:]
    (
        fold_out, fold_over, fold_beside, r1, acc, ra1, acca, ra2, rb1, accb, rb2, change, packed,
        above, beside, wide, held, mix, mine, inbox, send, arrive,
    ) = rest
    row, col = (lax.axis_index("tx"), lax.axis_index("ty"))
    core, side = (col % 2, col // 2)
    high, broad = (change.shape[1], change.shape[-1])
    first_part = ra1.shape[0]
    planes = got.shape[0]
    modes = planes // 2
    own_rows = row_range(0, high)
    peers = everyone(row, col)
    partner = {"tx": row, "ty": side * 2 + (1 - core)}
    across = {"tx": row, "ty": (1 - side) * 2 + core}
    along = [(row + j) % 4 for j in (1, 2, 3)]
    copies = Copies(send, arrive)

    barrier = pltpu.get_barrier_semaphore()
    for peer in peers:
        pl.semaphore_signal(barrier, 1, device_id=peer, device_id_type=pl.DeviceIdType.MESH)
    for k, (i, j) in enumerate(SIDES):
        block = totals[:, row_range(i, high), :, broad:]
        fold_out[k] = pack_first(block) if j == 1 else pack_last(block)

    def fold_source(i, j):
        if j == 0:
            return totals.at[:, row_range(i, high), :, slice(0, broad)]
        return fold_out.at[SIDES.index((i, j))]

    def fold_target(i, j):
        return fold_over.at[(i + 1) // 2] if j == 0 else fold_beside.at[SIDES.index((i, j))]

    fold = Ring(copies, row, col, fold_source, fold_target)
    halo = halo_ring(copies, row, col, change, packed, above, beside)

    fold.blank()
    halo.blank()
    pl.semaphore_wait(barrier, len(peers))
    core_step = copies.start(sums.at[:, 1 - core], r1, partner)
    fold.start()
    core_step.wait_recv()
    acc[...] = sums[:, core] + r1[...]
    a_step = [copies.start(acc.at[:first_part, 1 - side], ra1, across)]
    b_step = [
        copies.start(acc.at[first_part:, :, j], rb1.at[k], {"tx": j, "ty": col})
        for k, j in enumerate(along)
    ]

    fold.receive()
    firsts = fold_beside[SIDES.index((0, -1))]
    lasts = fold_beside[SIDES.index((0, 1))]
    for i in (-1, 1):
        firsts += fold_beside[SIDES.index((i, -1))]
        lasts += fold_beside[SIDES.index((i, 1))]
    interior = totals[:, own_rows, :, :broad] + fold_over[0] + fold_over[1]
    interior += unpack(firsts, lasts)
    moved = interior[:2] / jnp.maximum(interior[2], 1.0)
    change[...] = moved
    packed[0] = pack_first(moved)
    packed[1] = pack_last(moved)
    halo.start()
    curve = jnp.sum((moved[0] * moved[0] + moved[1] * moved[1]) * interior[2])
    slope = jnp.sum(interior[:2] * moved)

    a_step[0].wait_recv()
    acca[...] = acc[:first_part, side] + ra1[...]
    a_step = [
        copies.start(acca.at[:, j], ra2.at[k], {"tx": j, "ty": col})
        for k, j in enumerate(along)
    ]
    for copy in b_step:
        copy.wait_recv()
    accb[...] = acc[first_part:, :, row] + rb1[0] + rb1[1] + rb1[2]
    b_step = [copies.start(accb.at[:, 1 - side], rb2, across)]

    halo.receive()
    spread_halo(change[...], above, beside, wide)
    product_r = wide[0] * object_map[0] + wide[1] * object_map[1]
    product_i = wide[0] * object_map[1] - wide[1] * object_map[0]
    held[0] = product_r
    held[1] = product_i
    tall = 2 * high
    sublane = lax.broadcasted_iota(jnp.int32, (tall, 8, broad), 1)
    gathered = []
    for plane in range(2):
        running = jnp.zeros((tall, 8, broad), jnp.float32)
        for slot in range(places.shape[0]):
            tile, back, shift, upward = (places[slot, n] for n in range(4))
            part = held[plane, pl.ds(tile, tall + 1)]
            part = pltpu.roll(part, back, 2)[:, :, :broad]
            part = pltpu.roll(part, upward, 1)
            running += weights[slot] * jnp.where(sublane + shift < 8, part[:tall], part[1:])
        gathered.append(running)

    for copy in a_step + b_step:
        copy.wait_recv()
    total_a = acca[:, row] + ra2[0] + ra2[1] + ra2[2]
    total_b = accb[:, side] + rb2[...]
    total = jnp.concatenate([total_a, total_b], axis=0)
    weight = total[planes:]
    found = total[:planes] / (weight + 1e-05)
    got[:, core, side, row] = found
    probe_curve = jnp.sum(found * found * weight)
    probe_slope = jnp.sum(total[:planes] * found)
    probe_r, probe_i = (probes[0, :, core, side, row], probes[1, :, core, side, row])
    found_r, found_i = (found[:modes], found[modes:])
    mix[0, core, side, row] = jnp.sum(probe_r * found_r + probe_i * found_i, axis=0)
    mix[1, core, side, row] = jnp.sum(probe_r * found_i - probe_i * found_r, axis=0)

    spot = mix.at[:, core, side, row]
    mixes = [copies.start(spot, spot, peer) for peer in peers]

    def give(block, peer):
        return copies.start(block, block, peer)

    cutoff = 10
    one = got.at[:cutoff, core, side, row]
    give_a = [give(one, {"tx": j, "ty": col}) for j in along]
    one = got.at[cutoff:, core, side, row]
    give_b = [give(one, across)]
    for copy in give_a:
        copy.wait_recv()
    next_a = [give(got.at[:cutoff, core, side], across)]
    pass_on = [give(got.at[:cutoff, core, side], partner)]
    give_b[0].wait_recv()
    one = got.at[cutoff:, core, :, row]
    next_b = [give(one, {"tx": j, "ty": col}) for j in along]
    pass_on.append(give(one, partner))

    for copy in mixes:
        copy.wait_recv()
    mix_all = mix[...].reshape(2, tall, 8, broad)
    cross = jnp.sum(gathered[0] * mix_all[0] - gathered[1] * mix_all[1])
    mine[...] = in_rows((curve, slope, probe_curve, probe_slope, cross), broad)
    terms = [copies.start(mine, inbox.at[k], peer) for k, peer in enumerate(peers)]

    next_a[0].wait_recv()
    pass_on.append(give(got.at[:cutoff, core, 1 - side], partner))
    for copy, j in zip(next_b, along):
        copy.wait_recv()
    for j in along:
        pass_on.append(give(got.at[cutoff:, core, :, j], partner))
    for copy in terms:
        copy.wait_recv()
    sent = mine[...] + jnp.sum(inbox[...], axis=0)
    object_rate, probe_rate = solve_steps(
        sent[0:1], sent[4:5], sent[2:3], sent[1:2], sent[3:4]
    )
    object_rate = jnp.broadcast_to(object_rate, (8, broad))
    probe_rate = jnp.broadcast_to(probe_rate, (8, broad))
    if last:
        at = lax.broadcasted_iota(jnp.int32, (8, broad), 0)
        rates_out[...] = jnp.where(at == 0, object_rate, probe_rate)
        change_own[...] = change[...]
        for copy in pass_on:
            copy.wait_recv()
    else:
        both = jnp.concatenate([object_rate, object_rate], axis=1)
        new_map[...] = object_map[...] + both * wide[...]
        for copy in pass_on:
            copy.wait_recv()
        for part in range(2):
            new_probes[part] = probes[part] + probe_rate * got[part * modes : (part + 1) * modes]
    copies.finish()
    fold.finish()
    halo.finish()


def settle(last, places, weights, totals, sums, object_map, probes):
    _, rows, _, lanes = totals.shape
    modes, length = (probes.shape[1], probes.shape[-1])
    planes = 2 * modes
    high, broad = (rows // 3, lanes // 2)
    first_part = 11
    second_part = planes + 1 - first_part
    f32 = jnp.float32
    grid = (2, 2, 4)
    step = jax.ShapeDtypeStruct((planes,) + grid + (8, length), f32)
    if last:
        out_shape = (
            step,
            jax.ShapeDtypeStruct((2, high, 8, broad), f32),
            jax.ShapeDtypeStruct((8, broad), f32),
        )
    else:
        out_shape = (
            jax.ShapeDtypeStruct(object_map.shape, f32),
            jax.ShapeDtypeStruct((2, modes) + grid + (8, length), f32),
            step,
        )
    return pl.pallas_call(
        functools.partial(settle_kernel, last),
        out_shape=out_shape,
        in_specs=[scalars, scalars] + [memory] * 4,
        out_specs=(memory,) * 3,
        scratch_shapes=[
            pltpu.VMEM((6, 3, high // 2, 8, broad), f32),
            pltpu.VMEM((2, 3, high, 8, broad), f32),
            pltpu.VMEM((6, 3, high // 2, 8, broad), f32),
            pltpu.VMEM((planes + 1, 2, 4, 8, length), f32),
            pltpu.VMEM((planes + 1, 2, 4, 8, length), f32),
            pltpu.VMEM((first_part, 4, 8, length), f32),
            pltpu.VMEM((first_part, 4, 8, length), f32),
            pltpu.VMEM((3, first_part, 8, length), f32),
            pltpu.VMEM((3, second_part, 2, 8, length), f32),
            pltpu.VMEM((second_part, 2, 8, length), f32),
            pltpu.VMEM((second_part, 8, length), f32),
            pltpu.VMEM((2, high, 8, broad), f32),
        ]
        + halo_scratch(high, broad)
        + [
            pltpu.VMEM((2, rows, 8, lanes), f32),
            pltpu.VMEM((2, rows, 8, lanes), f32),
            pltpu.VMEM((2,) + grid + (8, length), f32),
            pltpu.VMEM((8, broad), f32),
            pltpu.VMEM((15, 8, broad), f32),
            pltpu.SemaphoreType.DMA((80,)),
            pltpu.SemaphoreType.DMA((80,)),
        ],
        compiler_params=pltpu.CompilerParams(
            collective_id=2 if last else 1,
            has_side_effects=True,
            vmem_limit_bytes=24 * 1024 * 1024,
        ),
        name="finish" if last else "settle",
    )(
        places,
        weights,
        totals,
        sums.reshape((planes + 1,) + grid + (8, length)),
        object_map,
        probes.reshape((2, modes) + grid + (8, length)),
    )


def direct(object_field, probe_modes, positions, counts, intensity):
    two, modes, length, _ = probe_modes.shape
    margin = length // 2
    _, height, breadth = object_field.shape
    anchor = jnp.stack(
        [lax.axis_index("tx") * height - margin, lax.axis_index("ty") * breadth - margin]
    )
    starts = positions - anchor[None, :]
    lanes = 2 * breadth
    places = window_places(starts, height + 2 * margin, lanes, length, margin)
    weights = (jnp.arange(positions.shape[0], dtype=jnp.int32) < counts[0]).astype(jnp.float32)
    object_map, probes, turns, measured = widen_tiles(
        object_field.reshape(2, height // 8, 8, breadth),
        probe_modes,
        jnp.asarray(split_tables(length)),
        intensity,
    )
    for repeat in range(ITERS):
        totals, sums = accumulate(object_map, probes, places, counts, measured, turns)
        last = repeat + 1 == ITERS
        settled = settle(last, places, weights, totals, sums, object_map, probes)
        if not last:
            object_map, probes, _ = settled
            probes = probes.reshape(probe_modes.shape)
    step, change, rates = settled
    own = object_map[:, height // 8 : height // 4, :, :breadth]
    return (
        (own + rates[0, 0] * change).reshape(object_field.shape),
        probes + rates[1, 0] * step.reshape(probes.shape),
    )


def shards(object_field, probe_modes, positions, counts, intensity):
    _, height, breadth = object_field.shape
    length = probe_modes.shape[-1]
    grid = (lax.axis_size("tx"), lax.axis_size("ty"))
    arguments = (object_field, probe_modes, positions, counts, intensity)
    if grid == (4, 4) and length == 128 and (2 * height, breadth) == (length, length):
        return direct(*arguments)
    return general(*arguments)


def solution(mesh):
    return jax.shard_map(
        shards,
        mesh=mesh,
        in_specs=(
            P("groups", "tx", "ty"),
            P("groups", None, None, None),
            P(("groups", "tx", "ty"), None),
            P(("groups", "tx", "ty")),
            P(("groups", "tx", "ty"), None, None),
        ),
        out_specs=(P("groups", "tx", "ty"), P("groups", None, None, None)),
        check_vma=False,
    )
```

```python
import functools

import jax
import jax.numpy as jnp
import ml_dtypes
import numpy as np
from jax import lax
from jax.experimental import pallas as pl
from jax.experimental.pallas import tpu as pltpu
from jax.sharding import PartitionSpec as P

ITERS = 2
memory = pl.BlockSpec(memory_space=pltpu.VMEM)
scalars = pl.BlockSpec(memory_space=pltpu.SMEM)


def with_halo(value, sides, width):
    for axis, dim in sides:
        size, length = (lax.axis_size(axis), value.shape[dim])
        up = [(i, (i + 1) % size) for i in range(size - 1)]
        down = [(j, i) for i, j in up]
        last = lax.slice_in_dim(value, length - width, length, axis=dim)
        first = lax.slice_in_dim(value, 0, width, axis=dim)
        before = lax.ppermute(last, axis, up)
        after = lax.ppermute(first, axis, down)
        value = jnp.concatenate([before, value, after], axis=dim)
    return value


def from_behind(block, axis, distance):
    devices = range(lax.axis_size(axis))
    route = [(i - distance, i) for i in devices if i - distance in devices]
    return lax.ppermute(block, axis, route)


def split_tables(length):
    indices = np.arange(length)
    angles = (indices[:, None] * indices[None, :] % length) * (2.0 * np.pi / length)
    cos_table = np.cos(angles) / np.sqrt(length)
    sin_table = np.sin(angles) / np.sqrt(length)
    forward = np.block([[cos_table, -sin_table], [sin_table, cos_table]])
    inverse = np.block([[cos_table, sin_table], [-sin_table, cos_table]])

    def stacked(table):
        coarse = table.astype(np.float32).astype(ml_dtypes.bfloat16)
        fine = (table - coarse.astype(np.float64)).astype(ml_dtypes.bfloat16)
        return np.concatenate([coarse, coarse, fine], axis=0)

    return np.stack([stacked(forward), stacked(inverse)])


def halves(value, axis):
    coarse = value.astype(jnp.bfloat16)
    fine = (value - coarse.astype(jnp.float32)).astype(jnp.bfloat16)
    return jnp.concatenate([coarse, fine, coarse], axis=axis)


def along_lanes(value, table):
    return jnp.dot(halves(value, 1), table, preferred_element_type=jnp.float32)


def along_rows(value, table):
    dims = (((0,), (0,)), ((), ()))
    return lax.dot_general(halves(value, 0), table, dims, preferred_element_type=jnp.float32)


def regroup(value, length):
    top, bottom = (value[:length], value[length:])
    return jnp.concatenate(
        [
            jnp.concatenate([top[:, :length], bottom[:, :length]], axis=1),
            jnp.concatenate([top[:, length:], bottom[:, length:]], axis=1),
        ],
        axis=0,
    )


def slots_kernel(
    places, counts, object_map, probes, intensity, turns, totals, sums, window, far, power, terms
):
    modes, length = (probes.shape[1], probes.shape[-1])
    breadth = object_map.shape[-1]
    tall = length // 8
    slots = intensity.shape[0]
    live = counts[0]
    sublane = lax.broadcasted_iota(jnp.int32, (tall, 8, length), 1)
    sublane_more = lax.broadcasted_iota(jnp.int32, (tall + 1, 8, length), 1)
    totals[...] = jnp.zeros_like(totals)
    lighting = jnp.zeros((length, length), jnp.float32)
    for mode in range(modes):
        lighting += probes[0, mode] * probes[0, mode] + probes[1, mode] * probes[1, mode]
    terms[0, 2] = lighting
    coverage = jnp.zeros((length, length), jnp.float32)
    for slot in range(slots):
        tile, back, shift, upward = (places[slot, n] for n in range(4))
        for plane in range(2):
            wide = object_map[plane, pl.ds(tile, tall + 1)]
            wide = pltpu.roll(wide, back, 2)[:, :, :length]
            wide = pltpu.roll(wide, upward, 1)
            wide = jnp.where(sublane + shift < 8, wide[:tall], wide[1:])
            window[slot, plane] = wide.reshape(length, length)
        lit = window[slot, 0] * window[slot, 0] + window[slot, 1] * window[slot, 1]
        coverage += jnp.where(slot < live, lit, 0.0)
    sums[2 * modes] = coverage

    for pair in range(modes // 2):
        for slot in range(slots):
            waves = []
            for mode in (2 * pair, 2 * pair + 1):
                probe_r, probe_i = (probes[0, mode], probes[1, mode])
                obj_r, obj_i = (window[slot, 0], window[slot, 1])
                wave_r = probe_r * obj_r - probe_i * obj_i
                wave_i = probe_r * obj_i + probe_i * obj_r
                waves.append(jnp.concatenate([wave_r, wave_i], axis=1))
            half = regroup(along_lanes(jnp.concatenate(waves, axis=0), turns[0]), length)
            spread = along_rows(half, turns[0])
            far[slot, pair] = spread
            square = spread * spread
            square = square[:, :length] + square[:, length:]
            square = square[:length] + square[length:]
            if pair == 0:
                power[slot] = square
            else:
                power[slot] += square
    for slot in range(slots):
        ratio = jnp.sqrt(intensity[slot].T / jnp.maximum(power[slot], 1.0)) - 1.0
        power[slot] = jnp.where(slot < live, ratio, 0.0)
    for pair in range(modes // 2):
        for slot in range(slots):
            factor = power[slot]
            factor = jnp.concatenate([factor, factor], axis=1)
            factor = jnp.concatenate([factor, factor], axis=0)
            half = regroup(along_lanes(far[slot, pair] * factor, turns[1]), length)
            change = along_rows(half, turns[1])
            obj_r, obj_i = (window[slot, 0], window[slot, 1])
            terms_r = jnp.zeros((length, length), jnp.float32)
            terms_i = jnp.zeros((length, length), jnp.float32)
            for which in range(2):
                mode = 2 * pair + which
                rows = slice(which * length, (which + 1) * length)
                change_r, change_i = (change[rows, :length], change[rows, length:])
                probe_r, probe_i = (probes[0, mode], probes[1, mode])
                terms_r += probe_r * change_r + probe_i * change_i
                terms_i += probe_r * change_i - probe_i * change_r
                moved_r = obj_r * change_r + obj_i * change_i
                moved_i = obj_r * change_i - obj_i * change_r
                if slot == 0:
                    sums[mode] = moved_r
                    sums[modes + mode] = moved_i
                else:
                    sums[mode] += moved_r
                    sums[modes + mode] += moved_i
            if pair == 0:
                terms[slot, 0] = terms_r
                terms[slot, 1] = terms_i
            else:
                terms[slot, 0] += terms_r
                terms[slot, 1] += terms_i

    def place_slot(slot, carry):
        tile, back, shift = (places[slot, n] for n in range(3))
        onward = lax.rem(breadth - back, breadth)
        blank = jnp.zeros((1, 8, length), jnp.float32)
        margin = jnp.zeros((tall + 1, 8, breadth - length), jnp.float32)
        for plane in range(3):
            part = terms[slot, plane] if plane < 2 else terms[0, 2]
            part = pltpu.roll(part.reshape(tall, 8, length), lax.rem(shift, 8), 1)
            part = jnp.where(
                sublane_more >= shift,
                jnp.concatenate([part, blank], axis=0),
                jnp.concatenate([blank, part], axis=0),
            )
            wide = pltpu.roll(jnp.concatenate([part, margin], axis=2), onward, 2)
            totals[plane, pl.ds(tile, tall + 1)] += wide
        return carry

    lax.fori_loop(0, live, place_slot, 0)


def accumulate(object_map, probes, places, counts, intensity, turns):
    _, modes, length, _ = probes.shape
    slots = intensity.shape[0]
    return pl.pallas_call(
        slots_kernel,
        out_shape=(
            jax.ShapeDtypeStruct((3,) + object_map.shape[1:], jnp.float32),
            jax.ShapeDtypeStruct((2 * modes + 1, length, length), jnp.float32),
        ),
        in_specs=[scalars, scalars] + [memory] * 4,
        out_specs=(memory, memory),
        scratch_shapes=[
            pltpu.VMEM((slots, 2, length, length), jnp.float32),
            pltpu.VMEM((slots, modes // 2, 2 * length, 2 * length), jnp.float32),
            pltpu.VMEM((slots, length, length), jnp.float32),
            pltpu.VMEM((slots, 3, length, length), jnp.float32),
        ],
        compiler_params=pltpu.CompilerParams(vmem_limit_bytes=36 * 1024 * 1024),
        name="slots",
    )(places, counts, object_map, probes, intensity, turns)


def window_places(starts, rows, lanes, length, lead):
    rows_at = jnp.clip(starts[:, 0], 0, rows - length)
    cols_at = jnp.clip(starts[:, 1], 0, lanes - length)
    tile = jnp.minimum(rows_at // 8, (rows - length) // 8 - 1)
    shift = rows_at - 8 * tile
    back = (lanes + lead - cols_at) % lanes
    return jnp.stack([tile, back, shift, (8 - shift) % 8], axis=1)


def mixing(probes, probe_step):
    mix_r = jnp.sum(probes[0] * probe_step[0] + probes[1] * probe_step[1], axis=0)
    mix_i = jnp.sum(probes[0] * probe_step[1] - probes[1] * probe_step[0], axis=0)
    return (mix_r, mix_i)


def cross_term(object_map, change, starts, active, mix_r, mix_i):
    length = mix_r.shape[-1]
    anchor_index = jnp.int32(0)

    def cross_visit_slot(running, element):
        corner_at, weight = element
        corner = (anchor_index, corner_at[0], corner_at[1])
        object_win = lax.dynamic_slice(object_map, corner, (2, length, length))
        change_win = lax.dynamic_slice(change, corner, (2, length, length))
        aligned = change_win[0] * object_win[0] + change_win[1] * object_win[1]
        rotated = change_win[0] * object_win[1] - change_win[1] * object_win[0]
        return (running + weight * jnp.sum(aligned * mix_r - rotated * mix_i), None)

    running, _ = lax.scan(cross_visit_slot, jnp.zeros((), jnp.float32), (starts, active))
    return running


def solve_steps(object_curve, cross_curve, probe_curve, object_slope, probe_slope):
    object_diag = 1.1 * object_curve + 0.001
    probe_diag = 1.1 * probe_curve + 0.001
    determinant = object_diag * probe_diag - cross_curve * cross_curve
    object_rate = (probe_diag * object_slope - cross_curve * probe_slope) / determinant
    probe_rate = (object_diag * probe_slope - cross_curve * object_slope) / determinant
    return (object_rate, probe_rate)


def widen(planes, margin):
    return with_halo(planes, (("tx", 1), ("ty", 2)), margin)


def fold_rims(totals, margin, height, breadth):
    middle = totals[:, margin : margin + height, :]
    for direction in (1, -1):
        border = totals[:, margin + height :, :] if direction == 1 else totals[:, :margin, :]
        arrived = from_behind(border, "tx", direction)
        if direction == 1:
            middle = jnp.concatenate([middle + arrived, middle[:, margin:, :]], axis=1)
        else:
            middle = jnp.concatenate([middle[:, : height - margin, :], middle + arrived], axis=1)
    interior = middle[:, :, margin : margin + breadth]
    for direction in (1, -1):
        border = middle[:, :, margin + breadth :] if direction == 1 else middle[:, :, :margin]
        arrived = from_behind(border, "ty", direction)
        if direction == 1:
            interior = jnp.concatenate(
                [interior[:, :, :margin] + arrived, interior[:, :, margin:]], axis=2
            )
        else:
            interior = jnp.concatenate(
                [interior[:, :, : breadth - margin], interior[:, :, breadth - margin :] + arrived],
                axis=2,
            )
    return interior


def general(object_field, probe_modes, positions, counts, intensity):
    length = probe_modes.shape[-1]
    margin = length // 2
    height = object_field.shape[1]
    breadth = object_field.shape[2]
    turns = split_tables(length)
    modes = probe_modes.shape[1]
    anchor = jnp.stack(
        [lax.axis_index("tx") * height - margin, lax.axis_index("ty") * breadth - margin]
    )
    starts = positions - anchor[None, :]
    active = (jnp.arange(positions.shape[0], dtype=jnp.int32) < counts[0]).astype(jnp.float32)
    places = window_places(starts, height + 2 * margin, breadth + 2 * margin, length, 0)
    object_map = object_field
    probes = probe_modes
    extended = widen(object_map, margin)
    for repeat in range(ITERS):
        tiled = extended.reshape(2, -1, 8, extended.shape[-1])
        totals, sums = accumulate(tiled, probes, places, counts, intensity, turns)
        totals = totals.reshape((3,) + extended.shape[1:])
        interior = fold_rims(totals, margin, height, breadth)
        change = interior[:2] / jnp.maximum(interior[2], 1.0)
        object_part = jnp.sum((change[0] * change[0] + change[1] * change[1]) * interior[2])
        slope_part = jnp.sum(interior[:2] * change)
        wide_change = widen(change, margin)
        sums = lax.psum(sums, ("tx", "ty"))
        probe_total = sums[: 2 * modes].reshape(probes.shape)
        weight_total = sums[2 * modes]
        probe_step = probe_total / (weight_total + 1e-05)
        mix_r, mix_i = mixing(probes, probe_step)
        cross_part = cross_term(extended, wide_change, starts, active, mix_r, mix_i)
        object_curve, cross_curve, object_slope = lax.psum(
            (object_part, cross_part, slope_part), ("tx", "ty")
        )
        probe_curve = jnp.sum(
            (probe_step[0] * probe_step[0] + probe_step[1] * probe_step[1]) * weight_total
        )
        probe_slope = jnp.sum(probe_total * probe_step)
        object_rate, probe_rate = solve_steps(
            object_curve, cross_curve, probe_curve, object_slope, probe_slope
        )
        object_map = object_map + object_rate * change
        probes = probes + probe_rate * probe_step
        if repeat + 1 < ITERS:
            extended = extended + object_rate * wide_change
    return (object_map, probes)

outside = pl.BlockSpec(memory_space=pltpu.HBM)
OTHERS = [(i, j) for i in range(4) for j in range(4) if i or j]
AROUND = [(i, j) for i in (-1, 0, 1) for j in (-1, 0, 1) if i or j]
SIDES = [(i, j) for i in (-1, 0, 1) for j in (-1, 1)]


def everyone(row, col):
    return [{"tx": (row + i) % 4, "ty": (col + j) % 4} for i, j in OTHERS]


def greet(peers):
    barrier = pltpu.get_barrier_semaphore()
    for peer in peers:
        pl.semaphore_signal(barrier, 1, device_id=peer, device_id_type=pl.DeviceIdType.MESH)
    pl.semaphore_wait(barrier, len(peers))


class Copies:
    def __init__(self, send, arrive):
        self.send, self.arrive, self.count = (send, arrive, 0)
        self.unsent = []

    def slots(self, number):
        self.count += number
        return self.count - number

    def make(self, source, target, index, landing, peer):
        return pltpu.make_async_remote_copy(
            src_ref=source,
            dst_ref=target,
            send_sem=self.send.at[index],
            recv_sem=self.arrive.at[landing],
            device_id=peer,
            device_id_type=pl.DeviceIdType.MESH,
        )

    def start(self, source, target, peer):
        index = self.slots(1)
        copy = self.make(source, target, index, index, peer)
        copy.start()
        self.unsent.append(copy)
        return copy

    def finish(self):
        for copy in self.unsent:
            copy.wait_send()


class Ring:
    def __init__(self, copies, row, col, source, target):
        self.copies, self.row, self.col = (copies, row, col)
        self.source, self.target = (source, target)
        self.base = copies.slots(len(AROUND))

    def each(self, what):
        for k, (i, j) in enumerate(AROUND):
            row, col = (self.row + i, self.col + j)
            inside = (row >= 0) & (row < 4) & (col >= 0) & (col < 4)
            pl.when(inside)(functools.partial(what, k, i, j, {"tx": row, "ty": col}))

    def outgoing(self, k, i, j, peer):
        landing = AROUND.index((-i, -j))
        return self.copies.make(
            self.source(i, j), self.target(-i, -j), self.base + k, self.base + landing, peer
        )

    def blank(self):
        for i, j in AROUND:
            row, col = (self.row + i, self.col + j)
            inside = (row >= 0) & (row < 4) & (col >= 0) & (col < 4)
            target = self.target(i, j)

            @pl.when(jnp.logical_not(inside))
            def _():
                target[...] = jnp.zeros(target.shape, jnp.float32)

    def start(self):
        self.each(lambda k, i, j, peer: self.outgoing(k, i, j, peer).start())

    def receive(self):
        def arrived(k, i, j, peer):
            index = self.base + k
            self.copies.make(self.source(i, j), self.target(i, j), index, index, peer).wait_recv()

        self.each(arrived)

    def finish(self):
        self.each(lambda k, i, j, peer: self.outgoing(k, i, j, peer).wait_send())


def early_lanes(value):
    return lax.broadcasted_iota(jnp.int32, value.shape, value.ndim - 1) < value.shape[-1] // 2


def turned(value):
    return pltpu.roll(value, value.shape[-1] // 2, value.ndim - 1)


def pack_first(block):
    half = block.shape[1] // 2
    top, bottom = (block[:, :half], block[:, half:])
    return jnp.where(early_lanes(top), top, turned(bottom))


def pack_last(block):
    half = block.shape[1] // 2
    top, bottom = (block[:, :half], block[:, half:])
    return jnp.where(early_lanes(top), turned(top), bottom)


def unpack(first, last):
    early = early_lanes(first)
    top = jnp.where(early, first, turned(last))
    bottom = jnp.where(early, turned(first), last)
    return jnp.concatenate([top, bottom], axis=1)


def row_range(i, high):
    return slice((i + 1) * high, (i + 2) * high)


def halo_ring(copies, row, col, own, packed, above, beside):
    def source(i, j):
        return own if j == 0 else packed.at[(j + 1) // 2]

    def target(i, j):
        return above.at[(i + 1) // 2] if j == 0 else beside.at[SIDES.index((i, j))]

    return Ring(copies, row, col, source, target)


def spread_halo(own, above, beside, wide):
    high, broad = (own.shape[1], own.shape[-1])
    for i in (-1, 0, 1):
        rows = row_range(i, high)
        wide[:, rows, :, :broad] = own if i == 0 else above[(i + 1) // 2]
        wide[:, rows, :, broad:] = unpack(
            beside[SIDES.index((i, 1))], beside[SIDES.index((i, -1))]
        )


def widen_kernel(
    own_at, probes_at, turns_at, intensity_at, wide, probes, turns, intensity, own, whole, packed, above,
    beside, local, send, arrive,
):
    row, col = (lax.axis_index("tx"), lax.axis_index("ty"))
    fetches = [
        pltpu.make_async_copy(source, target, local.at[k])
        for k, (source, target) in enumerate(
            ((own_at, own), (probes_at, probes), (turns_at, turns), (intensity_at, intensity))
        )
    ]
    for fetch in fetches:
        fetch.start()
    copies = Copies(send, arrive)
    ring = halo_ring(copies, row, col, whole, packed, above, beside)
    ring.blank()
    fetches[0].wait()
    block = own[...].reshape(2, own.shape[1] // 8, 8, own.shape[2])
    whole[...] = block
    packed[0] = pack_first(block)
    packed[1] = pack_last(block)
    greet(everyone(row, col))
    ring.start()
    for fetch in fetches[1:]:
        fetch.wait()
    ring.receive()
    spread_halo(block, above, beside, wide)
    ring.finish()


def halo_scratch(high, broad):
    return [
        pltpu.VMEM((2, 2, high // 2, 8, broad), jnp.float32),
        pltpu.VMEM((2, 2, high, 8, broad), jnp.float32),
        pltpu.VMEM((6, 2, high // 2, 8, broad), jnp.float32),
    ]


def widen_tiles(own, probes, turns, intensity):
    two, height, broad = own.shape
    high = height // 8

    def like(value):
        return jax.ShapeDtypeStruct(value.shape, value.dtype)

    return pl.pallas_call(
        widen_kernel,
        out_shape=(
            jax.ShapeDtypeStruct((two, 3 * high, 8, 2 * broad), jnp.float32),
            like(probes),
            like(turns),
            like(intensity),
        ),
        in_specs=[outside] * 4,
        out_specs=(memory,) * 4,
        scratch_shapes=[
            pltpu.VMEM(own.shape, jnp.float32),
            pltpu.VMEM((two, high, 8, broad), jnp.float32),
        ]
        + halo_scratch(high, broad)
        + [
            pltpu.SemaphoreType.DMA((4,)),
            pltpu.SemaphoreType.DMA((8,)),
            pltpu.SemaphoreType.DMA((8,)),
        ],
        compiler_params=pltpu.CompilerParams(
            collective_id=0, has_side_effects=True, vmem_limit_bytes=12 * 1024 * 1024
        ),
        name="widen",
    )(own, probes, turns, intensity)


def in_rows(values, lanes):
    at = lax.broadcasted_iota(jnp.int32, (8, lanes), 0)
    result = jnp.zeros((8, lanes), jnp.float32)
    for place, value in enumerate(values):
        result = jnp.where(at == place, value, result)
    return result


def settle_kernel(
    last, places, weights, totals, sums, object_map, probes, *rest
):
    if last:
        got, change_own, rates_out = rest[:3]
        rest = rest[3:]
    else:
        new_map, new_probes, got = rest[:3]
        rest = rest[3:]
    (
        fold_out, fold_over, fold_beside, r1, acc, ra1, acca, ra2, rb1, accb, rb2, change, packed,
        above, beside, wide, held, mix, mine, inbox, send, arrive,
    ) = rest
    row, col = (lax.axis_index("tx"), lax.axis_index("ty"))
    core, side = (col % 2, col // 2)
    high, broad = (change.shape[1], change.shape[-1])
    first_part = ra1.shape[0]
    planes = got.shape[0]
    modes = planes // 2
    own_rows = row_range(0, high)
    peers = everyone(row, col)
    partner = {"tx": row, "ty": side * 2 + (1 - core)}
    across = {"tx": row, "ty": (1 - side) * 2 + core}
    along = [(row + j) % 4 for j in (1, 2, 3)]
    copies = Copies(send, arrive)

    barrier = pltpu.get_barrier_semaphore()
    for peer in peers:
        pl.semaphore_signal(barrier, 1, device_id=peer, device_id_type=pl.DeviceIdType.MESH)
    for k, (i, j) in enumerate(SIDES):
        block = totals[:, row_range(i, high), :, broad:]
        fold_out[k] = pack_first(block) if j == 1 else pack_last(block)

    def fold_source(i, j):
        if j == 0:
            return totals.at[:, row_range(i, high), :, slice(0, broad)]
        return fold_out.at[SIDES.index((i, j))]

    def fold_target(i, j):
        return fold_over.at[(i + 1) // 2] if j == 0 else fold_beside.at[SIDES.index((i, j))]

    fold = Ring(copies, row, col, fold_source, fold_target)
    halo = halo_ring(copies, row, col, change, packed, above, beside)

    fold.blank()
    halo.blank()
    pl.semaphore_wait(barrier, len(peers))
    core_step = copies.start(sums.at[:, 1 - core], r1, partner)
    fold.start()
    core_step.wait_recv()
    acc[...] = sums[:, core] + r1[...]
    a_step = [copies.start(acc.at[:first_part, 1 - side], ra1, across)]
    b_step = [
        copies.start(acc.at[first_part:, :, j], rb1.at[k], {"tx": j, "ty": col})
        for k, j in enumerate(along)
    ]

    fold.receive()
    firsts = fold_beside[SIDES.index((0, -1))]
    lasts = fold_beside[SIDES.index((0, 1))]
    for i in (-1, 1):
        firsts += fold_beside[SIDES.index((i, -1))]
        lasts += fold_beside[SIDES.index((i, 1))]
    interior = totals[:, own_rows, :, :broad] + fold_over[0] + fold_over[1]
    interior += unpack(firsts, lasts)
    moved = interior[:2] / jnp.maximum(interior[2], 1.0)
    change[...] = moved
    packed[0] = pack_first(moved)
    packed[1] = pack_last(moved)
    halo.start()
    curve = jnp.sum((moved[0] * moved[0] + moved[1] * moved[1]) * interior[2])
    slope = jnp.sum(interior[:2] * moved)

    a_step[0].wait_recv()
    acca[...] = acc[:first_part, side] + ra1[...]
    a_step = [
        copies.start(acca.at[:, j], ra2.at[k], {"tx": j, "ty": col})
        for k, j in enumerate(along)
    ]
    for copy in b_step:
        copy.wait_recv()
    accb[...] = acc[first_part:, :, row] + rb1[0] + rb1[1] + rb1[2]
    b_step = [copies.start(accb.at[:, 1 - side], rb2, across)]

    halo.receive()
    spread_halo(change[...], above, beside, wide)
    product_r = wide[0] * object_map[0] + wide[1] * object_map[1]
    product_i = wide[0] * object_map[1] - wide[1] * object_map[0]
    held[0] = product_r
    held[1] = product_i
    tall = 2 * high
    sublane = lax.broadcasted_iota(jnp.int32, (tall, 8, broad), 1)
    gathered = []
    for plane in range(2):
        running = jnp.zeros((tall, 8, broad), jnp.float32)
        for slot in range(places.shape[0]):
            tile, back, shift, upward = (places[slot, n] for n in range(4))
            part = held[plane, pl.ds(tile, tall + 1)]
            part = pltpu.roll(part, back, 2)[:, :, :broad]
            part = pltpu.roll(part, upward, 1)
            running += weights[slot] * jnp.where(sublane + shift < 8, part[:tall], part[1:])
        gathered.append(running)

    for copy in a_step + b_step:
        copy.wait_recv()
    total_a = acca[:, row] + ra2[0] + ra2[1] + ra2[2]
    total_b = accb[:, side] + rb2[...]
    total = jnp.concatenate([total_a, total_b], axis=0)
    weight = total[planes:]
    found = total[:planes] / (weight + 1e-05)
    got[:, core, side, row] = found
    probe_curve = jnp.sum(found * found * weight)
    probe_slope = jnp.sum(total[:planes] * found)
    probe_r, probe_i = (probes[0, :, core, side, row], probes[1, :, core, side, row])
    found_r, found_i = (found[:modes], found[modes:])
    mix[0, core, side, row] = jnp.sum(probe_r * found_r + probe_i * found_i, axis=0)
    mix[1, core, side, row] = jnp.sum(probe_r * found_i - probe_i * found_r, axis=0)

    spot = mix.at[:, core, side, row]
    mixes = [copies.start(spot, spot, peer) for peer in peers]

    def give(block, peer):
        return copies.start(block, block, peer)

    cutoff = 10
    one = got.at[:cutoff, core, side, row]
    give_a = [give(one, {"tx": j, "ty": col}) for j in along]
    one = got.at[cutoff:, core, side, row]
    give_b = [give(one, across)]
    for copy in give_a:
        copy.wait_recv()
    next_a = [give(got.at[:cutoff, core, side], across)]
    pass_on = [give(got.at[:cutoff, core, side], partner)]
    give_b[0].wait_recv()
    one = got.at[cutoff:, core, :, row]
    next_b = [give(one, {"tx": j, "ty": col}) for j in along]
    pass_on.append(give(one, partner))

    for copy in mixes:
        copy.wait_recv()
    mix_all = mix[...].reshape(2, tall, 8, broad)
    cross = jnp.sum(gathered[0] * mix_all[0] - gathered[1] * mix_all[1])
    mine[...] = in_rows((curve, slope, probe_curve, probe_slope, cross), broad)
    terms = [copies.start(mine, inbox.at[k], peer) for k, peer in enumerate(peers)]

    next_a[0].wait_recv()
    pass_on.append(give(got.at[:cutoff, core, 1 - side], partner))
    for copy, j in zip(next_b, along):
        copy.wait_recv()
    for j in along:
        pass_on.append(give(got.at[cutoff:, core, :, j], partner))
    for copy in terms:
        copy.wait_recv()
    sent = mine[...] + jnp.sum(inbox[...], axis=0)
    object_rate, probe_rate = solve_steps(
        sent[0:1], sent[4:5], sent[2:3], sent[1:2], sent[3:4]
    )
    object_rate = jnp.broadcast_to(object_rate, (8, broad))
    probe_rate = jnp.broadcast_to(probe_rate, (8, broad))
    if last:
        at = lax.broadcasted_iota(jnp.int32, (8, broad), 0)
        rates_out[...] = jnp.where(at == 0, object_rate, probe_rate)
        change_own[...] = change[...]
        for copy in pass_on:
            copy.wait_recv()
    else:
        both = jnp.concatenate([object_rate, object_rate], axis=1)
        new_map[...] = object_map[...] + both * wide[...]
        for copy in pass_on:
            copy.wait_recv()
        for part in range(2):
            new_probes[part] = probes[part] + probe_rate * got[part * modes : (part + 1) * modes]
    copies.finish()
    fold.finish()
    halo.finish()


def settle(last, places, weights, totals, sums, object_map, probes):
    _, rows, _, lanes = totals.shape
    modes, length = (probes.shape[1], probes.shape[-1])
    planes = 2 * modes
    high, broad = (rows // 3, lanes // 2)
    first_part = 11
    second_part = planes + 1 - first_part
    f32 = jnp.float32
    grid = (2, 2, 4)
    step = jax.ShapeDtypeStruct((planes,) + grid + (8, length), f32)
    if last:
        out_shape = (
            step,
            jax.ShapeDtypeStruct((2, high, 8, broad), f32),
            jax.ShapeDtypeStruct((8, broad), f32),
        )
    else:
        out_shape = (
            jax.ShapeDtypeStruct(object_map.shape, f32),
            jax.ShapeDtypeStruct((2, modes) + grid + (8, length), f32),
            step,
        )
    return pl.pallas_call(
        functools.partial(settle_kernel, last),
        out_shape=out_shape,
        in_specs=[scalars, scalars] + [memory] * 4,
        out_specs=(memory,) * 3,
        scratch_shapes=[
            pltpu.VMEM((6, 3, high // 2, 8, broad), f32),
            pltpu.VMEM((2, 3, high, 8, broad), f32),
            pltpu.VMEM((6, 3, high // 2, 8, broad), f32),
            pltpu.VMEM((planes + 1, 2, 4, 8, length), f32),
            pltpu.VMEM((planes + 1, 2, 4, 8, length), f32),
            pltpu.VMEM((first_part, 4, 8, length), f32),
            pltpu.VMEM((first_part, 4, 8, length), f32),
            pltpu.VMEM((3, first_part, 8, length), f32),
            pltpu.VMEM((3, second_part, 2, 8, length), f32),
            pltpu.VMEM((second_part, 2, 8, length), f32),
            pltpu.VMEM((second_part, 8, length), f32),
            pltpu.VMEM((2, high, 8, broad), f32),
        ]
        + halo_scratch(high, broad)
        + [
            pltpu.VMEM((2, rows, 8, lanes), f32),
            pltpu.VMEM((2, rows, 8, lanes), f32),
            pltpu.VMEM((2,) + grid + (8, length), f32),
            pltpu.VMEM((8, broad), f32),
            pltpu.VMEM((15, 8, broad), f32),
            pltpu.SemaphoreType.DMA((80,)),
            pltpu.SemaphoreType.DMA((80,)),
        ],
        compiler_params=pltpu.CompilerParams(
            collective_id=2 if last else 1,
            has_side_effects=True,
            vmem_limit_bytes=24 * 1024 * 1024,
        ),
        name="finish" if last else "settle",
    )(
        places,
        weights,
        totals,
        sums.reshape((planes + 1,) + grid + (8, length)),
        object_map,
        probes.reshape((2, modes) + grid + (8, length)),
    )


def apply_kernel(object_map, change, probes, step, rates, object_at, probes_at, tile, fresh, done):
    modes = probes.shape[1]
    high, broad = (change.shape[1], change.shape[3])
    object_rate = jnp.broadcast_to(rates[0:1], (8, broad))
    probe_rate = jnp.broadcast_to(rates[1:2], (8, broad))
    copies = []
    for part in range(2):
        for first in range(0, modes, 4):
            some = slice(first, first + 4)
            stepped = step[part * modes + first : part * modes + first + 4]
            moved = probes[part, some] + probe_rate * stepped
            fresh[part, some] = moved.reshape((4,) + fresh.shape[2:])
            block = (part, pl.ds(first, 4))
            copies.append(
                pltpu.make_async_copy(fresh.at[block], probes_at.at[block], done.at[len(copies)])
            )
            copies[-1].start()
    moved = object_map[:, high : 2 * high, :, :broad] + object_rate * change[...]
    tile[...] = moved.reshape(tile.shape)
    copies.append(pltpu.make_async_copy(tile, object_at, done.at[len(copies)]))
    copies[-1].start()
    for copy in copies:
        copy.wait()


def apply(object_map, change, probes, step, rates):
    _, high, _, broad = change.shape
    modes, length = (probes.shape[1], probes.shape[-1])
    shapes = ((2, 8 * high, broad), (2, modes, length, length))
    blocks = (2, modes, length // 8, 8, length)
    return pl.pallas_call(
        apply_kernel,
        out_shape=tuple(jax.ShapeDtypeStruct(shape, jnp.float32) for shape in shapes),
        in_specs=[memory] * 5,
        out_specs=(outside,) * 2,
        scratch_shapes=[pltpu.VMEM(shape, jnp.float32) for shape in shapes]
        + [pltpu.SemaphoreType.DMA((modes // 2 + 1,))],
        compiler_params=pltpu.CompilerParams(vmem_limit_bytes=8 * 1024 * 1024),
        name="apply",
    )(
        object_map,
        change,
        probes.reshape(blocks),
        step.reshape((2 * modes,) + blocks[2:]),
        rates,
    )


def direct(object_field, probe_modes, positions, counts, intensity):
    two, modes, length, _ = probe_modes.shape
    margin = length // 2
    _, height, breadth = object_field.shape
    anchor = jnp.stack(
        [lax.axis_index("tx") * height - margin, lax.axis_index("ty") * breadth - margin]
    )
    starts = positions - anchor[None, :]
    lanes = 2 * breadth
    places = window_places(starts, height + 2 * margin, lanes, length, margin)
    weights = (jnp.arange(positions.shape[0], dtype=jnp.int32) < counts[0]).astype(jnp.float32)
    object_map, probes, turns, measured = widen_tiles(
        object_field,
        probe_modes,
        jnp.asarray(split_tables(length)),
        intensity,
    )
    for repeat in range(ITERS):
        totals, sums = accumulate(object_map, probes, places, counts, measured, turns)
        last = repeat + 1 == ITERS
        settled = settle(last, places, weights, totals, sums, object_map, probes)
        if not last:
            object_map, probes, _ = settled
            probes = probes.reshape(probe_modes.shape)
    step, change, rates = settled
    return apply(object_map, change, probes, step, rates)


def shards(object_field, probe_modes, positions, counts, intensity):
    _, height, breadth = object_field.shape
    length = probe_modes.shape[-1]
    grid = (lax.axis_size("tx"), lax.axis_size("ty"))
    arguments = (object_field, probe_modes, positions, counts, intensity)
    if grid == (4, 4) and length == 128 and (2 * height, breadth) == (length, length):
        return direct(*arguments)
    return general(*arguments)


def solution(mesh):
    return jax.shard_map(
        shards,
        mesh=mesh,
        in_specs=(
            P("groups", "tx", "ty"),
            P("groups", None, None, None),
            P(("groups", "tx", "ty"), None),
            P(("groups", "tx", "ty")),
            P(("groups", "tx", "ty"), None, None),
        ),
        out_specs=(P("groups", "tx", "ty"), P("groups", None, None, None)),
        check_vma=False,
    )
```

```python
import functools

import jax
import jax.numpy as jnp
import ml_dtypes
import numpy as np
from jax import lax
from jax.experimental import pallas as pl
from jax.experimental.pallas import tpu as pltpu
from jax.sharding import PartitionSpec as P

ITERS = 2
memory = pl.BlockSpec(memory_space=pltpu.VMEM)
scalars = pl.BlockSpec(memory_space=pltpu.SMEM)


def with_halo(value, sides, width):
    for axis, dim in sides:
        size, length = (lax.axis_size(axis), value.shape[dim])
        up = [(i, (i + 1) % size) for i in range(size - 1)]
        down = [(j, i) for i, j in up]
        last = lax.slice_in_dim(value, length - width, length, axis=dim)
        first = lax.slice_in_dim(value, 0, width, axis=dim)
        before = lax.ppermute(last, axis, up)
        after = lax.ppermute(first, axis, down)
        value = jnp.concatenate([before, value, after], axis=dim)
    return value


def from_behind(block, axis, distance):
    devices = range(lax.axis_size(axis))
    route = [(i - distance, i) for i in devices if i - distance in devices]
    return lax.ppermute(block, axis, route)


def split_tables(length):
    indices = np.arange(length)
    angles = (indices[:, None] * indices[None, :] % length) * (2.0 * np.pi / length)
    cos_table = np.cos(angles) / np.sqrt(length)
    sin_table = np.sin(angles) / np.sqrt(length)
    forward = np.block([[cos_table, -sin_table], [sin_table, cos_table]])
    inverse = np.block([[cos_table, sin_table], [-sin_table, cos_table]])

    def stacked(table):
        coarse = table.astype(np.float32).astype(ml_dtypes.bfloat16)
        fine = (table - coarse.astype(np.float64)).astype(ml_dtypes.bfloat16)
        return np.concatenate([coarse, coarse, fine], axis=0)

    return np.stack([stacked(forward), stacked(inverse)])


def halves(value, axis):
    coarse = value.astype(jnp.bfloat16)
    fine = (value - coarse.astype(jnp.float32)).astype(jnp.bfloat16)
    return jnp.concatenate([coarse, fine, coarse], axis=axis)


def along_lanes(value, table):
    return jnp.dot(halves(value, 1), table, preferred_element_type=jnp.float32)


def along_rows(value, table):
    dims = (((0,), (0,)), ((), ()))
    return lax.dot_general(halves(value, 0), table, dims, preferred_element_type=jnp.float32)


def regroup(value, length):
    top, bottom = (value[:length], value[length:])
    return jnp.concatenate(
        [
            jnp.concatenate([top[:, :length], bottom[:, :length]], axis=1),
            jnp.concatenate([top[:, length:], bottom[:, length:]], axis=1),
        ],
        axis=0,
    )


def cut_window(places, slot, maps, plane, length):
    tall = length // 8
    tile, back, shift, upward = (places[slot, n] for n in range(4))
    sublane = lax.broadcasted_iota(jnp.int32, (tall, 8, length), 1)
    part = maps[plane, pl.ds(tile, tall + 1)]
    part = pltpu.roll(part, back, 2)[:, :, :length]
    part = pltpu.roll(part, upward, 1)
    return jnp.where(sublane + shift < 8, part[:tall], part[1:])


def lower(part, shift):
    tall, _, length = part.shape
    sublane = lax.broadcasted_iota(jnp.int32, (tall + 1, 8, length), 1)
    blank = jnp.zeros((1, 8, length), jnp.float32)
    part = pltpu.roll(part, lax.rem(shift, 8), 1)
    return jnp.where(
        sublane >= shift,
        jnp.concatenate([part, blank], axis=0),
        jnp.concatenate([blank, part], axis=0),
    )


def broaden(part, onward, breadth):
    margin = jnp.zeros(part.shape[:2] + (breadth - part.shape[2],), jnp.float32)
    return pltpu.roll(jnp.concatenate([part, margin], axis=2), onward, 2)


def add_placed(places, slot, part, totals, plane):
    breadth = totals.shape[-1]
    tile, back, shift = (places[slot, n] for n in range(3))
    onward = lax.rem(breadth - back, breadth)
    wide = broaden(lower(part, shift), onward, breadth)
    totals[plane, pl.ds(tile, wide.shape[0])] += wide


def lighting_of(probes):
    length = probes.shape[-1]
    lighting = jnp.zeros((length, length), jnp.float32)
    for mode in range(probes.shape[1]):
        lighting += probes[0, mode] * probes[0, mode] + probes[1, mode] * probes[1, mode]
    return lighting


def forward_slots(places, live, object_map, probes, intensity, turns, window, far, power):
    modes, length = (probes.shape[1], probes.shape[-1])
    slots = intensity.shape[0]
    coverage = jnp.zeros((length, length), jnp.float32)
    for slot in range(slots):
        for plane in range(2):
            part = cut_window(places, slot, object_map, plane, length)
            window[slot, plane] = part.reshape(length, length)
        lit = window[slot, 0] * window[slot, 0] + window[slot, 1] * window[slot, 1]
        coverage += jnp.where(slot < live, lit, 0.0)
    for pair in range(modes // 2):
        for slot in range(slots):
            waves = []
            for mode in (2 * pair, 2 * pair + 1):
                probe_r, probe_i = (probes[0, mode], probes[1, mode])
                obj_r, obj_i = (window[slot, 0], window[slot, 1])
                wave_r = probe_r * obj_r - probe_i * obj_i
                wave_i = probe_r * obj_i + probe_i * obj_r
                waves.append(jnp.concatenate([wave_r, wave_i], axis=1))
            half = regroup(along_lanes(jnp.concatenate(waves, axis=0), turns[0]), length)
            spread = along_rows(half, turns[0])
            far[slot, pair] = spread
            square = spread * spread
            square = square[:, :length] + square[:, length:]
            square = square[:length] + square[length:]
            if pair == 0:
                power[slot] = square
            else:
                power[slot] += square
    for slot in range(slots):
        ratio = jnp.sqrt(intensity[slot].T / jnp.maximum(power[slot], 1.0)) - 1.0
        power[slot] = jnp.where(slot < live, ratio, 0.0)
    return coverage


def backward_slot(slot, pair, probes_of, turns, window, far, power, terms):
    length = power.shape[-1]
    factor = power[slot]
    factor = jnp.concatenate([factor, factor], axis=1)
    factor = jnp.concatenate([factor, factor], axis=0)
    half = regroup(along_lanes(far[slot, pair] * factor, turns[1]), length)
    change = along_rows(half, turns[1])
    obj_r, obj_i = (window[slot, 0], window[slot, 1])
    terms_r = jnp.zeros((length, length), jnp.float32)
    terms_i = jnp.zeros((length, length), jnp.float32)
    moved_r, moved_i = ([], [])
    for which in range(2):
        rows = slice(which * length, (which + 1) * length)
        change_r, change_i = (change[rows, :length], change[rows, length:])
        probe_r, probe_i = probes_of(2 * pair + which)
        terms_r += probe_r * change_r + probe_i * change_i
        terms_i += probe_r * change_i - probe_i * change_r
        moved_r.append(obj_r * change_r + obj_i * change_i)
        moved_i.append(obj_r * change_i - obj_i * change_r)
    if pair == 0:
        terms[slot, 0] = terms_r
        terms[slot, 1] = terms_i
    else:
        terms[slot, 0] += terms_r
        terms[slot, 1] += terms_i
    return moved_r, moved_i


def slots_kernel(
    places, counts, object_map, probes, intensity, turns, totals, sums, window, far, power, terms
):
    modes, length = (probes.shape[1], probes.shape[-1])
    tall = length // 8
    live = counts[0]
    totals[...] = jnp.zeros_like(totals)
    terms[0, 2] = lighting_of(probes)
    sums[2 * modes] = forward_slots(
        places, live, object_map, probes, intensity, turns, window, far, power
    )
    for pair in range(modes // 2):
        for slot in range(intensity.shape[0]):
            moved_r, moved_i = backward_slot(
                slot, pair, lambda k: (probes[0, k], probes[1, k]), turns, window, far, power, terms
            )
            for which in range(2):
                mode = 2 * pair + which
                if slot == 0:
                    sums[mode] = moved_r[which]
                    sums[modes + mode] = moved_i[which]
                else:
                    sums[mode] += moved_r[which]
                    sums[modes + mode] += moved_i[which]

    def place_slot(slot, carry):
        for plane in range(3):
            part = terms[slot, plane] if plane < 2 else terms[0, 2]
            add_placed(places, slot, part.reshape(tall, 8, length), totals, plane)
        return carry

    lax.fori_loop(0, live, place_slot, 0)


def accumulate(object_map, probes, places, counts, intensity, turns):
    _, modes, length, _ = probes.shape
    slots = intensity.shape[0]
    return pl.pallas_call(
        slots_kernel,
        out_shape=(
            jax.ShapeDtypeStruct((3,) + object_map.shape[1:], jnp.float32),
            jax.ShapeDtypeStruct((2 * modes + 1, length, length), jnp.float32),
        ),
        in_specs=[scalars, scalars] + [memory] * 4,
        out_specs=(memory, memory),
        scratch_shapes=[
            pltpu.VMEM((slots, 2, length, length), jnp.float32),
            pltpu.VMEM((slots, modes // 2, 2 * length, 2 * length), jnp.float32),
            pltpu.VMEM((slots, length, length), jnp.float32),
            pltpu.VMEM((slots, 3, length, length), jnp.float32),
        ],
        compiler_params=pltpu.CompilerParams(vmem_limit_bytes=36 * 1024 * 1024),
        name="slots",
    )(places, counts, object_map, probes, intensity, turns)


def outward_kernel(
    places, counts, object_map, probes, intensity, turns, window, far, power, coverage, lit, light
):
    length = probes.shape[-1]
    live = counts[0]
    lit[...] = jnp.zeros_like(lit)
    light[...] = lighting_of(probes).reshape(light.shape)
    coverage[...] = forward_slots(
        places, live, object_map, probes, intensity, turns, window, far, power
    )

    def place_slot(slot, carry):
        add_placed(places, slot, light[...], lit, 0)
        return carry

    lax.fori_loop(0, live, place_slot, 0)


def outward(object_map, probes, places, counts, intensity, turns):
    _, modes, length, _ = probes.shape
    slots = intensity.shape[0]
    shapes = (
        (slots, 2, length, length),
        (slots, modes // 2, 2 * length, 2 * length),
        (slots, length, length),
        (length, length),
        (1,) + object_map.shape[1:],
    )
    return pl.pallas_call(
        outward_kernel,
        out_shape=tuple(jax.ShapeDtypeStruct(shape, jnp.float32) for shape in shapes),
        in_specs=[scalars, scalars] + [memory] * 4,
        out_specs=(memory,) * 5,
        scratch_shapes=[pltpu.VMEM((length // 8, 8, length), jnp.float32)],
        compiler_params=pltpu.CompilerParams(vmem_limit_bytes=20 * 1024 * 1024),
        name="outward",
    )(places, counts, object_map, probes, intensity, turns)


def window_places(starts, rows, lanes, length, lead):
    rows_at = jnp.clip(starts[:, 0], 0, rows - length)
    cols_at = jnp.clip(starts[:, 1], 0, lanes - length)
    tile = jnp.minimum(rows_at // 8, (rows - length) // 8 - 1)
    shift = rows_at - 8 * tile
    back = (lanes + lead - cols_at) % lanes
    return jnp.stack([tile, back, shift, (8 - shift) % 8], axis=1)


def mixing(probes, probe_step):
    mix_r = jnp.sum(probes[0] * probe_step[0] + probes[1] * probe_step[1], axis=0)
    mix_i = jnp.sum(probes[0] * probe_step[1] - probes[1] * probe_step[0], axis=0)
    return (mix_r, mix_i)


def cross_term(object_map, change, starts, active, mix_r, mix_i):
    length = mix_r.shape[-1]
    anchor_index = jnp.int32(0)

    def cross_visit_slot(running, element):
        corner_at, weight = element
        corner = (anchor_index, corner_at[0], corner_at[1])
        object_win = lax.dynamic_slice(object_map, corner, (2, length, length))
        change_win = lax.dynamic_slice(change, corner, (2, length, length))
        aligned = change_win[0] * object_win[0] + change_win[1] * object_win[1]
        rotated = change_win[0] * object_win[1] - change_win[1] * object_win[0]
        return (running + weight * jnp.sum(aligned * mix_r - rotated * mix_i), None)

    running, _ = lax.scan(cross_visit_slot, jnp.zeros((), jnp.float32), (starts, active))
    return running


def solve_steps(object_curve, cross_curve, probe_curve, object_slope, probe_slope):
    object_diag = 1.1 * object_curve + 0.001
    probe_diag = 1.1 * probe_curve + 0.001
    determinant = object_diag * probe_diag - cross_curve * cross_curve
    object_rate = (probe_diag * object_slope - cross_curve * probe_slope) / determinant
    probe_rate = (object_diag * probe_slope - cross_curve * object_slope) / determinant
    return (object_rate, probe_rate)


def widen(planes, margin):
    return with_halo(planes, (("tx", 1), ("ty", 2)), margin)


def fold_rims(totals, margin, height, breadth):
    middle = totals[:, margin : margin + height, :]
    for direction in (1, -1):
        border = totals[:, margin + height :, :] if direction == 1 else totals[:, :margin, :]
        arrived = from_behind(border, "tx", direction)
        if direction == 1:
            middle = jnp.concatenate([middle + arrived, middle[:, margin:, :]], axis=1)
        else:
            middle = jnp.concatenate([middle[:, : height - margin, :], middle + arrived], axis=1)
    interior = middle[:, :, margin : margin + breadth]
    for direction in (1, -1):
        border = middle[:, :, margin + breadth :] if direction == 1 else middle[:, :, :margin]
        arrived = from_behind(border, "ty", direction)
        if direction == 1:
            interior = jnp.concatenate(
                [interior[:, :, :margin] + arrived, interior[:, :, margin:]], axis=2
            )
        else:
            interior = jnp.concatenate(
                [interior[:, :, : breadth - margin], interior[:, :, breadth - margin :] + arrived],
                axis=2,
            )
    return interior


def general(object_field, probe_modes, positions, counts, intensity):
    length = probe_modes.shape[-1]
    margin = length // 2
    height = object_field.shape[1]
    breadth = object_field.shape[2]
    turns = split_tables(length)
    modes = probe_modes.shape[1]
    anchor = jnp.stack(
        [lax.axis_index("tx") * height - margin, lax.axis_index("ty") * breadth - margin]
    )
    starts = positions - anchor[None, :]
    active = (jnp.arange(positions.shape[0], dtype=jnp.int32) < counts[0]).astype(jnp.float32)
    places = window_places(starts, height + 2 * margin, breadth + 2 * margin, length, 0)
    object_map = object_field
    probes = probe_modes
    extended = widen(object_map, margin)
    for repeat in range(ITERS):
        tiled = extended.reshape(2, -1, 8, extended.shape[-1])
        totals, sums = accumulate(tiled, probes, places, counts, intensity, turns)
        totals = totals.reshape((3,) + extended.shape[1:])
        interior = fold_rims(totals, margin, height, breadth)
        change = interior[:2] / jnp.maximum(interior[2], 1.0)
        object_part = jnp.sum((change[0] * change[0] + change[1] * change[1]) * interior[2])
        slope_part = jnp.sum(interior[:2] * change)
        wide_change = widen(change, margin)
        sums = lax.psum(sums, ("tx", "ty"))
        probe_total = sums[: 2 * modes].reshape(probes.shape)
        weight_total = sums[2 * modes]
        probe_step = probe_total / (weight_total + 1e-05)
        mix_r, mix_i = mixing(probes, probe_step)
        cross_part = cross_term(extended, wide_change, starts, active, mix_r, mix_i)
        object_curve, cross_curve, object_slope = lax.psum(
            (object_part, cross_part, slope_part), ("tx", "ty")
        )
        probe_curve = jnp.sum(
            (probe_step[0] * probe_step[0] + probe_step[1] * probe_step[1]) * weight_total
        )
        probe_slope = jnp.sum(probe_total * probe_step)
        object_rate, probe_rate = solve_steps(
            object_curve, cross_curve, probe_curve, object_slope, probe_slope
        )
        object_map = object_map + object_rate * change
        probes = probes + probe_rate * probe_step
        if repeat + 1 < ITERS:
            extended = extended + object_rate * wide_change
    return (object_map, probes)

outside = pl.BlockSpec(memory_space=pltpu.HBM)
OTHERS = [(i, j) for i in range(4) for j in range(4) if i or j]
AROUND = [(i, j) for i in (-1, 0, 1) for j in (-1, 0, 1) if i or j]
SIDES = [(i, j) for i in (-1, 0, 1) for j in (-1, 1)]


def everyone(row, col):
    return [{"tx": (row + i) % 4, "ty": (col + j) % 4} for i, j in OTHERS]


def greet(peers):
    barrier = pltpu.get_barrier_semaphore()
    for peer in peers:
        pl.semaphore_signal(barrier, 1, device_id=peer, device_id_type=pl.DeviceIdType.MESH)
    pl.semaphore_wait(barrier, len(peers))


class Copies:
    def __init__(self, send, arrive):
        self.send, self.arrive, self.count = (send, arrive, 0)
        self.unsent = []

    def slots(self, number):
        self.count += number
        return self.count - number

    def make(self, source, target, index, landing, peer):
        return pltpu.make_async_remote_copy(
            src_ref=source,
            dst_ref=target,
            send_sem=self.send.at[index],
            recv_sem=self.arrive.at[landing],
            device_id=peer,
            device_id_type=pl.DeviceIdType.MESH,
        )

    def start(self, source, target, peer):
        index = self.slots(1)
        copy = self.make(source, target, index, index, peer)
        copy.start()
        self.unsent.append(copy)
        return copy

    def finish(self):
        for copy in self.unsent:
            copy.wait_send()


class Ring:
    def __init__(self, copies, row, col, source, target):
        self.copies, self.row, self.col = (copies, row, col)
        self.source, self.target = (source, target)
        self.base = copies.slots(len(AROUND))

    def each(self, what):
        for k, (i, j) in enumerate(AROUND):
            row, col = (self.row + i, self.col + j)
            inside = (row >= 0) & (row < 4) & (col >= 0) & (col < 4)
            pl.when(inside)(functools.partial(what, k, i, j, {"tx": row, "ty": col}))

    def outgoing(self, k, i, j, peer):
        landing = AROUND.index((-i, -j))
        return self.copies.make(
            self.source(i, j), self.target(-i, -j), self.base + k, self.base + landing, peer
        )

    def blank(self):
        for i, j in AROUND:
            row, col = (self.row + i, self.col + j)
            inside = (row >= 0) & (row < 4) & (col >= 0) & (col < 4)
            target = self.target(i, j)

            @pl.when(jnp.logical_not(inside))
            def _():
                target[...] = jnp.zeros(target.shape, jnp.float32)

    def start(self):
        self.each(lambda k, i, j, peer: self.outgoing(k, i, j, peer).start())

    def receive(self):
        def arrived(k, i, j, peer):
            index = self.base + k
            self.copies.make(self.source(i, j), self.target(i, j), index, index, peer).wait_recv()

        self.each(arrived)

    def finish(self):
        self.each(lambda k, i, j, peer: self.outgoing(k, i, j, peer).wait_send())


def early_lanes(value):
    return lax.broadcasted_iota(jnp.int32, value.shape, value.ndim - 1) < value.shape[-1] // 2


def turned(value):
    return pltpu.roll(value, value.shape[-1] // 2, value.ndim - 1)


def pack_first(block):
    half = block.shape[1] // 2
    top, bottom = (block[:, :half], block[:, half:])
    return jnp.where(early_lanes(top), top, turned(bottom))


def pack_last(block):
    half = block.shape[1] // 2
    top, bottom = (block[:, :half], block[:, half:])
    return jnp.where(early_lanes(top), turned(top), bottom)


def unpack(first, last):
    early = early_lanes(first)
    top = jnp.where(early, first, turned(last))
    bottom = jnp.where(early, turned(first), last)
    return jnp.concatenate([top, bottom], axis=1)


def row_range(i, high):
    return slice((i + 1) * high, (i + 2) * high)


def halo_ring(copies, row, col, own, packed, above, beside):
    def source(i, j):
        return own if j == 0 else packed.at[(j + 1) // 2]

    def target(i, j):
        return above.at[(i + 1) // 2] if j == 0 else beside.at[SIDES.index((i, j))]

    return Ring(copies, row, col, source, target)


def spread_halo(own, above, beside, wide):
    high, broad = (own.shape[1], own.shape[-1])
    for i in (-1, 0, 1):
        rows = row_range(i, high)
        wide[:, rows, :, :broad] = own if i == 0 else above[(i + 1) // 2]
        wide[:, rows, :, broad:] = unpack(
            beside[SIDES.index((i, 1))], beside[SIDES.index((i, -1))]
        )


def widen_kernel(
    own_at, probes_at, turns_at, intensity_at, wide, probes, turns, intensity, own, whole, packed, above,
    beside, local, send, arrive,
):
    row, col = (lax.axis_index("tx"), lax.axis_index("ty"))
    fetches = [
        pltpu.make_async_copy(source, target, local.at[k])
        for k, (source, target) in enumerate(
            ((own_at, own), (probes_at, probes), (turns_at, turns), (intensity_at, intensity))
        )
    ]
    for fetch in fetches:
        fetch.start()
    copies = Copies(send, arrive)
    ring = halo_ring(copies, row, col, whole, packed, above, beside)
    ring.blank()
    fetches[0].wait()
    block = own[...].reshape(2, own.shape[1] // 8, 8, own.shape[2])
    whole[...] = block
    packed[0] = pack_first(block)
    packed[1] = pack_last(block)
    greet(everyone(row, col))
    ring.start()
    for fetch in fetches[1:]:
        fetch.wait()
    ring.receive()
    spread_halo(block, above, beside, wide)
    ring.finish()


def halo_scratch(high, broad):
    return [
        pltpu.VMEM((2, 2, high // 2, 8, broad), jnp.float32),
        pltpu.VMEM((2, 2, high, 8, broad), jnp.float32),
        pltpu.VMEM((6, 2, high // 2, 8, broad), jnp.float32),
    ]


def widen_tiles(own, probes, turns, intensity):
    two, height, broad = own.shape
    high = height // 8

    def like(value):
        return jax.ShapeDtypeStruct(value.shape, value.dtype)

    return pl.pallas_call(
        widen_kernel,
        out_shape=(
            jax.ShapeDtypeStruct((two, 3 * high, 8, 2 * broad), jnp.float32),
            like(probes),
            like(turns),
            like(intensity),
        ),
        in_specs=[outside] * 4,
        out_specs=(memory,) * 4,
        scratch_shapes=[
            pltpu.VMEM(own.shape, jnp.float32),
            pltpu.VMEM((two, high, 8, broad), jnp.float32),
        ]
        + halo_scratch(high, broad)
        + [
            pltpu.SemaphoreType.DMA((4,)),
            pltpu.SemaphoreType.DMA((8,)),
            pltpu.SemaphoreType.DMA((8,)),
        ],
        compiler_params=pltpu.CompilerParams(
            collective_id=0, has_side_effects=True, vmem_limit_bytes=12 * 1024 * 1024
        ),
        name="widen",
    )(own, probes, turns, intensity)


def in_rows(values, lanes):
    at = lax.broadcasted_iota(jnp.int32, (8, lanes), 0)
    result = jnp.zeros((8, lanes), jnp.float32)
    for place, value in enumerate(values):
        result = jnp.where(at == place, value, result)
    return result


def settle_kernel(
    last, places, weights, object_map, probes, turns, window, far, power, coverage, lit, *rest
):
    if last:
        got, change_own, rates_out = rest[:3]
    else:
        new_map, new_probes, got = rest[:3]
    (
        sums, terms, padded, totals, fold_out, fold_over, fold_beside, r1, acc, ra1, acca, ra2,
        change, packed, above, beside, wide, held, mix, mine, inbox, send, arrive,
    ) = rest[3:]
    row, col = (lax.axis_index("tx"), lax.axis_index("ty"))
    core, side = (col % 2, col // 2)
    high, broad = (change.shape[1], change.shape[-1])
    tall, length = (2 * high, power.shape[-1])
    slots = places.shape[0]
    modes = got.shape[0] // 2
    pairs = modes // 2
    blocks = got.shape[1:]
    own_rows = row_range(0, high)
    peers = everyone(row, col)
    partner = {"tx": row, "ty": side * 2 + (1 - core)}
    across = {"tx": row, "ty": (1 - side) * 2 + core}
    along = [{"tx": (row + j) % 4, "ty": col} for j in (1, 2, 3)]
    copies = Copies(send, arrive)
    spot = (core, side, row)

    barrier = pltpu.get_barrier_semaphore()
    for peer in peers:
        pl.semaphore_signal(barrier, 1, device_id=peer, device_id_type=pl.DeviceIdType.MESH)

    def fold_source(i, j):
        if j == 0:
            return totals.at[:, row_range(i, high), :, slice(0, broad)]
        return fold_out.at[SIDES.index((i, j))]

    def fold_target(i, j):
        return fold_over.at[(i + 1) // 2] if j == 0 else fold_beside.at[SIDES.index((i, j))]

    fold = Ring(copies, row, col, fold_source, fold_target)
    halo = halo_ring(copies, row, col, change, packed, above, beside)
    fold.blank()
    halo.blank()
    padded[...] = jnp.zeros_like(padded)
    totals[:2] = jnp.zeros((2,) + totals.shape[1:], jnp.float32)
    totals[2] = lit[0]

    def probes_of(mode):
        return tuple(probes[part, mode].reshape(length, length) for part in range(2))

    def compute(pair, some):
        base = 1 + 4 * pair
        for slot in some:
            moved_r, moved_i = backward_slot(
                slot, pair, probes_of, turns, window, far, power, terms
            )
            for n, value in enumerate(moved_r + moved_i):
                value = value.reshape(blocks)
                if slot == 0:
                    sums[base + n] = value
                else:
                    sums[base + n] += value

    def chunk(pair):
        return slice(1 + 4 * pair if pair else 0, 5 + 4 * pair)

    reduced = {}
    shared = {}
    cores, fields, rows_sent, given, crossed, passed = ({}, {}, {}, {}, {}, [])

    def core_start(pair):
        part = chunk(pair)
        cores[pair] = copies.start(sums.at[part, 1 - core], r1.at[part], partner)

    def field_start(pair):
        part = chunk(pair)
        cores[pair].wait_recv()
        acc[part] = sums[part, core] + r1[part]
        fields[pair] = copies.start(acc.at[part, 1 - side], ra1.at[part], across)

    def rows_start(pair):
        part = chunk(pair)
        fields[pair].wait_recv()
        acca[part] = acc[part, side] + ra1[part]
        rows_sent[pair] = [
            copies.start(acca.at[part, peer["tx"]], ra2.at[k, part], peer)
            for k, peer in enumerate(along)
        ]

    def slab(pair):
        part = chunk(pair)
        for copy in rows_sent[pair]:
            copy.wait_recv()
        total = acca[part, row] + ra2[0, part] + ra2[1, part] + ra2[2, part]
        if pair == 0:
            shared["weight"] = total[0]
            total = total[1:]
        weight = shared["weight"]
        found = total / (weight + 1e-05)
        planes = slice(4 * pair, 4 * pair + 4)
        got[(planes,) + spot] = found
        some = slice(2 * pair, 2 * pair + 2)
        probe_r, probe_i = (probes[(0, some) + spot], probes[(1, some) + spot])
        for name, value in (
            ("mix_r", probe_r * found[:2] + probe_i * found[2:]),
            ("mix_i", probe_r * found[2:] - probe_i * found[:2]),
            ("curve", found * found * weight),
            ("slope", total * found),
        ):
            value = jnp.sum(value, axis=0)
            shared[name] = value if pair == 0 else shared[name] + value
        block = got.at[(planes,) + spot]
        given[pair] = [copies.start(block, block, peer) for peer in along]

    def cross_start(pair):
        for copy in given[pair]:
            copy.wait_recv()
        block = got.at[slice(4 * pair, 4 * pair + 4), core, side]
        crossed[pair] = copies.start(block, block, across)
        passed.append(copies.start(block, block, partner))

    def pass_start(pair):
        crossed[pair].wait_recv()
        block = got.at[slice(4 * pair, 4 * pair + 4), core, 1 - side]
        passed.append(copies.start(block, block, partner))

    early, late = (range(slots // 2), range(slots // 2, slots))
    sums[0] = coverage[...].reshape(blocks)
    compute(0, early)
    compute(0, late)
    pl.semaphore_wait(barrier, len(peers))
    core_start(0)
    compute(1, early)
    field_start(0)
    compute(1, late)
    core_start(1)
    compute(2, early)
    field_start(1)
    compute(2, late)
    core_start(2)
    rows_start(0)
    compute(3, early)
    field_start(2)
    compute(3, late)
    core_start(3)
    rows_start(1)

    for slot in range(slots):
        tile, back, shift = (places[slot, n] for n in range(3))
        onward = lax.rem(2 * broad - back, 2 * broad)
        for plane in range(2):
            keep = padded.at[slot % 2, plane]
            keep[high : high + tall + 1] = lower(terms[slot, plane].reshape(tall, 8, length), shift)
            part = padded[slot % 2, plane, pl.ds(high - tile, 3 * high)]
            totals[plane] += broaden(part, onward, 2 * broad)
    for k, (i, j) in enumerate(SIDES):
        block = totals[:, row_range(i, high), :, broad:]
        fold_out[k] = pack_first(block) if j == 1 else pack_last(block)
    fold.start()
    field_start(3)
    slab(0)
    rows_start(2)
    slab(1)
    cross_start(0)
    rows_start(3)

    fold.receive()
    firsts = fold_beside[SIDES.index((0, -1))]
    lasts = fold_beside[SIDES.index((0, 1))]
    for i in (-1, 1):
        firsts += fold_beside[SIDES.index((i, -1))]
        lasts += fold_beside[SIDES.index((i, 1))]
    interior = totals[:, own_rows, :, :broad] + fold_over[0] + fold_over[1]
    interior += unpack(firsts, lasts)
    moved = interior[:2] / jnp.maximum(interior[2], 1.0)
    change[...] = moved
    packed[0] = pack_first(moved)
    packed[1] = pack_last(moved)
    halo.start()
    slab(2)
    cross_start(1)
    slab(3)
    mix[(0,) + spot] = shared["mix_r"]
    mix[(1,) + spot] = shared["mix_i"]
    block = mix.at[(slice(None),) + spot]
    mixes = [copies.start(block, block, peer) for peer in peers]
    curve = jnp.sum((moved[0] * moved[0] + moved[1] * moved[1]) * interior[2])
    slope = jnp.sum(interior[:2] * moved)
    probe_curve = jnp.sum(shared["curve"])
    probe_slope = jnp.sum(shared["slope"])
    pass_start(0)
    cross_start(2)

    halo.receive()
    spread_halo(change[...], above, beside, wide)
    held[0] = wide[0] * object_map[0] + wide[1] * object_map[1]
    held[1] = wide[0] * object_map[1] - wide[1] * object_map[0]
    gathered = []
    for plane in range(2):
        running = jnp.zeros((tall, 8, broad), jnp.float32)
        for slot in range(slots):
            running += weights[slot] * cut_window(places, slot, held, plane, length)
        gathered.append(running)
    cross_start(3)
    pass_start(1)

    for copy in mixes:
        copy.wait_recv()
    mix_all = mix[...].reshape(2, tall, 8, broad)
    cross = jnp.sum(gathered[0] * mix_all[0] - gathered[1] * mix_all[1])
    mine[...] = in_rows((curve, slope, probe_curve, probe_slope, cross), broad)
    scalars_sent = [copies.start(mine, inbox.at[k], peer) for k, peer in enumerate(peers)]
    pass_start(2)
    pass_start(3)
    for copy in scalars_sent:
        copy.wait_recv()
    sent = mine[...] + jnp.sum(inbox[...], axis=0)
    object_rate, probe_rate = solve_steps(
        sent[0:1], sent[4:5], sent[2:3], sent[1:2], sent[3:4]
    )
    object_rate = jnp.broadcast_to(object_rate, (8, broad))
    probe_rate = jnp.broadcast_to(probe_rate, (8, broad))
    if last:
        at = lax.broadcasted_iota(jnp.int32, (8, broad), 0)
        rates_out[...] = jnp.where(at == 0, object_rate, probe_rate)
        change_own[...] = change[...]
    else:
        both = jnp.concatenate([object_rate, object_rate], axis=1)
        new_map[...] = object_map[...] + both * wide[...]
    for copy in passed:
        copy.wait_recv()
    if not last:
        for pair in range(pairs):
            some = slice(2 * pair, 2 * pair + 2)
            for part in range(2):
                first = 4 * pair + 2 * part
                new_probes[part, some] = probes[part, some] + probe_rate * got[first : first + 2]
    copies.finish()
    fold.finish()
    halo.finish()


def settle(last, places, weights, object_map, probes, turns, spread):
    _, rows, _, lanes = object_map.shape
    modes, length = (probes.shape[1], probes.shape[-1])
    slots = places.shape[0]
    planes = 2 * modes
    high, broad = (rows // 3, lanes // 2)
    f32 = jnp.float32
    grid = (2, 2, 4)
    step = jax.ShapeDtypeStruct((planes,) + grid + (8, length), f32)
    if last:
        out_shape = (
            step,
            jax.ShapeDtypeStruct((2, high, 8, broad), f32),
            jax.ShapeDtypeStruct((8, broad), f32),
        )
    else:
        out_shape = (
            jax.ShapeDtypeStruct(object_map.shape, f32),
            jax.ShapeDtypeStruct((2, modes) + grid + (8, length), f32),
            step,
        )
    return pl.pallas_call(
        functools.partial(settle_kernel, last),
        out_shape=out_shape,
        in_specs=[scalars, scalars] + [memory] * 8,
        out_specs=(memory,) * 3,
        scratch_shapes=[
            pltpu.VMEM((planes + 1,) + grid + (8, length), f32),
            pltpu.VMEM((slots, 2, length, length), f32),
            pltpu.VMEM((2, 2, 4 * high + 1, 8, length), f32),
            pltpu.VMEM((3, rows, 8, lanes), f32),
            pltpu.VMEM((6, 3, high // 2, 8, broad), f32),
            pltpu.VMEM((2, 3, high, 8, broad), f32),
            pltpu.VMEM((6, 3, high // 2, 8, broad), f32),
            pltpu.VMEM((planes + 1, 2, 4, 8, length), f32),
            pltpu.VMEM((planes + 1, 2, 4, 8, length), f32),
            pltpu.VMEM((planes + 1, 4, 8, length), f32),
            pltpu.VMEM((planes + 1, 4, 8, length), f32),
            pltpu.VMEM((3, planes + 1, 8, length), f32),
            pltpu.VMEM((2, high, 8, broad), f32),
        ]
        + halo_scratch(high, broad)
        + [
            pltpu.VMEM((2, rows, 8, lanes), f32),
            pltpu.VMEM((2, rows, 8, lanes), f32),
            pltpu.VMEM((2,) + grid + (8, length), f32),
            pltpu.VMEM((8, broad), f32),
            pltpu.VMEM((15, 8, broad), f32),
            pltpu.SemaphoreType.DMA((92,)),
            pltpu.SemaphoreType.DMA((92,)),
        ],
        compiler_params=pltpu.CompilerParams(
            collective_id=2 if last else 1,
            has_side_effects=True,
            vmem_limit_bytes=28 * 1024 * 1024,
        ),
        name="finish" if last else "settle",
    )(
        places,
        weights,
        object_map,
        probes.reshape((2, modes) + grid + (8, length)),
        turns,
        *spread,
    )


def apply_kernel(object_map, change, probes, step, rates, object_at, probes_at, tile, fresh, done):
    modes = probes.shape[1]
    high, broad = (change.shape[1], change.shape[3])
    object_rate = jnp.broadcast_to(rates[0:1], (8, broad))
    probe_rate = jnp.broadcast_to(rates[1:2], (8, broad))
    copies = []
    for part in range(2):
        for first in range(0, modes, 4):
            some = slice(first, first + 4)
            base = 2 * (first + part)
            stepped = jnp.concatenate(
                [step[base : base + 2], step[base + 4 : base + 6]], axis=0
            )
            moved = probes[part, some] + probe_rate * stepped
            fresh[part, some] = moved.reshape((4,) + fresh.shape[2:])
            block = (part, pl.ds(first, 4))
            copies.append(
                pltpu.make_async_copy(fresh.at[block], probes_at.at[block], done.at[len(copies)])
            )
            copies[-1].start()
    moved = object_map[:, high : 2 * high, :, :broad] + object_rate * change[...]
    tile[...] = moved.reshape(tile.shape)
    copies.append(pltpu.make_async_copy(tile, object_at, done.at[len(copies)]))
    copies[-1].start()
    for copy in copies:
        copy.wait()


def apply(object_map, change, probes, step, rates):
    _, high, _, broad = change.shape
    modes, length = (probes.shape[1], probes.shape[-1])
    shapes = ((2, 8 * high, broad), (2, modes, length, length))
    blocks = (2, modes, length // 8, 8, length)
    return pl.pallas_call(
        apply_kernel,
        out_shape=tuple(jax.ShapeDtypeStruct(shape, jnp.float32) for shape in shapes),
        in_specs=[memory] * 5,
        out_specs=(outside,) * 2,
        scratch_shapes=[pltpu.VMEM(shape, jnp.float32) for shape in shapes]
        + [pltpu.SemaphoreType.DMA((modes // 2 + 1,))],
        compiler_params=pltpu.CompilerParams(vmem_limit_bytes=8 * 1024 * 1024),
        name="apply",
    )(
        object_map,
        change,
        probes.reshape(blocks),
        step.reshape((2 * modes,) + blocks[2:]),
        rates,
    )


def direct(object_field, probe_modes, positions, counts, intensity):
    two, modes, length, _ = probe_modes.shape
    margin = length // 2
    _, height, breadth = object_field.shape
    anchor = jnp.stack(
        [lax.axis_index("tx") * height - margin, lax.axis_index("ty") * breadth - margin]
    )
    starts = positions - anchor[None, :]
    lanes = 2 * breadth
    places = window_places(starts, height + 2 * margin, lanes, length, margin)
    weights = (jnp.arange(positions.shape[0], dtype=jnp.int32) < counts[0]).astype(jnp.float32)
    object_map, probes, turns, measured = widen_tiles(
        object_field,
        probe_modes,
        jnp.asarray(split_tables(length)),
        intensity,
    )
    for repeat in range(ITERS):
        spread = outward(object_map, probes, places, counts, measured, turns)
        last = repeat + 1 == ITERS
        settled = settle(last, places, weights, object_map, probes, turns, spread)
        if not last:
            object_map, probes, _ = settled
            probes = probes.reshape(probe_modes.shape)
    step, change, rates = settled
    return apply(object_map, change, probes, step, rates)


def shards(object_field, probe_modes, positions, counts, intensity):
    _, height, breadth = object_field.shape
    length = probe_modes.shape[-1]
    grid = (lax.axis_size("tx"), lax.axis_size("ty"))
    arguments = (object_field, probe_modes, positions, counts, intensity)
    if grid == (4, 4) and length == 128 and (2 * height, breadth) == (length, length):
        return direct(*arguments)
    return general(*arguments)


def solution(mesh):
    return jax.shard_map(
        shards,
        mesh=mesh,
        in_specs=(
            P("groups", "tx", "ty"),
            P("groups", None, None, None),
            P(("groups", "tx", "ty"), None),
            P(("groups", "tx", "ty")),
            P(("groups", "tx", "ty"), None, None),
        ),
        out_specs=(P("groups", "tx", "ty"), P("groups", None, None, None)),
        check_vma=False,
    )
```

```python
import functools

import jax
import jax.numpy as jnp
import ml_dtypes
import numpy as np
from jax import lax
from jax.experimental import pallas as pl
from jax.experimental.pallas import tpu as pltpu
from jax.sharding import PartitionSpec as P

ITERS = 2
memory = pl.BlockSpec(memory_space=pltpu.VMEM)
scalars = pl.BlockSpec(memory_space=pltpu.SMEM)


def with_halo(value, sides, width):
    for axis, dim in sides:
        size, length = (lax.axis_size(axis), value.shape[dim])
        up = [(i, (i + 1) % size) for i in range(size - 1)]
        down = [(j, i) for i, j in up]
        last = lax.slice_in_dim(value, length - width, length, axis=dim)
        first = lax.slice_in_dim(value, 0, width, axis=dim)
        before = lax.ppermute(last, axis, up)
        after = lax.ppermute(first, axis, down)
        value = jnp.concatenate([before, value, after], axis=dim)
    return value


def from_behind(block, axis, distance):
    devices = range(lax.axis_size(axis))
    route = [(i - distance, i) for i in devices if i - distance in devices]
    return lax.ppermute(block, axis, route)


def split_tables(length):
    indices = np.arange(length)
    angles = (indices[:, None] * indices[None, :] % length) * (2.0 * np.pi / length)
    cos_table = np.cos(angles) / np.sqrt(length)
    sin_table = np.sin(angles) / np.sqrt(length)
    forward = np.block([[cos_table, -sin_table], [sin_table, cos_table]])
    inverse = np.block([[cos_table, sin_table], [-sin_table, cos_table]])

    def stacked(table):
        coarse = table.astype(np.float32).astype(ml_dtypes.bfloat16)
        fine = (table - coarse.astype(np.float64)).astype(ml_dtypes.bfloat16)
        return np.concatenate([coarse, coarse, fine], axis=0)

    return np.stack([stacked(forward), stacked(inverse)])


def halves(value, axis):
    coarse = value.astype(jnp.bfloat16)
    fine = (value - coarse.astype(jnp.float32)).astype(jnp.bfloat16)
    return jnp.concatenate([coarse, fine, coarse], axis=axis)


def along_lanes(value, table):
    return jnp.dot(halves(value, 1), table, preferred_element_type=jnp.float32)


def along_rows(value, table):
    dims = (((0,), (0,)), ((), ()))
    return lax.dot_general(halves(value, 0), table, dims, preferred_element_type=jnp.float32)


def regroup(value, length):
    top, bottom = (value[:length], value[length:])
    return jnp.concatenate(
        [
            jnp.concatenate([top[:, :length], bottom[:, :length]], axis=1),
            jnp.concatenate([top[:, length:], bottom[:, length:]], axis=1),
        ],
        axis=0,
    )


def cut_window(places, slot, maps, plane, length):
    tall = length // 8
    tile, back, shift, upward = (places[slot, n] for n in range(4))
    sublane = lax.broadcasted_iota(jnp.int32, (tall, 8, length), 1)
    part = maps[plane, pl.ds(tile, tall + 1)]
    part = pltpu.roll(part, back, 2)[:, :, :length]
    part = pltpu.roll(part, upward, 1)
    return jnp.where(sublane + shift < 8, part[:tall], part[1:])


def lower(part, shift):
    tall, _, length = part.shape
    sublane = lax.broadcasted_iota(jnp.int32, (tall + 1, 8, length), 1)
    blank = jnp.zeros((1, 8, length), jnp.float32)
    part = pltpu.roll(part, lax.rem(shift, 8), 1)
    return jnp.where(
        sublane >= shift,
        jnp.concatenate([part, blank], axis=0),
        jnp.concatenate([blank, part], axis=0),
    )


def broaden(part, onward, breadth):
    margin = jnp.zeros(part.shape[:2] + (breadth - part.shape[2],), jnp.float32)
    return pltpu.roll(jnp.concatenate([part, margin], axis=2), onward, 2)


def add_placed(places, slot, part, totals, plane):
    breadth = totals.shape[-1]
    tile, back, shift = (places[slot, n] for n in range(3))
    onward = lax.rem(breadth - back, breadth)
    wide = broaden(lower(part, shift), onward, breadth)
    totals[plane, pl.ds(tile, wide.shape[0])] += wide


def lighting_of(probes):
    length = probes.shape[-1]
    lighting = jnp.zeros((length, length), jnp.float32)
    for mode in range(probes.shape[1]):
        lighting += probes[0, mode] * probes[0, mode] + probes[1, mode] * probes[1, mode]
    return lighting


def forward_slots(places, live, object_map, probes, intensity, turns, window, far, power):
    modes, length = (probes.shape[1], probes.shape[-1])
    slots = intensity.shape[0]
    coverage = jnp.zeros((length, length), jnp.float32)
    for slot in range(slots):
        for plane in range(2):
            part = cut_window(places, slot, object_map, plane, length)
            window[slot, plane] = part.reshape(length, length)
        lit = window[slot, 0] * window[slot, 0] + window[slot, 1] * window[slot, 1]
        coverage += jnp.where(slot < live, lit, 0.0)
    for pair in range(modes // 2):
        for slot in range(slots):
            waves = []
            for mode in (2 * pair, 2 * pair + 1):
                probe_r, probe_i = (probes[0, mode], probes[1, mode])
                obj_r, obj_i = (window[slot, 0], window[slot, 1])
                wave_r = probe_r * obj_r - probe_i * obj_i
                wave_i = probe_r * obj_i + probe_i * obj_r
                waves.append(jnp.concatenate([wave_r, wave_i], axis=1))
            half = regroup(along_lanes(jnp.concatenate(waves, axis=0), turns[0]), length)
            spread = along_rows(half, turns[0])
            far[slot, pair] = spread
            square = spread * spread
            square = square[:, :length] + square[:, length:]
            square = square[:length] + square[length:]
            if pair == 0:
                power[slot] = square
            else:
                power[slot] += square
    for slot in range(slots):
        ratio = jnp.sqrt(intensity[slot].T / jnp.maximum(power[slot], 1.0)) - 1.0
        power[slot] = jnp.where(slot < live, ratio, 0.0)
    return coverage


def backward_slot(slot, pair, probes_of, turns, window, far, power, terms):
    length = power.shape[-1]
    factor = power[slot]
    factor = jnp.concatenate([factor, factor], axis=1)
    factor = jnp.concatenate([factor, factor], axis=0)
    half = regroup(along_lanes(far[slot, pair] * factor, turns[1]), length)
    change = along_rows(half, turns[1])
    obj_r, obj_i = (window[slot, 0], window[slot, 1])
    terms_r = jnp.zeros((length, length), jnp.float32)
    terms_i = jnp.zeros((length, length), jnp.float32)
    moved_r, moved_i = ([], [])
    for which in range(2):
        rows = slice(which * length, (which + 1) * length)
        change_r, change_i = (change[rows, :length], change[rows, length:])
        probe_r, probe_i = probes_of(2 * pair + which)
        terms_r += probe_r * change_r + probe_i * change_i
        terms_i += probe_r * change_i - probe_i * change_r
        moved_r.append(obj_r * change_r + obj_i * change_i)
        moved_i.append(obj_r * change_i - obj_i * change_r)
    if pair == 0:
        terms[slot, 0] = terms_r
        terms[slot, 1] = terms_i
    else:
        terms[slot, 0] += terms_r
        terms[slot, 1] += terms_i
    return moved_r, moved_i


def slots_kernel(
    places, counts, object_map, probes, intensity, turns, totals, sums, window, far, power, terms
):
    modes, length = (probes.shape[1], probes.shape[-1])
    tall = length // 8
    live = counts[0]
    totals[...] = jnp.zeros_like(totals)
    terms[0, 2] = lighting_of(probes)
    sums[2 * modes] = forward_slots(
        places, live, object_map, probes, intensity, turns, window, far, power
    )
    for pair in range(modes // 2):
        for slot in range(intensity.shape[0]):
            moved_r, moved_i = backward_slot(
                slot, pair, lambda k: (probes[0, k], probes[1, k]), turns, window, far, power, terms
            )
            for which in range(2):
                mode = 2 * pair + which
                if slot == 0:
                    sums[mode] = moved_r[which]
                    sums[modes + mode] = moved_i[which]
                else:
                    sums[mode] += moved_r[which]
                    sums[modes + mode] += moved_i[which]

    def place_slot(slot, carry):
        for plane in range(3):
            part = terms[slot, plane] if plane < 2 else terms[0, 2]
            add_placed(places, slot, part.reshape(tall, 8, length), totals, plane)
        return carry

    lax.fori_loop(0, live, place_slot, 0)


def accumulate(object_map, probes, places, counts, intensity, turns):
    _, modes, length, _ = probes.shape
    slots = intensity.shape[0]
    return pl.pallas_call(
        slots_kernel,
        out_shape=(
            jax.ShapeDtypeStruct((3,) + object_map.shape[1:], jnp.float32),
            jax.ShapeDtypeStruct((2 * modes + 1, length, length), jnp.float32),
        ),
        in_specs=[scalars, scalars] + [memory] * 4,
        out_specs=(memory, memory),
        scratch_shapes=[
            pltpu.VMEM((slots, 2, length, length), jnp.float32),
            pltpu.VMEM((slots, modes // 2, 2 * length, 2 * length), jnp.float32),
            pltpu.VMEM((slots, length, length), jnp.float32),
            pltpu.VMEM((slots, 3, length, length), jnp.float32),
        ],
        compiler_params=pltpu.CompilerParams(vmem_limit_bytes=36 * 1024 * 1024),
        name="slots",
    )(places, counts, object_map, probes, intensity, turns)


def outward_kernel(
    places, counts, object_map, probes, intensity, turns, window, far, power, coverage, lit, light
):
    length = probes.shape[-1]
    live = counts[0]
    lit[...] = jnp.zeros_like(lit)
    light[...] = lighting_of(probes).reshape(light.shape)
    coverage[...] = forward_slots(
        places, live, object_map, probes, intensity, turns, window, far, power
    )

    def place_slot(slot, carry):
        add_placed(places, slot, light[...], lit, 0)
        return carry

    lax.fori_loop(0, live, place_slot, 0)


def outward(object_map, probes, places, counts, intensity, turns):
    _, modes, length, _ = probes.shape
    slots = intensity.shape[0]
    shapes = (
        (slots, 2, length, length),
        (slots, modes // 2, 2 * length, 2 * length),
        (slots, length, length),
        (length, length),
        (1,) + object_map.shape[1:],
    )
    return pl.pallas_call(
        outward_kernel,
        out_shape=tuple(jax.ShapeDtypeStruct(shape, jnp.float32) for shape in shapes),
        in_specs=[scalars, scalars] + [memory] * 4,
        out_specs=(memory,) * 5,
        scratch_shapes=[pltpu.VMEM((length // 8, 8, length), jnp.float32)],
        compiler_params=pltpu.CompilerParams(vmem_limit_bytes=20 * 1024 * 1024),
        name="outward",
    )(places, counts, object_map, probes, intensity, turns)


def window_places(starts, rows, lanes, length, lead):
    rows_at = jnp.clip(starts[:, 0], 0, rows - length)
    cols_at = jnp.clip(starts[:, 1], 0, lanes - length)
    tile = jnp.minimum(rows_at // 8, (rows - length) // 8 - 1)
    shift = rows_at - 8 * tile
    back = (lanes + lead - cols_at) % lanes
    return jnp.stack([tile, back, shift, (8 - shift) % 8], axis=1)


def mixing(probes, probe_step):
    mix_r = jnp.sum(probes[0] * probe_step[0] + probes[1] * probe_step[1], axis=0)
    mix_i = jnp.sum(probes[0] * probe_step[1] - probes[1] * probe_step[0], axis=0)
    return (mix_r, mix_i)


def cross_term(object_map, change, starts, active, mix_r, mix_i):
    length = mix_r.shape[-1]
    anchor_index = jnp.int32(0)

    def cross_visit_slot(running, element):
        corner_at, weight = element
        corner = (anchor_index, corner_at[0], corner_at[1])
        object_win = lax.dynamic_slice(object_map, corner, (2, length, length))
        change_win = lax.dynamic_slice(change, corner, (2, length, length))
        aligned = change_win[0] * object_win[0] + change_win[1] * object_win[1]
        rotated = change_win[0] * object_win[1] - change_win[1] * object_win[0]
        return (running + weight * jnp.sum(aligned * mix_r - rotated * mix_i), None)

    running, _ = lax.scan(cross_visit_slot, jnp.zeros((), jnp.float32), (starts, active))
    return running


def solve_steps(object_curve, cross_curve, probe_curve, object_slope, probe_slope):
    object_diag = 1.1 * object_curve + 0.001
    probe_diag = 1.1 * probe_curve + 0.001
    determinant = object_diag * probe_diag - cross_curve * cross_curve
    object_rate = (probe_diag * object_slope - cross_curve * probe_slope) / determinant
    probe_rate = (object_diag * probe_slope - cross_curve * object_slope) / determinant
    return (object_rate, probe_rate)


def widen(planes, margin):
    return with_halo(planes, (("tx", 1), ("ty", 2)), margin)


def fold_rims(totals, margin, height, breadth):
    middle = totals[:, margin : margin + height, :]
    for direction in (1, -1):
        border = totals[:, margin + height :, :] if direction == 1 else totals[:, :margin, :]
        arrived = from_behind(border, "tx", direction)
        if direction == 1:
            middle = jnp.concatenate([middle + arrived, middle[:, margin:, :]], axis=1)
        else:
            middle = jnp.concatenate([middle[:, : height - margin, :], middle + arrived], axis=1)
    interior = middle[:, :, margin : margin + breadth]
    for direction in (1, -1):
        border = middle[:, :, margin + breadth :] if direction == 1 else middle[:, :, :margin]
        arrived = from_behind(border, "ty", direction)
        if direction == 1:
            interior = jnp.concatenate(
                [interior[:, :, :margin] + arrived, interior[:, :, margin:]], axis=2
            )
        else:
            interior = jnp.concatenate(
                [interior[:, :, : breadth - margin], interior[:, :, breadth - margin :] + arrived],
                axis=2,
            )
    return interior


def general(object_field, probe_modes, positions, counts, intensity):
    length = probe_modes.shape[-1]
    margin = length // 2
    height = object_field.shape[1]
    breadth = object_field.shape[2]
    turns = split_tables(length)
    modes = probe_modes.shape[1]
    anchor = jnp.stack(
        [lax.axis_index("tx") * height - margin, lax.axis_index("ty") * breadth - margin]
    )
    starts = positions - anchor[None, :]
    active = (jnp.arange(positions.shape[0], dtype=jnp.int32) < counts[0]).astype(jnp.float32)
    places = window_places(starts, height + 2 * margin, breadth + 2 * margin, length, 0)
    object_map = object_field
    probes = probe_modes
    extended = widen(object_map, margin)
    for repeat in range(ITERS):
        tiled = extended.reshape(2, -1, 8, extended.shape[-1])
        totals, sums = accumulate(tiled, probes, places, counts, intensity, turns)
        totals = totals.reshape((3,) + extended.shape[1:])
        interior = fold_rims(totals, margin, height, breadth)
        change = interior[:2] / jnp.maximum(interior[2], 1.0)
        object_part = jnp.sum((change[0] * change[0] + change[1] * change[1]) * interior[2])
        slope_part = jnp.sum(interior[:2] * change)
        wide_change = widen(change, margin)
        sums = lax.psum(sums, ("tx", "ty"))
        probe_total = sums[: 2 * modes].reshape(probes.shape)
        weight_total = sums[2 * modes]
        probe_step = probe_total / (weight_total + 1e-05)
        mix_r, mix_i = mixing(probes, probe_step)
        cross_part = cross_term(extended, wide_change, starts, active, mix_r, mix_i)
        object_curve, cross_curve, object_slope = lax.psum(
            (object_part, cross_part, slope_part), ("tx", "ty")
        )
        probe_curve = jnp.sum(
            (probe_step[0] * probe_step[0] + probe_step[1] * probe_step[1]) * weight_total
        )
        probe_slope = jnp.sum(probe_total * probe_step)
        object_rate, probe_rate = solve_steps(
            object_curve, cross_curve, probe_curve, object_slope, probe_slope
        )
        object_map = object_map + object_rate * change
        probes = probes + probe_rate * probe_step
        if repeat + 1 < ITERS:
            extended = extended + object_rate * wide_change
    return (object_map, probes)

outside = pl.BlockSpec(memory_space=pltpu.HBM)
OTHERS = [(i, j) for i in range(4) for j in range(4) if i or j]
AROUND = [(i, j) for i in (-1, 0, 1) for j in (-1, 0, 1) if i or j]
SIDES = [(i, j) for i in (-1, 0, 1) for j in (-1, 1)]


def everyone(row, col):
    return [{"tx": (row + i) % 4, "ty": (col + j) % 4} for i, j in OTHERS]


def greet(peers):
    barrier = pltpu.get_barrier_semaphore()
    for peer in peers:
        pl.semaphore_signal(barrier, 1, device_id=peer, device_id_type=pl.DeviceIdType.MESH)
    pl.semaphore_wait(barrier, len(peers))


class Copies:
    def __init__(self, send, arrive):
        self.send, self.arrive, self.count = (send, arrive, 0)
        self.unsent = []

    def slots(self, number):
        self.count += number
        return self.count - number

    def make(self, source, target, index, landing, peer):
        return pltpu.make_async_remote_copy(
            src_ref=source,
            dst_ref=target,
            send_sem=self.send.at[index],
            recv_sem=self.arrive.at[landing],
            device_id=peer,
            device_id_type=pl.DeviceIdType.MESH,
        )

    def start(self, source, target, peer):
        index = self.slots(1)
        copy = self.make(source, target, index, index, peer)
        copy.start()
        self.unsent.append(copy)
        return copy

    def group(self, items, view):
        index = self.slots(1)
        for source, target, peer in items:
            self.make(source, target, index, index, peer).start()
        whole = self.make(view, view, index, index, items[0][2])
        self.unsent.append(whole)
        return whole

    def finish(self):
        for copy in self.unsent:
            copy.wait_send()
        self.unsent = []


class Ring:
    def __init__(self, copies, row, col, source, target):
        self.copies, self.row, self.col = (copies, row, col)
        self.source, self.target = (source, target)
        self.base = copies.slots(len(AROUND))

    def each(self, what):
        for k, (i, j) in enumerate(AROUND):
            row, col = (self.row + i, self.col + j)
            inside = (row >= 0) & (row < 4) & (col >= 0) & (col < 4)
            pl.when(inside)(functools.partial(what, k, i, j, {"tx": row, "ty": col}))

    def outgoing(self, k, i, j, peer):
        landing = AROUND.index((-i, -j))
        return self.copies.make(
            self.source(i, j), self.target(-i, -j), self.base + k, self.base + landing, peer
        )

    def blank(self):
        for i, j in AROUND:
            row, col = (self.row + i, self.col + j)
            inside = (row >= 0) & (row < 4) & (col >= 0) & (col < 4)
            target = self.target(i, j)

            @pl.when(jnp.logical_not(inside))
            def _():
                target[...] = jnp.zeros(target.shape, jnp.float32)

    def start(self):
        self.each(lambda k, i, j, peer: self.outgoing(k, i, j, peer).start())

    def receive(self):
        def arrived(k, i, j, peer):
            index = self.base + k
            self.copies.make(self.source(i, j), self.target(i, j), index, index, peer).wait_recv()

        self.each(arrived)

    def finish(self):
        self.each(lambda k, i, j, peer: self.outgoing(k, i, j, peer).wait_send())


def early_lanes(value):
    return lax.broadcasted_iota(jnp.int32, value.shape, value.ndim - 1) < value.shape[-1] // 2


def turned(value):
    return pltpu.roll(value, value.shape[-1] // 2, value.ndim - 1)


def pack_first(block):
    half = block.shape[1] // 2
    top, bottom = (block[:, :half], block[:, half:])
    return jnp.where(early_lanes(top), top, turned(bottom))


def pack_last(block):
    half = block.shape[1] // 2
    top, bottom = (block[:, :half], block[:, half:])
    return jnp.where(early_lanes(top), turned(top), bottom)


def unpack(first, last):
    early = early_lanes(first)
    top = jnp.where(early, first, turned(last))
    bottom = jnp.where(early, turned(first), last)
    return jnp.concatenate([top, bottom], axis=1)


def row_range(i, high):
    return slice((i + 1) * high, (i + 2) * high)


def halo_ring(copies, row, col, own, packed, above, beside):
    def source(i, j):
        return own if j == 0 else packed.at[(j + 1) // 2]

    def target(i, j):
        return above.at[(i + 1) // 2] if j == 0 else beside.at[SIDES.index((i, j))]

    return Ring(copies, row, col, source, target)


def spread_halo(own, above, beside, wide):
    high, broad = (own.shape[1], own.shape[-1])
    for i in (-1, 0, 1):
        rows = row_range(i, high)
        wide[:, rows, :, :broad] = own if i == 0 else above[(i + 1) // 2]
        wide[:, rows, :, broad:] = unpack(
            beside[SIDES.index((i, 1))], beside[SIDES.index((i, -1))]
        )


def widen_kernel(
    own_at, probes_at, turns_at, intensity_at, wide, probes, turns, intensity, own, whole, packed, above,
    beside, local, send, arrive,
):
    row, col = (lax.axis_index("tx"), lax.axis_index("ty"))
    fetches = [
        pltpu.make_async_copy(source, target, local.at[k])
        for k, (source, target) in enumerate(
            ((own_at, own), (probes_at, probes), (turns_at, turns), (intensity_at, intensity))
        )
    ]
    for fetch in fetches:
        fetch.start()
    copies = Copies(send, arrive)
    ring = halo_ring(copies, row, col, whole, packed, above, beside)
    ring.blank()
    fetches[0].wait()
    block = own[...].reshape(2, own.shape[1] // 8, 8, own.shape[2])
    whole[...] = block
    packed[0] = pack_first(block)
    packed[1] = pack_last(block)
    greet(everyone(row, col))
    ring.start()
    for fetch in fetches[1:]:
        fetch.wait()
    ring.receive()
    spread_halo(block, above, beside, wide)
    ring.finish()


def halo_scratch(high, broad):
    return [
        pltpu.VMEM((2, 2, high // 2, 8, broad), jnp.float32),
        pltpu.VMEM((2, 2, high, 8, broad), jnp.float32),
        pltpu.VMEM((6, 2, high // 2, 8, broad), jnp.float32),
    ]


def widen_tiles(own, probes, turns, intensity):
    two, height, broad = own.shape
    high = height // 8

    def like(value):
        return jax.ShapeDtypeStruct(value.shape, value.dtype)

    return pl.pallas_call(
        widen_kernel,
        out_shape=(
            jax.ShapeDtypeStruct((two, 3 * high, 8, 2 * broad), jnp.float32),
            like(probes),
            like(turns),
            like(intensity),
        ),
        in_specs=[outside] * 4,
        out_specs=(memory,) * 4,
        scratch_shapes=[
            pltpu.VMEM(own.shape, jnp.float32),
            pltpu.VMEM((two, high, 8, broad), jnp.float32),
        ]
        + halo_scratch(high, broad)
        + [
            pltpu.SemaphoreType.DMA((4,)),
            pltpu.SemaphoreType.DMA((8,)),
            pltpu.SemaphoreType.DMA((8,)),
        ],
        compiler_params=pltpu.CompilerParams(
            collective_id=0, has_side_effects=True, vmem_limit_bytes=12 * 1024 * 1024
        ),
        name="widen",
    )(own, probes, turns, intensity)


def in_rows(values, lanes):
    at = lax.broadcasted_iota(jnp.int32, (8, lanes), 0)
    result = jnp.zeros((8, lanes), jnp.float32)
    for place, value in enumerate(values):
        result = jnp.where(at == place, value, result)
    return result


def settle_kernel(
    last, places, weights, object_map, probes, turns, window, far, power, coverage, lit, *rest
):
    if last:
        got, change_own, rates_out = rest[:3]
    else:
        new_map, new_probes, got = rest[:3]
    (
        sums, terms, padded, totals, fold_out, fold_over, fold_beside, r1, acc, ra1, acca, ra2,
        change, packed, above, beside, wide, held, mine, inbox, send, arrive,
    ) = rest[3:]
    row, col = (lax.axis_index("tx"), lax.axis_index("ty"))
    core, side = (col % 2, col // 2)
    high, broad = (change.shape[1], change.shape[-1])
    tall, length = (2 * high, power.shape[-1])
    slots = places.shape[0]
    modes = probes.shape[1]
    pairs = modes // 2
    blocks = got.shape[1:]
    mix_planes = slice(2 * modes, 2 * modes + 2)
    own_rows = row_range(0, high)
    peers = everyone(row, col)
    partner = {"tx": row, "ty": side * 2 + (1 - core)}
    across = {"tx": row, "ty": (1 - side) * 2 + core}
    along = [{"tx": (row + j) % 4, "ty": col} for j in (1, 2, 3)]
    copies = Copies(send, arrive)
    spot = (core, side, row)

    barrier = pltpu.get_barrier_semaphore()
    for peer in peers:
        pl.semaphore_signal(barrier, 1, device_id=peer, device_id_type=pl.DeviceIdType.MESH)

    def fold_source(i, j):
        if j == 0:
            return totals.at[:, row_range(i, high), :, slice(0, broad)]
        return fold_out.at[SIDES.index((i, j))]

    def fold_target(i, j):
        return fold_over.at[(i + 1) // 2] if j == 0 else fold_beside.at[SIDES.index((i, j))]

    fold = Ring(copies, row, col, fold_source, fold_target)
    halo = halo_ring(copies, row, col, change, packed, above, beside)
    fold.blank()
    halo.blank()
    padded[...] = jnp.zeros_like(padded)
    totals[:2] = jnp.zeros((2,) + totals.shape[1:], jnp.float32)
    totals[2] = lit[0]

    def probes_of(mode):
        return tuple(probes[part, mode].reshape(length, length) for part in range(2))

    def compute(pair, some):
        base = 1 + 4 * pair
        for slot in some:
            moved_r, moved_i = backward_slot(
                slot, pair, probes_of, turns, window, far, power, terms
            )
            for n, value in enumerate(moved_r + moved_i):
                value = value.reshape(blocks)
                if slot == 0:
                    sums[base + n] = value
                else:
                    sums[base + n] += value

    def chunk(n):
        return slice(0, modes + 1) if n == 0 else slice(modes + 1, 2 * modes + 1)

    def shares(n):
        return slice(0, modes) if n == 0 else slice(modes, 2 * modes + 2)

    shared = {}
    cores, fields, rows_sent, given, crossed, passed = ({}, {}, {}, {}, {}, {})

    def core_start(n):
        part = chunk(n)
        cores[n] = copies.start(sums.at[part, 1 - core], r1.at[part], partner)

    def field_start(n):
        part = chunk(n)
        cores[n].wait_recv()
        acc[part] = sums[part, core] + r1[part]
        fields[n] = copies.start(acc.at[part, 1 - side], ra1.at[part], across)

    def rows_start(n):
        part = chunk(n)
        fields[n].wait_recv()
        acca[part] = acc[part, side] + ra1[part]
        items = [
            (acca.at[part, peer["tx"]], ra2.at[k, part], peer) for k, peer in enumerate(along)
        ]
        rows_sent[n] = copies.group(items, ra2.at[:, part])

    def slab(n):
        part = chunk(n)
        rows_sent[n].wait_recv()
        total = acca[part, row] + ra2[0, part] + ra2[1, part] + ra2[2, part]
        if n == 0:
            shared["weight"] = total[0]
            total = total[1:]
        weight = shared["weight"]
        found = total / (weight + 1e-05)
        got[(slice(n * modes, (n + 1) * modes),) + spot] = found
        for pair in range(n * pairs // 2, (n + 1) * pairs // 2):
            some = slice(2 * pair, 2 * pair + 2)
            base = 4 * pair - n * modes
            probe_r, probe_i = (probes[(0, some) + spot], probes[(1, some) + spot])
            found_r, found_i = (found[base : base + 2], found[base + 2 : base + 4])
            for name, value in (
                ("mix_r", probe_r * found_r + probe_i * found_i),
                ("mix_i", probe_r * found_i - probe_i * found_r),
            ):
                value = jnp.sum(value, axis=0)
                shared[name] = shared[name] + value if name in shared else value
        for name, value in (("curve", found * found * weight), ("slope", total * found)):
            value = jnp.sum(value, axis=0)
            shared[name] = shared[name] + value if name in shared else value
        if n == 1:
            got[(2 * modes,) + spot] = shared["mix_r"]
            got[(2 * modes + 1,) + spot] = shared["mix_i"]
        block = got.at[(shares(n),) + spot]
        view = got.at[shares(n), core, side, pl.ds(0, 3)]
        given[n] = copies.group([(block, block, peer) for peer in along], view)

    def cross_start(n):
        given[n].wait_recv()
        block = got.at[shares(n), core, side]
        crossed[n] = copies.start(block, block, across)

    def pass_start(n):
        crossed[n].wait_recv()
        block = got.at[shares(n), core]
        passed[n] = copies.start(block, block, partner)

    everything = range(slots)
    sums[0] = coverage[...].reshape(blocks)
    compute(0, everything)
    compute(1, everything)
    pl.semaphore_wait(barrier, len(peers))
    core_start(0)
    compute(2, everything)
    field_start(0)
    compute(3, everything)
    core_start(1)
    rows_start(0)

    for slot in range(slots):
        tile, back, shift = (places[slot, n] for n in range(3))
        onward = lax.rem(2 * broad - back, 2 * broad)
        for plane in range(2):
            keep = padded.at[slot % 2, plane]
            keep[high : high + tall + 1] = lower(terms[slot, plane].reshape(tall, 8, length), shift)
            part = padded[slot % 2, plane, pl.ds(high - tile, 3 * high)]
            totals[plane] += broaden(part, onward, 2 * broad)
    for k, (i, j) in enumerate(SIDES):
        block = totals[:, row_range(i, high), :, broad:]
        fold_out[k] = pack_first(block) if j == 1 else pack_last(block)
    fold.start()
    field_start(1)
    slab(0)
    rows_start(1)

    fold.receive()
    firsts = fold_beside[SIDES.index((0, -1))]
    lasts = fold_beside[SIDES.index((0, 1))]
    for i in (-1, 1):
        firsts += fold_beside[SIDES.index((i, -1))]
        lasts += fold_beside[SIDES.index((i, 1))]
    interior = totals[:, own_rows, :, :broad] + fold_over[0] + fold_over[1]
    interior += unpack(firsts, lasts)
    moved = interior[:2] / jnp.maximum(interior[2], 1.0)
    change[...] = moved
    packed[0] = pack_first(moved)
    packed[1] = pack_last(moved)
    halo.start()
    cross_start(0)
    curve = jnp.sum((moved[0] * moved[0] + moved[1] * moved[1]) * interior[2])
    slope = jnp.sum(interior[:2] * moved)
    slab(1)
    probe_curve = jnp.sum(shared["curve"])
    probe_slope = jnp.sum(shared["slope"])
    pass_start(0)
    cross_start(1)

    halo.receive()
    spread_halo(change[...], above, beside, wide)
    held[0] = wide[0] * object_map[0] + wide[1] * object_map[1]
    held[1] = wide[0] * object_map[1] - wide[1] * object_map[0]
    gathered = []
    for plane in range(2):
        running = jnp.zeros((tall, 8, broad), jnp.float32)
        for slot in range(slots):
            running += weights[slot] * cut_window(places, slot, held, plane, length)
        gathered.append(running)
    pass_start(1)
    copies.finish()
    fold.finish()
    halo.finish()
    passed[1].wait_recv()
    mix_all = got[mix_planes].reshape(2, tall, 8, broad)
    cross = jnp.sum(gathered[0] * mix_all[0] - gathered[1] * mix_all[1])
    mine[...] = in_rows((curve, slope, probe_curve, probe_slope, cross), broad)
    scalars_sent = copies.group(
        [(mine, inbox.at[k], peer) for k, peer in enumerate(peers)], inbox
    )
    passed[0].wait_recv()
    scalars_sent.wait_recv()
    sent = mine[...] + jnp.sum(inbox[...], axis=0)
    object_rate, probe_rate = solve_steps(
        sent[0:1], sent[4:5], sent[2:3], sent[1:2], sent[3:4]
    )
    object_rate = jnp.broadcast_to(object_rate, (8, broad))
    probe_rate = jnp.broadcast_to(probe_rate, (8, broad))
    if last:
        at = lax.broadcasted_iota(jnp.int32, (8, broad), 0)
        rates_out[...] = jnp.where(at == 0, object_rate, probe_rate)
        change_own[...] = change[...]
    else:
        both = jnp.concatenate([object_rate, object_rate], axis=1)
        new_map[...] = object_map[...] + both * wide[...]
        for pair in range(pairs):
            some = slice(2 * pair, 2 * pair + 2)
            for part in range(2):
                first = 4 * pair + 2 * part
                new_probes[part, some] = probes[part, some] + probe_rate * got[first : first + 2]
    copies.finish()


def settle(last, places, weights, object_map, probes, turns, spread):
    _, rows, _, lanes = object_map.shape
    modes, length = (probes.shape[1], probes.shape[-1])
    slots = places.shape[0]
    planes = 2 * modes
    high, broad = (rows // 3, lanes // 2)
    f32 = jnp.float32
    grid = (2, 2, 4)
    step = jax.ShapeDtypeStruct((planes + 2,) + grid + (8, length), f32)
    if last:
        out_shape = (
            step,
            jax.ShapeDtypeStruct((2, high, 8, broad), f32),
            jax.ShapeDtypeStruct((8, broad), f32),
        )
    else:
        out_shape = (
            jax.ShapeDtypeStruct(object_map.shape, f32),
            jax.ShapeDtypeStruct((2, modes) + grid + (8, length), f32),
            step,
        )
    return pl.pallas_call(
        functools.partial(settle_kernel, last),
        out_shape=out_shape,
        in_specs=[scalars, scalars] + [memory] * 8,
        out_specs=(memory,) * 3,
        scratch_shapes=[
            pltpu.VMEM((planes + 1,) + grid + (8, length), f32),
            pltpu.VMEM((slots, 2, length, length), f32),
            pltpu.VMEM((2, 2, 4 * high + 1, 8, length), f32),
            pltpu.VMEM((3, rows, 8, lanes), f32),
            pltpu.VMEM((6, 3, high // 2, 8, broad), f32),
            pltpu.VMEM((2, 3, high, 8, broad), f32),
            pltpu.VMEM((6, 3, high // 2, 8, broad), f32),
            pltpu.VMEM((planes + 1, 2, 4, 8, length), f32),
            pltpu.VMEM((planes + 1, 2, 4, 8, length), f32),
            pltpu.VMEM((planes + 1, 4, 8, length), f32),
            pltpu.VMEM((planes + 1, 4, 8, length), f32),
            pltpu.VMEM((3, planes + 1, 8, length), f32),
            pltpu.VMEM((2, high, 8, broad), f32),
        ]
        + halo_scratch(high, broad)
        + [
            pltpu.VMEM((2, rows, 8, lanes), f32),
            pltpu.VMEM((2, rows, 8, lanes), f32),
            pltpu.VMEM((8, broad), f32),
            pltpu.VMEM((15, 8, broad), f32),
            pltpu.SemaphoreType.DMA((32,)),
            pltpu.SemaphoreType.DMA((32,)),
        ],
        compiler_params=pltpu.CompilerParams(
            collective_id=2 if last else 1,
            has_side_effects=True,
            vmem_limit_bytes=28 * 1024 * 1024,
        ),
        name="finish" if last else "settle",
    )(
        places,
        weights,
        object_map,
        probes.reshape((2, modes) + grid + (8, length)),
        turns,
        *spread,
    )


def apply_kernel(object_map, change, probes, step, rates, object_at, probes_at, tile, fresh, done):
    modes = probes.shape[1]
    high, broad = (change.shape[1], change.shape[3])
    object_rate = jnp.broadcast_to(rates[0:1], (8, broad))
    probe_rate = jnp.broadcast_to(rates[1:2], (8, broad))
    copies = []
    for part in range(2):
        for first in range(0, modes, 4):
            some = slice(first, first + 4)
            base = 2 * (first + part)
            stepped = jnp.concatenate(
                [step[base : base + 2], step[base + 4 : base + 6]], axis=0
            )
            moved = probes[part, some] + probe_rate * stepped
            fresh[part, some] = moved.reshape((4,) + fresh.shape[2:])
            block = (part, pl.ds(first, 4))
            copies.append(
                pltpu.make_async_copy(fresh.at[block], probes_at.at[block], done.at[len(copies)])
            )
            copies[-1].start()
    moved = object_map[:, high : 2 * high, :, :broad] + object_rate * change[...]
    tile[...] = moved.reshape(tile.shape)
    copies.append(pltpu.make_async_copy(tile, object_at, done.at[len(copies)]))
    copies[-1].start()
    for copy in copies:
        copy.wait()


def apply(object_map, change, probes, step, rates):
    _, high, _, broad = change.shape
    modes, length = (probes.shape[1], probes.shape[-1])
    shapes = ((2, 8 * high, broad), (2, modes, length, length))
    blocks = (2, modes, length // 8, 8, length)
    return pl.pallas_call(
        apply_kernel,
        out_shape=tuple(jax.ShapeDtypeStruct(shape, jnp.float32) for shape in shapes),
        in_specs=[memory] * 5,
        out_specs=(outside,) * 2,
        scratch_shapes=[pltpu.VMEM(shape, jnp.float32) for shape in shapes]
        + [pltpu.SemaphoreType.DMA((modes // 2 + 1,))],
        compiler_params=pltpu.CompilerParams(vmem_limit_bytes=8 * 1024 * 1024),
        name="apply",
    )(
        object_map,
        change,
        probes.reshape(blocks),
        step.reshape((2 * modes + 2,) + blocks[2:]),
        rates,
    )


def direct(object_field, probe_modes, positions, counts, intensity):
    two, modes, length, _ = probe_modes.shape
    margin = length // 2
    _, height, breadth = object_field.shape
    anchor = jnp.stack(
        [lax.axis_index("tx") * height - margin, lax.axis_index("ty") * breadth - margin]
    )
    starts = positions - anchor[None, :]
    lanes = 2 * breadth
    places = window_places(starts, height + 2 * margin, lanes, length, margin)
    weights = (jnp.arange(positions.shape[0], dtype=jnp.int32) < counts[0]).astype(jnp.float32)
    object_map, probes, turns, measured = widen_tiles(
        object_field,
        probe_modes,
        jnp.asarray(split_tables(length)),
        intensity,
    )
    for repeat in range(ITERS):
        spread = outward(object_map, probes, places, counts, measured, turns)
        last = repeat + 1 == ITERS
        settled = settle(last, places, weights, object_map, probes, turns, spread)
        if not last:
            object_map, probes, _ = settled
            probes = probes.reshape(probe_modes.shape)
    step, change, rates = settled
    return apply(object_map, change, probes, step, rates)


def shards(object_field, probe_modes, positions, counts, intensity):
    _, height, breadth = object_field.shape
    length = probe_modes.shape[-1]
    grid = (lax.axis_size("tx"), lax.axis_size("ty"))
    arguments = (object_field, probe_modes, positions, counts, intensity)
    if grid == (4, 4) and length == 128 and (2 * height, breadth) == (length, length):
        return direct(*arguments)
    return general(*arguments)


def solution(mesh):
    return jax.shard_map(
        shards,
        mesh=mesh,
        in_specs=(
            P("groups", "tx", "ty"),
            P("groups", None, None, None),
            P(("groups", "tx", "ty"), None),
            P(("groups", "tx", "ty")),
            P(("groups", "tx", "ty"), None, None),
        ),
        out_specs=(P("groups", "tx", "ty"), P("groups", None, None, None)),
        check_vma=False,
    )
```

```python
import functools

import jax
import jax.numpy as jnp
import ml_dtypes
import numpy as np
from jax import lax
from jax.experimental import pallas as pl
from jax.experimental.pallas import tpu as pltpu
from jax.sharding import PartitionSpec as P

ITERS = 2
memory = pl.BlockSpec(memory_space=pltpu.VMEM)
scalars = pl.BlockSpec(memory_space=pltpu.SMEM)


def with_halo(value, sides, width):
    for axis, dim in sides:
        size, length = (lax.axis_size(axis), value.shape[dim])
        up = [(i, (i + 1) % size) for i in range(size - 1)]
        down = [(j, i) for i, j in up]
        last = lax.slice_in_dim(value, length - width, length, axis=dim)
        first = lax.slice_in_dim(value, 0, width, axis=dim)
        before = lax.ppermute(last, axis, up)
        after = lax.ppermute(first, axis, down)
        value = jnp.concatenate([before, value, after], axis=dim)
    return value


def from_behind(block, axis, distance):
    devices = range(lax.axis_size(axis))
    route = [(i - distance, i) for i in devices if i - distance in devices]
    return lax.ppermute(block, axis, route)


def split_tables(length):
    indices = np.arange(length)
    angles = (indices[:, None] * indices[None, :] % length) * (2.0 * np.pi / length)
    cos_table = np.cos(angles) / np.sqrt(length)
    sin_table = np.sin(angles) / np.sqrt(length)
    forward = np.block([[cos_table, -sin_table], [sin_table, cos_table]])
    inverse = np.block([[cos_table, sin_table], [-sin_table, cos_table]])

    def stacked(table):
        coarse = table.astype(np.float32).astype(ml_dtypes.bfloat16)
        fine = (table - coarse.astype(np.float64)).astype(ml_dtypes.bfloat16)
        return np.concatenate([coarse, coarse, fine], axis=0)

    return np.stack([stacked(forward), stacked(inverse)])


def halves(value, axis):
    coarse = value.astype(jnp.bfloat16)
    fine = (value - coarse.astype(jnp.float32)).astype(jnp.bfloat16)
    return jnp.concatenate([coarse, fine, coarse], axis=axis)


def along_lanes(value, table):
    return jnp.dot(halves(value, 1), table, preferred_element_type=jnp.float32)


def along_rows(value, table):
    dims = (((0,), (0,)), ((), ()))
    return lax.dot_general(halves(value, 0), table, dims, preferred_element_type=jnp.float32)


def regroup(value, length):
    top, bottom = (value[:length], value[length:])
    return jnp.concatenate(
        [
            jnp.concatenate([top[:, :length], bottom[:, :length]], axis=1),
            jnp.concatenate([top[:, length:], bottom[:, length:]], axis=1),
        ],
        axis=0,
    )


def cut_window(places, slot, maps, plane, length):
    tall = length // 8
    tile, back, shift, upward = (places[slot, n] for n in range(4))
    sublane = lax.broadcasted_iota(jnp.int32, (tall, 8, length), 1)
    part = maps[plane, pl.ds(tile, tall + 1)]
    part = pltpu.roll(part, back, 2)[:, :, :length]
    part = pltpu.roll(part, upward, 1)
    return jnp.where(sublane + shift < 8, part[:tall], part[1:])


def lower(part, shift):
    tall, _, length = part.shape
    sublane = lax.broadcasted_iota(jnp.int32, (tall + 1, 8, length), 1)
    blank = jnp.zeros((1, 8, length), jnp.float32)
    part = pltpu.roll(part, lax.rem(shift, 8), 1)
    return jnp.where(
        sublane >= shift,
        jnp.concatenate([part, blank], axis=0),
        jnp.concatenate([blank, part], axis=0),
    )


def broaden(part, onward, breadth):
    margin = jnp.zeros(part.shape[:2] + (breadth - part.shape[2],), jnp.float32)
    return pltpu.roll(jnp.concatenate([part, margin], axis=2), onward, 2)


def add_placed(places, slot, part, totals, plane):
    breadth = totals.shape[-1]
    tile, back, shift = (places[slot, n] for n in range(3))
    onward = lax.rem(breadth - back, breadth)
    wide = broaden(lower(part, shift), onward, breadth)
    totals[plane, pl.ds(tile, wide.shape[0])] += wide


def lighting_of(probes):
    length = probes.shape[-1]
    lighting = jnp.zeros((length, length), jnp.float32)
    for mode in range(probes.shape[1]):
        lighting += probes[0, mode] * probes[0, mode] + probes[1, mode] * probes[1, mode]
    return lighting


def forward_slots(places, live, object_map, probes, intensity, turns, window, far, power):
    modes, length = (probes.shape[1], probes.shape[-1])
    slots = intensity.shape[0]
    coverage = jnp.zeros((length, length), jnp.float32)
    for slot in range(slots):
        for plane in range(2):
            part = cut_window(places, slot, object_map, plane, length)
            window[slot, plane] = part.reshape(length, length)
        lit = window[slot, 0] * window[slot, 0] + window[slot, 1] * window[slot, 1]
        coverage += jnp.where(slot < live, lit, 0.0)
    for pair in range(modes // 2):
        for slot in range(slots):
            waves = []
            for mode in (2 * pair, 2 * pair + 1):
                probe_r, probe_i = (probes[0, mode], probes[1, mode])
                obj_r, obj_i = (window[slot, 0], window[slot, 1])
                wave_r = probe_r * obj_r - probe_i * obj_i
                wave_i = probe_r * obj_i + probe_i * obj_r
                waves.append(jnp.concatenate([wave_r, wave_i], axis=1))
            half = regroup(along_lanes(jnp.concatenate(waves, axis=0), turns[0]), length)
            spread = along_rows(half, turns[0])
            far[slot, pair] = spread
            square = spread * spread
            square = square[:, :length] + square[:, length:]
            square = square[:length] + square[length:]
            if pair == 0:
                power[slot] = square
            else:
                power[slot] += square
    for slot in range(slots):
        ratio = jnp.sqrt(intensity[slot].T / jnp.maximum(power[slot], 1.0)) - 1.0
        power[slot] = jnp.where(slot < live, ratio, 0.0)
    return coverage


def backward_slot(slot, pair, probes_of, turns, window, far, power, terms):
    length = power.shape[-1]
    factor = power[slot]
    factor = jnp.concatenate([factor, factor], axis=1)
    factor = jnp.concatenate([factor, factor], axis=0)
    half = regroup(along_lanes(far[slot, pair] * factor, turns[1]), length)
    change = along_rows(half, turns[1])
    obj_r, obj_i = (window[slot, 0], window[slot, 1])
    terms_r = jnp.zeros((length, length), jnp.float32)
    terms_i = jnp.zeros((length, length), jnp.float32)
    moved_r, moved_i = ([], [])
    for which in range(2):
        rows = slice(which * length, (which + 1) * length)
        change_r, change_i = (change[rows, :length], change[rows, length:])
        probe_r, probe_i = probes_of(2 * pair + which)
        terms_r += probe_r * change_r + probe_i * change_i
        terms_i += probe_r * change_i - probe_i * change_r
        moved_r.append(obj_r * change_r + obj_i * change_i)
        moved_i.append(obj_r * change_i - obj_i * change_r)
    if pair == 0:
        terms[slot, 0] = terms_r
        terms[slot, 1] = terms_i
    else:
        terms[slot, 0] += terms_r
        terms[slot, 1] += terms_i
    return moved_r, moved_i


def slots_kernel(
    places, counts, object_map, probes, intensity, turns, totals, sums, window, far, power, terms
):
    modes, length = (probes.shape[1], probes.shape[-1])
    tall = length // 8
    live = counts[0]
    totals[...] = jnp.zeros_like(totals)
    terms[0, 2] = lighting_of(probes)
    sums[2 * modes] = forward_slots(
        places, live, object_map, probes, intensity, turns, window, far, power
    )
    for pair in range(modes // 2):
        for slot in range(intensity.shape[0]):
            moved_r, moved_i = backward_slot(
                slot, pair, lambda k: (probes[0, k], probes[1, k]), turns, window, far, power, terms
            )
            for which in range(2):
                mode = 2 * pair + which
                if slot == 0:
                    sums[mode] = moved_r[which]
                    sums[modes + mode] = moved_i[which]
                else:
                    sums[mode] += moved_r[which]
                    sums[modes + mode] += moved_i[which]

    def place_slot(slot, carry):
        for plane in range(3):
            part = terms[slot, plane] if plane < 2 else terms[0, 2]
            add_placed(places, slot, part.reshape(tall, 8, length), totals, plane)
        return carry

    lax.fori_loop(0, live, place_slot, 0)


def accumulate(object_map, probes, places, counts, intensity, turns):
    _, modes, length, _ = probes.shape
    slots = intensity.shape[0]
    return pl.pallas_call(
        slots_kernel,
        out_shape=(
            jax.ShapeDtypeStruct((3,) + object_map.shape[1:], jnp.float32),
            jax.ShapeDtypeStruct((2 * modes + 1, length, length), jnp.float32),
        ),
        in_specs=[scalars, scalars] + [memory] * 4,
        out_specs=(memory, memory),
        scratch_shapes=[
            pltpu.VMEM((slots, 2, length, length), jnp.float32),
            pltpu.VMEM((slots, modes // 2, 2 * length, 2 * length), jnp.float32),
            pltpu.VMEM((slots, length, length), jnp.float32),
            pltpu.VMEM((slots, 3, length, length), jnp.float32),
        ],
        compiler_params=pltpu.CompilerParams(vmem_limit_bytes=36 * 1024 * 1024),
        name="slots",
    )(places, counts, object_map, probes, intensity, turns)


def outward_kernel(
    places, counts, object_map, probes, intensity, turns, window, far, power, coverage, lit, light
):
    length = probes.shape[-1]
    live = counts[0]
    lit[...] = jnp.zeros_like(lit)
    light[...] = lighting_of(probes).reshape(light.shape)
    coverage[...] = forward_slots(
        places, live, object_map, probes, intensity, turns, window, far, power
    )

    def place_slot(slot, carry):
        add_placed(places, slot, light[...], lit, 0)
        return carry

    lax.fori_loop(0, live, place_slot, 0)


def outward(object_map, probes, places, counts, intensity, turns):
    _, modes, length, _ = probes.shape
    slots = intensity.shape[0]
    shapes = (
        (slots, 2, length, length),
        (slots, modes // 2, 2 * length, 2 * length),
        (slots, length, length),
        (length, length),
        (1,) + object_map.shape[1:],
    )
    return pl.pallas_call(
        outward_kernel,
        out_shape=tuple(jax.ShapeDtypeStruct(shape, jnp.float32) for shape in shapes),
        in_specs=[scalars, scalars] + [memory] * 4,
        out_specs=(memory,) * 5,
        scratch_shapes=[pltpu.VMEM((length // 8, 8, length), jnp.float32)],
        compiler_params=pltpu.CompilerParams(vmem_limit_bytes=20 * 1024 * 1024),
        name="outward",
    )(places, counts, object_map, probes, intensity, turns)


def window_places(starts, rows, lanes, length, lead):
    rows_at = jnp.clip(starts[:, 0], 0, rows - length)
    cols_at = jnp.clip(starts[:, 1], 0, lanes - length)
    tile = jnp.minimum(rows_at // 8, (rows - length) // 8 - 1)
    shift = rows_at - 8 * tile
    back = (lanes + lead - cols_at) % lanes
    return jnp.stack([tile, back, shift, (8 - shift) % 8], axis=1)


def mixing(probes, probe_step):
    mix_r = jnp.sum(probes[0] * probe_step[0] + probes[1] * probe_step[1], axis=0)
    mix_i = jnp.sum(probes[0] * probe_step[1] - probes[1] * probe_step[0], axis=0)
    return (mix_r, mix_i)


def cross_term(object_map, change, starts, active, mix_r, mix_i):
    length = mix_r.shape[-1]
    anchor_index = jnp.int32(0)

    def cross_visit_slot(running, element):
        corner_at, weight = element
        corner = (anchor_index, corner_at[0], corner_at[1])
        object_win = lax.dynamic_slice(object_map, corner, (2, length, length))
        change_win = lax.dynamic_slice(change, corner, (2, length, length))
        aligned = change_win[0] * object_win[0] + change_win[1] * object_win[1]
        rotated = change_win[0] * object_win[1] - change_win[1] * object_win[0]
        return (running + weight * jnp.sum(aligned * mix_r - rotated * mix_i), None)

    running, _ = lax.scan(cross_visit_slot, jnp.zeros((), jnp.float32), (starts, active))
    return running


def solve_steps(object_curve, cross_curve, probe_curve, object_slope, probe_slope):
    object_diag = 1.1 * object_curve + 0.001
    probe_diag = 1.1 * probe_curve + 0.001
    determinant = object_diag * probe_diag - cross_curve * cross_curve
    object_rate = (probe_diag * object_slope - cross_curve * probe_slope) / determinant
    probe_rate = (object_diag * probe_slope - cross_curve * object_slope) / determinant
    return (object_rate, probe_rate)


def widen(planes, margin):
    return with_halo(planes, (("tx", 1), ("ty", 2)), margin)


def fold_rims(totals, margin, height, breadth):
    middle = totals[:, margin : margin + height, :]
    for direction in (1, -1):
        border = totals[:, margin + height :, :] if direction == 1 else totals[:, :margin, :]
        arrived = from_behind(border, "tx", direction)
        if direction == 1:
            middle = jnp.concatenate([middle + arrived, middle[:, margin:, :]], axis=1)
        else:
            middle = jnp.concatenate([middle[:, : height - margin, :], middle + arrived], axis=1)
    interior = middle[:, :, margin : margin + breadth]
    for direction in (1, -1):
        border = middle[:, :, margin + breadth :] if direction == 1 else middle[:, :, :margin]
        arrived = from_behind(border, "ty", direction)
        if direction == 1:
            interior = jnp.concatenate(
                [interior[:, :, :margin] + arrived, interior[:, :, margin:]], axis=2
            )
        else:
            interior = jnp.concatenate(
                [interior[:, :, : breadth - margin], interior[:, :, breadth - margin :] + arrived],
                axis=2,
            )
    return interior


def general(object_field, probe_modes, positions, counts, intensity):
    length = probe_modes.shape[-1]
    margin = length // 2
    height = object_field.shape[1]
    breadth = object_field.shape[2]
    turns = split_tables(length)
    modes = probe_modes.shape[1]
    anchor = jnp.stack(
        [lax.axis_index("tx") * height - margin, lax.axis_index("ty") * breadth - margin]
    )
    starts = positions - anchor[None, :]
    active = (jnp.arange(positions.shape[0], dtype=jnp.int32) < counts[0]).astype(jnp.float32)
    places = window_places(starts, height + 2 * margin, breadth + 2 * margin, length, 0)
    object_map = object_field
    probes = probe_modes
    extended = widen(object_map, margin)
    for repeat in range(ITERS):
        tiled = extended.reshape(2, -1, 8, extended.shape[-1])
        totals, sums = accumulate(tiled, probes, places, counts, intensity, turns)
        totals = totals.reshape((3,) + extended.shape[1:])
        interior = fold_rims(totals, margin, height, breadth)
        change = interior[:2] / jnp.maximum(interior[2], 1.0)
        object_part = jnp.sum((change[0] * change[0] + change[1] * change[1]) * interior[2])
        slope_part = jnp.sum(interior[:2] * change)
        wide_change = widen(change, margin)
        sums = lax.psum(sums, ("tx", "ty"))
        probe_total = sums[: 2 * modes].reshape(probes.shape)
        weight_total = sums[2 * modes]
        probe_step = probe_total / (weight_total + 1e-05)
        mix_r, mix_i = mixing(probes, probe_step)
        cross_part = cross_term(extended, wide_change, starts, active, mix_r, mix_i)
        object_curve, cross_curve, object_slope = lax.psum(
            (object_part, cross_part, slope_part), ("tx", "ty")
        )
        probe_curve = jnp.sum(
            (probe_step[0] * probe_step[0] + probe_step[1] * probe_step[1]) * weight_total
        )
        probe_slope = jnp.sum(probe_total * probe_step)
        object_rate, probe_rate = solve_steps(
            object_curve, cross_curve, probe_curve, object_slope, probe_slope
        )
        object_map = object_map + object_rate * change
        probes = probes + probe_rate * probe_step
        if repeat + 1 < ITERS:
            extended = extended + object_rate * wide_change
    return (object_map, probes)

outside = pl.BlockSpec(memory_space=pltpu.HBM)
OTHERS = [(i, j) for i in range(4) for j in range(4) if i or j]
AROUND = [(i, j) for i in (-1, 0, 1) for j in (-1, 0, 1) if i or j]
SIDES = [(i, j) for i in (-1, 0, 1) for j in (-1, 1)]


def everyone(row, col):
    return [{"tx": (row + i) % 4, "ty": (col + j) % 4} for i, j in OTHERS]


def greet(peers):
    barrier = pltpu.get_barrier_semaphore()
    for peer in peers:
        pl.semaphore_signal(barrier, 1, device_id=peer, device_id_type=pl.DeviceIdType.MESH)
    pl.semaphore_wait(barrier, len(peers))


class Copies:
    def __init__(self, send, arrive):
        self.send, self.arrive, self.count = (send, arrive, 0)
        self.unsent = []

    def slots(self, number):
        self.count += number
        return self.count - number

    def make(self, source, target, index, landing, peer):
        return pltpu.make_async_remote_copy(
            src_ref=source,
            dst_ref=target,
            send_sem=self.send.at[index],
            recv_sem=self.arrive.at[landing],
            device_id=peer,
            device_id_type=pl.DeviceIdType.MESH,
        )

    def start(self, source, target, peer):
        index = self.slots(1)
        copy = self.make(source, target, index, index, peer)
        copy.start()
        self.unsent.append(copy)
        return copy

    def group(self, items, view):
        index = self.slots(1)
        for source, target, peer in items:
            self.make(source, target, index, index, peer).start()
        whole = self.make(view, view, index, index, items[0][2])
        self.unsent.append(whole)
        return whole

    def finish(self):
        for copy in self.unsent:
            copy.wait_send()
        self.unsent = []


class Ring:
    def __init__(self, copies, row, col, source, target):
        self.copies, self.row, self.col = (copies, row, col)
        self.source, self.target = (source, target)
        self.base = copies.slots(len(AROUND))

    def each(self, what):
        for k, (i, j) in enumerate(AROUND):
            row, col = (self.row + i, self.col + j)
            inside = (row >= 0) & (row < 4) & (col >= 0) & (col < 4)
            pl.when(inside)(functools.partial(what, k, i, j, {"tx": row, "ty": col}))

    def outgoing(self, k, i, j, peer):
        landing = AROUND.index((-i, -j))
        return self.copies.make(
            self.source(i, j), self.target(-i, -j), self.base + k, self.base + landing, peer
        )

    def blank(self):
        for i, j in AROUND:
            row, col = (self.row + i, self.col + j)
            inside = (row >= 0) & (row < 4) & (col >= 0) & (col < 4)
            target = self.target(i, j)

            @pl.when(jnp.logical_not(inside))
            def _():
                target[...] = jnp.zeros(target.shape, jnp.float32)

    def start(self):
        self.each(lambda k, i, j, peer: self.outgoing(k, i, j, peer).start())

    def receive(self):
        def arrived(k, i, j, peer):
            index = self.base + k
            self.copies.make(self.source(i, j), self.target(i, j), index, index, peer).wait_recv()

        self.each(arrived)

    def finish(self):
        self.each(lambda k, i, j, peer: self.outgoing(k, i, j, peer).wait_send())


class Edges:
    def __init__(self, copies, row, col, axis, source, target):
        self.copies, self.axis = (copies, axis)
        self.source, self.target = (source, target)
        self.place = {"tx": row, "ty": col}
        self.base = copies.slots(2)

    def each(self, what, missing=False):
        for k, ahead in ((0, -1), (1, 1)):
            there = self.place[self.axis] + ahead
            inside = (there >= 0) & (there < 4)
            inside = jnp.logical_not(inside) if missing else inside
            peer = {**self.place, self.axis: there}
            pl.when(inside)(functools.partial(what, k, peer))

    def blank(self):
        def clear(k, peer):
            target = self.target(k)
            target[...] = jnp.zeros(target.shape, jnp.float32)

        self.each(clear, missing=True)

    def outgoing(self, k, peer):
        landing = 1 - k
        return self.copies.make(
            self.source(k), self.target(landing), self.base + k, self.base + landing, peer
        )

    def start(self):
        self.each(lambda k, peer: self.outgoing(k, peer).start())

    def receive(self):
        def arrived(k, peer):
            index = self.base + k
            self.copies.make(self.source(k), self.target(k), index, index, peer).wait_recv()

        self.each(arrived)

    def finish(self):
        self.each(lambda k, peer: self.outgoing(k, peer).wait_send())


def early_lanes(value):
    return lax.broadcasted_iota(jnp.int32, value.shape, value.ndim - 1) < value.shape[-1] // 2


def turned(value):
    return pltpu.roll(value, value.shape[-1] // 2, value.ndim - 1)


def pack_first(block):
    half = block.shape[1] // 2
    top, bottom = (block[:, :half], block[:, half:])
    return jnp.where(early_lanes(top), top, turned(bottom))


def pack_last(block):
    half = block.shape[1] // 2
    top, bottom = (block[:, :half], block[:, half:])
    return jnp.where(early_lanes(top), turned(top), bottom)


def unpack(first, last):
    early = early_lanes(first)
    top = jnp.where(early, first, turned(last))
    bottom = jnp.where(early, turned(first), last)
    return jnp.concatenate([top, bottom], axis=1)


def row_range(i, high):
    return slice((i + 1) * high, (i + 2) * high)


def halo_ring(copies, row, col, own, packed, above, beside):
    def source(i, j):
        return own if j == 0 else packed.at[(j + 1) // 2]

    def target(i, j):
        return above.at[(i + 1) // 2] if j == 0 else beside.at[SIDES.index((i, j))]

    return Ring(copies, row, col, source, target)


def spread_halo(own, above, beside, wide):
    high, broad = (own.shape[1], own.shape[-1])
    for i in (-1, 0, 1):
        rows = row_range(i, high)
        wide[:, rows, :, :broad] = own if i == 0 else above[(i + 1) // 2]
        wide[:, rows, :, broad:] = unpack(
            beside[SIDES.index((i, 1))], beside[SIDES.index((i, -1))]
        )


def widen_kernel(
    own_at, probes_at, turns_at, intensity_at, wide, probes, turns, intensity, own, whole, packed, above,
    beside, local, send, arrive,
):
    row, col = (lax.axis_index("tx"), lax.axis_index("ty"))
    fetches = [
        pltpu.make_async_copy(source, target, local.at[k])
        for k, (source, target) in enumerate(
            ((own_at, own), (probes_at, probes), (turns_at, turns), (intensity_at, intensity))
        )
    ]
    for fetch in fetches:
        fetch.start()
    copies = Copies(send, arrive)
    ring = halo_ring(copies, row, col, whole, packed, above, beside)
    ring.blank()
    fetches[0].wait()
    block = own[...].reshape(2, own.shape[1] // 8, 8, own.shape[2])
    whole[...] = block
    packed[0] = pack_first(block)
    packed[1] = pack_last(block)
    greet(everyone(row, col))
    ring.start()
    for fetch in fetches[1:]:
        fetch.wait()
    ring.receive()
    spread_halo(block, above, beside, wide)
    ring.finish()


def halo_scratch(high, broad):
    return [
        pltpu.VMEM((2, 2, high // 2, 8, broad), jnp.float32),
        pltpu.VMEM((2, 2, high, 8, broad), jnp.float32),
        pltpu.VMEM((6, 2, high // 2, 8, broad), jnp.float32),
    ]


def widen_tiles(own, probes, turns, intensity):
    two, height, broad = own.shape
    high = height // 8

    def like(value):
        return jax.ShapeDtypeStruct(value.shape, value.dtype)

    return pl.pallas_call(
        widen_kernel,
        out_shape=(
            jax.ShapeDtypeStruct((two, 3 * high, 8, 2 * broad), jnp.float32),
            like(probes),
            like(turns),
            like(intensity),
        ),
        in_specs=[outside] * 4,
        out_specs=(memory,) * 4,
        scratch_shapes=[
            pltpu.VMEM(own.shape, jnp.float32),
            pltpu.VMEM((two, high, 8, broad), jnp.float32),
        ]
        + halo_scratch(high, broad)
        + [
            pltpu.SemaphoreType.DMA((4,)),
            pltpu.SemaphoreType.DMA((8,)),
            pltpu.SemaphoreType.DMA((8,)),
        ],
        compiler_params=pltpu.CompilerParams(
            collective_id=0, has_side_effects=True, vmem_limit_bytes=12 * 1024 * 1024
        ),
        name="widen",
    )(own, probes, turns, intensity)


def in_rows(values, lanes):
    at = lax.broadcasted_iota(jnp.int32, (8, lanes), 0)
    result = jnp.zeros((8, lanes), jnp.float32)
    for place, value in enumerate(values):
        result = jnp.where(at == place, value, result)
    return result


def settle_kernel(
    last, places, weights, object_map, probes, turns, window, far, power, coverage, lit, *rest
):
    if last:
        got, change_own, rates_out = rest[:3]
    else:
        new_map, new_probes, got = rest[:3]
    (
        sums, terms, padded, totals, fold_out, fold_in, upright, over, column, near_out, near, r1,
        acc, r2, acca, r3, accb, r4, wide, held, mix, mine, pair_in, ours, inbox, send, arrive,
    ) = rest[3:]
    row, col = (lax.axis_index("tx"), lax.axis_index("ty"))
    core, side, upper, lower_bit = (col % 2, col // 2, row // 2, row % 2)
    rows, broad = (column.shape[1], column.shape[-1])
    high = rows // 3
    tall, length = (2 * high, power.shape[-1])
    slots = places.shape[0]
    modes = probes.shape[1]
    pairs = modes // 2
    blocks = got.shape[1:]
    middle = slice(high, 2 * high)
    ends = (slice(0, high), slice(2 * high, 3 * high))
    peers = everyone(row, col)
    partner = {"tx": row, "ty": side * 2 + (1 - core)}
    across = {"tx": row, "ty": (1 - side) * 2 + core}
    beside = {"tx": row + 1 - 2 * lower_bit, "ty": col}
    beyond = {"tx": (row + 2) % 4, "ty": col}
    chips = [
        {"tx": (row + i) % 4, "ty": ((side + j) % 2) * 2 + core}
        for i in range(4)
        for j in range(2)
        if i or j
    ]
    copies = Copies(send, arrive)
    spot = (core, side, upper, lower_bit)

    barrier = pltpu.get_barrier_semaphore()
    for peer in peers:
        pl.semaphore_signal(barrier, 1, device_id=peer, device_id_type=pl.DeviceIdType.MESH)

    def edges(axis, source, target):
        made = Edges(copies, row, col, axis, source, target)
        made.blank()
        return made

    fold_side = edges("ty", lambda k: fold_out.at[k], lambda k: fold_in.at[k])
    fold_over = edges("tx", lambda k: upright.at[:, ends[k]], lambda k: over.at[k])
    halo_over = edges("tx", lambda k: column.at[:, middle], lambda k: column.at[:, ends[k]])
    halo_side = edges("ty", lambda k: near_out.at[k], lambda k: near.at[k])
    padded[...] = jnp.zeros_like(padded)
    totals[:2] = jnp.zeros((2,) + totals.shape[1:], jnp.float32)
    totals[2] = lit[0]

    def probes_of(mode):
        return tuple(probes[part, mode].reshape(length, length) for part in range(2))

    def compute(pair):
        base = 1 + 4 * pair
        for slot in range(slots):
            moved_r, moved_i = backward_slot(
                slot, pair, probes_of, turns, window, far, power, terms
            )
            for n, value in enumerate(moved_r + moved_i):
                value = value.reshape(blocks)
                if slot == 0:
                    sums[base + n] = value
                else:
                    sums[base + n] += value

    def chunk(n):
        return slice(1 + 4 * n if n else 0, 5 + 4 * n)

    def planes(n):
        return slice(4 * n, 4 * n + 4)

    shared = {}
    moving = {}

    def core_sum(n):
        part = chunk(n)
        moving[n] = copies.start(sums.at[part, 1 - core], r1.at[part], partner)

    def across_sum(n):
        part = chunk(n)
        moving[n].wait_recv()
        acc[part] = sums[part, core] + r1[part]
        moving[n] = copies.start(acc.at[part, 1 - side], r2.at[part], across)

    def beside_sum(n):
        part = chunk(n)
        moving[n].wait_recv()
        acca[part] = acc[part, side] + r2[part]
        moving[n] = copies.start(acca.at[part, :, 1 - lower_bit], r3.at[part], beside)

    def beyond_sum(n):
        part = chunk(n)
        moving[n].wait_recv()
        accb[part] = acca[part, :, lower_bit] + r3[part]
        moving[n] = copies.start(accb.at[part, 1 - upper], r4.at[part], beyond)

    def give(n, block, peer):
        moving[n] = copies.start(block, block, peer)

    def slab(n):
        part = chunk(n)
        moving[n].wait_recv()
        total = accb[part, upper] + r4[part]
        if n == 0:
            shared["weight"] = total[0]
            total = total[1:]
        weight = shared["weight"]
        found = total / (weight + 1e-05)
        got[(planes(n),) + spot] = found
        give(n, got.at[(planes(n),) + spot], beyond)
        some = slice(2 * n, 2 * n + 2)
        probe_r, probe_i = (probes[(0, some) + spot], probes[(1, some) + spot])
        for name, value in (
            ("mix_r", probe_r * found[:2] + probe_i * found[2:]),
            ("mix_i", probe_r * found[2:] - probe_i * found[:2]),
            ("curve", found * found * weight),
            ("slope", total * found),
        ):
            value = jnp.sum(value, axis=0)
            shared[name] = value if n == 0 else shared[name] + value

    def beside_give(n):
        moving[n].wait_recv()
        give(n, got.at[planes(n), core, side, :, lower_bit], beside)

    def across_give(n):
        moving[n].wait_recv()
        give(n, got.at[planes(n), core, side], across)

    def core_give(n):
        moving[n].wait_recv()
        give(n, got.at[planes(n), core], partner)

    sums[0] = coverage[...].reshape(blocks)
    compute(0)
    pl.semaphore_wait(barrier, len(peers))
    core_sum(0)
    compute(1)
    core_sum(1)
    across_sum(0)
    compute(2)
    core_sum(2)
    across_sum(1)
    compute(3)
    core_sum(3)
    across_sum(2)
    beside_sum(0)

    for slot in range(slots):
        tile, back, shift = (places[slot, n] for n in range(3))
        onward = lax.rem(2 * broad - back, 2 * broad)
        for plane in range(2):
            keep = padded.at[slot % 2, plane]
            keep[high : high + tall + 1] = lower(terms[slot, plane].reshape(tall, 8, length), shift)
            part = padded[slot % 2, plane, pl.ds(high - tile, 3 * high)]
            totals[plane] += broaden(part, onward, 2 * broad)
    rim = totals[:, :, :, broad:]
    fold_out[0] = pack_last(rim)
    fold_out[1] = pack_first(rim)
    fold_side.start()
    across_sum(3)
    beside_sum(1)
    beyond_sum(0)
    beside_sum(2)

    fold_side.receive()
    upright[...] = totals[:, :, :, :broad] + unpack(fold_in[0], fold_in[1])
    fold_over.start()
    beyond_sum(1)
    beside_sum(3)
    slab(0)
    beyond_sum(2)
    slab(1)
    beyond_sum(3)

    fold_over.receive()
    interior = upright[:, middle] + over[0] + over[1]
    moved = interior[:2] / jnp.maximum(interior[2], 1.0)
    column[:, middle] = moved
    halo_over.start()
    beside_give(0)
    slab(2)
    slab(3)
    mix[(0,) + spot] = shared["mix_r"]
    mix[(1,) + spot] = shared["mix_i"]
    block = mix.at[(slice(None),) + spot]
    mixes = [copies.start(block, block, peer) for peer in chips]
    beside_give(1)
    curve = jnp.sum((moved[0] * moved[0] + moved[1] * moved[1]) * interior[2])
    slope = jnp.sum(interior[:2] * moved)
    probe_curve = jnp.sum(shared["curve"])
    probe_slope = jnp.sum(shared["slope"])

    halo_over.receive()
    near_out[0] = pack_first(column[...])
    near_out[1] = pack_last(column[...])
    halo_side.start()
    across_give(0)
    beside_give(2)
    across_give(1)
    beside_give(3)
    wide[:, :, :, :broad] = column[...]

    halo_side.receive()
    wide[:, :, :, broad:] = unpack(near[1], near[0])
    held[0] = wide[0] * object_map[0] + wide[1] * object_map[1]
    held[1] = wide[0] * object_map[1] - wide[1] * object_map[0]
    gathered = []
    for plane in range(2):
        running = jnp.zeros((tall, 8, broad), jnp.float32)
        for slot in range(slots):
            running += weights[slot] * cut_window(places, slot, held, plane, length)
        gathered.append(running)
    for copy in mixes:
        copy.wait_recv()
    block = mix.at[:, core]
    mix_pass = copies.start(block, block, partner)
    core_give(0)
    across_give(2)
    across_give(3)
    mix_pass.wait_recv()
    mix_all = mix[...].reshape(2, tall, 8, broad)
    cross = jnp.sum(gathered[0] * mix_all[0] - gathered[1] * mix_all[1])
    mine[...] = in_rows((curve, slope, probe_curve, probe_slope, cross), broad)
    pair_sent = copies.start(mine, pair_in, partner)
    core_give(1)
    pair_sent.wait_recv()
    ours[...] = mine[...] + pair_in[...]
    scalars_sent = copies.group([(ours, inbox.at[k], peer) for k, peer in enumerate(chips)], inbox)
    core_give(2)
    core_give(3)
    copies.finish()
    for made in (fold_side, fold_over, halo_over, halo_side):
        made.finish()
    for n in range(pairs):
        moving[n].wait_recv()
    scalars_sent.wait_recv()
    sent = ours[...] + jnp.sum(inbox[...], axis=0)
    object_rate, probe_rate = solve_steps(
        sent[0:1], sent[4:5], sent[2:3], sent[1:2], sent[3:4]
    )
    object_rate = jnp.broadcast_to(object_rate, (8, broad))
    probe_rate = jnp.broadcast_to(probe_rate, (8, broad))
    if last:
        at = lax.broadcasted_iota(jnp.int32, (8, broad), 0)
        rates_out[...] = jnp.where(at == 0, object_rate, probe_rate)
        change_own[...] = column[:, middle]
    else:
        both = jnp.concatenate([object_rate, object_rate], axis=1)
        new_map[...] = object_map[...] + both * wide[...]
        for n in range(pairs):
            some = slice(2 * n, 2 * n + 2)
            for part in range(2):
                first = 4 * n + 2 * part
                new_probes[part, some] = probes[part, some] + probe_rate * got[first : first + 2]


def settle(last, places, weights, object_map, probes, turns, spread):
    _, rows, _, lanes = object_map.shape
    modes, length = (probes.shape[1], probes.shape[-1])
    slots = places.shape[0]
    planes = 2 * modes
    high, broad = (rows // 3, lanes // 2)
    f32 = jnp.float32
    grid = (2, 2, 2, 2)
    step = jax.ShapeDtypeStruct((planes,) + grid + (8, length), f32)
    if last:
        out_shape = (
            step,
            jax.ShapeDtypeStruct((2, high, 8, broad), f32),
            jax.ShapeDtypeStruct((8, broad), f32),
        )
    else:
        out_shape = (
            jax.ShapeDtypeStruct(object_map.shape, f32),
            jax.ShapeDtypeStruct((2, modes) + grid + (8, length), f32),
            step,
        )
    scratch = [
        (planes + 1,) + grid + (8, length),
        (slots, 2, length, length),
        (2, 2, 4 * high + 1, 8, length),
        (3, rows, 8, lanes),
        (2, 3, rows // 2, 8, broad),
        (2, 3, rows // 2, 8, broad),
        (3, rows, 8, broad),
        (2, 3, high, 8, broad),
        (2, rows, 8, broad),
        (2, 2, rows // 2, 8, broad),
        (2, 2, rows // 2, 8, broad),
        (planes + 1, 2, 2, 2, 8, length),
        (planes + 1, 2, 2, 2, 8, length),
        (planes + 1, 2, 2, 8, length),
        (planes + 1, 2, 2, 8, length),
        (planes + 1, 2, 8, length),
        (planes + 1, 2, 8, length),
        (planes + 1, 8, length),
        (2, rows, 8, lanes),
        (2, rows, 8, lanes),
        (2,) + grid + (8, length),
        (8, broad),
        (8, broad),
        (8, broad),
        (7, 8, broad),
    ]
    return pl.pallas_call(
        functools.partial(settle_kernel, last),
        out_shape=out_shape,
        in_specs=[scalars, scalars] + [memory] * 8,
        out_specs=(memory,) * 3,
        scratch_shapes=[pltpu.VMEM(shape, f32) for shape in scratch]
        + [pltpu.SemaphoreType.DMA((52,)), pltpu.SemaphoreType.DMA((52,))],
        compiler_params=pltpu.CompilerParams(
            collective_id=2 if last else 1,
            has_side_effects=True,
            vmem_limit_bytes=28 * 1024 * 1024,
        ),
        name="finish" if last else "settle",
    )(
        places,
        weights,
        object_map,
        probes.reshape((2, modes) + grid + (8, length)),
        turns,
        *spread,
    )


def apply_kernel(object_map, change, probes, step, rates, object_at, probes_at, tile, fresh, done):
    modes = probes.shape[1]
    high, broad = (change.shape[1], change.shape[3])
    object_rate = jnp.broadcast_to(rates[0:1], (8, broad))
    probe_rate = jnp.broadcast_to(rates[1:2], (8, broad))
    copies = []
    for part in range(2):
        for first in range(0, modes, 4):
            some = slice(first, first + 4)
            base = 2 * (first + part)
            stepped = jnp.concatenate(
                [step[base : base + 2], step[base + 4 : base + 6]], axis=0
            )
            moved = probes[part, some] + probe_rate * stepped
            fresh[part, some] = moved.reshape((4,) + fresh.shape[2:])
            block = (part, pl.ds(first, 4))
            copies.append(
                pltpu.make_async_copy(fresh.at[block], probes_at.at[block], done.at[len(copies)])
            )
            copies[-1].start()
    moved = object_map[:, high : 2 * high, :, :broad] + object_rate * change[...]
    tile[...] = moved.reshape(tile.shape)
    copies.append(pltpu.make_async_copy(tile, object_at, done.at[len(copies)]))
    copies[-1].start()
    for copy in copies:
        copy.wait()


def apply(object_map, change, probes, step, rates):
    _, high, _, broad = change.shape
    modes, length = (probes.shape[1], probes.shape[-1])
    shapes = ((2, 8 * high, broad), (2, modes, length, length))
    blocks = (2, modes, length // 8, 8, length)
    return pl.pallas_call(
        apply_kernel,
        out_shape=tuple(jax.ShapeDtypeStruct(shape, jnp.float32) for shape in shapes),
        in_specs=[memory] * 5,
        out_specs=(outside,) * 2,
        scratch_shapes=[pltpu.VMEM(shape, jnp.float32) for shape in shapes]
        + [pltpu.SemaphoreType.DMA((modes // 2 + 1,))],
        compiler_params=pltpu.CompilerParams(vmem_limit_bytes=8 * 1024 * 1024),
        name="apply",
    )(
        object_map,
        change,
        probes.reshape(blocks),
        step.reshape((2 * modes,) + blocks[2:]),
        rates,
    )


def direct(object_field, probe_modes, positions, counts, intensity):
    two, modes, length, _ = probe_modes.shape
    margin = length // 2
    _, height, breadth = object_field.shape
    anchor = jnp.stack(
        [lax.axis_index("tx") * height - margin, lax.axis_index("ty") * breadth - margin]
    )
    starts = positions - anchor[None, :]
    lanes = 2 * breadth
    places = window_places(starts, height + 2 * margin, lanes, length, margin)
    weights = (jnp.arange(positions.shape[0], dtype=jnp.int32) < counts[0]).astype(jnp.float32)
    object_map, probes, turns, measured = widen_tiles(
        object_field,
        probe_modes,
        jnp.asarray(split_tables(length)),
        intensity,
    )
    for repeat in range(ITERS):
        spread = outward(object_map, probes, places, counts, measured, turns)
        last = repeat + 1 == ITERS
        settled = settle(last, places, weights, object_map, probes, turns, spread)
        if not last:
            object_map, probes, _ = settled
            probes = probes.reshape(probe_modes.shape)
    step, change, rates = settled
    return apply(object_map, change, probes, step, rates)


def shards(object_field, probe_modes, positions, counts, intensity):
    _, height, breadth = object_field.shape
    length = probe_modes.shape[-1]
    grid = (lax.axis_size("tx"), lax.axis_size("ty"))
    arguments = (object_field, probe_modes, positions, counts, intensity)
    if grid == (4, 4) and length == 128 and (2 * height, breadth) == (length, length):
        return direct(*arguments)
    return general(*arguments)


def solution(mesh):
    return jax.shard_map(
        shards,
        mesh=mesh,
        in_specs=(
            P("groups", "tx", "ty"),
            P("groups", None, None, None),
            P(("groups", "tx", "ty"), None),
            P(("groups", "tx", "ty")),
            P(("groups", "tx", "ty"), None, None),
        ),
        out_specs=(P("groups", "tx", "ty"), P("groups", None, None, None)),
        check_vma=False,
    )
```

```python
import functools

import jax
import jax.numpy as jnp
import ml_dtypes
import numpy as np
from jax import lax
from jax.experimental import pallas as pl
from jax.experimental.pallas import tpu as pltpu
from jax.sharding import PartitionSpec as P

ITERS = 2
memory = pl.BlockSpec(memory_space=pltpu.VMEM)
scalars = pl.BlockSpec(memory_space=pltpu.SMEM)


def with_halo(value, sides, width):
    for axis, dim in sides:
        size, length = (lax.axis_size(axis), value.shape[dim])
        up = [(i, (i + 1) % size) for i in range(size - 1)]
        down = [(j, i) for i, j in up]
        last = lax.slice_in_dim(value, length - width, length, axis=dim)
        first = lax.slice_in_dim(value, 0, width, axis=dim)
        before = lax.ppermute(last, axis, up)
        after = lax.ppermute(first, axis, down)
        value = jnp.concatenate([before, value, after], axis=dim)
    return value


def from_behind(block, axis, distance):
    devices = range(lax.axis_size(axis))
    route = [(i - distance, i) for i in devices if i - distance in devices]
    return lax.ppermute(block, axis, route)


def split_tables(length):
    indices = np.arange(length)
    angles = (indices[:, None] * indices[None, :] % length) * (2.0 * np.pi / length)
    cos_table = np.cos(angles) / np.sqrt(length)
    sin_table = np.sin(angles) / np.sqrt(length)
    forward = np.block([[cos_table, -sin_table], [sin_table, cos_table]])
    inverse = np.block([[cos_table, sin_table], [-sin_table, cos_table]])

    def stacked(table):
        coarse = table.astype(np.float32).astype(ml_dtypes.bfloat16)
        fine = (table - coarse.astype(np.float64)).astype(ml_dtypes.bfloat16)
        return np.concatenate([coarse, coarse, fine], axis=0)

    return np.stack([stacked(forward), stacked(inverse)])


def halves(value, axis):
    coarse = value.astype(jnp.bfloat16)
    fine = (value - coarse.astype(jnp.float32)).astype(jnp.bfloat16)
    return jnp.concatenate([coarse, fine, coarse], axis=axis)


def along_lanes(value, table):
    return jnp.dot(halves(value, 1), table, preferred_element_type=jnp.float32)


def along_rows(value, table):
    dims = (((0,), (0,)), ((), ()))
    return lax.dot_general(halves(value, 0), table, dims, preferred_element_type=jnp.float32)


def regroup(value, length):
    top, bottom = (value[:length], value[length:])
    return jnp.concatenate(
        [
            jnp.concatenate([top[:, :length], bottom[:, :length]], axis=1),
            jnp.concatenate([top[:, length:], bottom[:, length:]], axis=1),
        ],
        axis=0,
    )


def cut_window(places, slot, maps, plane, length):
    tall = length // 8
    tile, back, shift, upward = (places[slot, n] for n in range(4))
    sublane = lax.broadcasted_iota(jnp.int32, (tall, 8, length), 1)
    part = maps[plane, pl.ds(tile, tall + 1)]
    part = pltpu.roll(part, back, 2)[:, :, :length]
    part = pltpu.roll(part, upward, 1)
    return jnp.where(sublane + shift < 8, part[:tall], part[1:])


def lower(part, shift):
    tall, _, length = part.shape
    sublane = lax.broadcasted_iota(jnp.int32, (tall + 1, 8, length), 1)
    blank = jnp.zeros((1, 8, length), jnp.float32)
    part = pltpu.roll(part, lax.rem(shift, 8), 1)
    return jnp.where(
        sublane >= shift,
        jnp.concatenate([part, blank], axis=0),
        jnp.concatenate([blank, part], axis=0),
    )


def broaden(part, onward, breadth):
    margin = jnp.zeros(part.shape[:2] + (breadth - part.shape[2],), jnp.float32)
    return pltpu.roll(jnp.concatenate([part, margin], axis=2), onward, 2)


def add_placed(places, slot, part, totals, plane):
    breadth = totals.shape[-1]
    tile, back, shift = (places[slot, n] for n in range(3))
    onward = lax.rem(breadth - back, breadth)
    wide = broaden(lower(part, shift), onward, breadth)
    totals[plane, pl.ds(tile, wide.shape[0])] += wide


def lighting_of(probes):
    length = probes.shape[-1]
    lighting = jnp.zeros((length, length), jnp.float32)
    for mode in range(probes.shape[1]):
        lighting += probes[0, mode] * probes[0, mode] + probes[1, mode] * probes[1, mode]
    return lighting


def forward_slots(places, live, object_map, probes, intensity, turns, window, far, power):
    modes, length = (probes.shape[1], probes.shape[-1])
    slots = intensity.shape[0]
    coverage = jnp.zeros((length, length), jnp.float32)
    for slot in range(slots):
        for plane in range(2):
            part = cut_window(places, slot, object_map, plane, length)
            window[slot, plane] = part.reshape(length, length)
        lit = window[slot, 0] * window[slot, 0] + window[slot, 1] * window[slot, 1]
        coverage += jnp.where(slot < live, lit, 0.0)
    for pair in range(modes // 2):
        for slot in range(slots):
            waves = []
            for mode in (2 * pair, 2 * pair + 1):
                probe_r, probe_i = (probes[0, mode], probes[1, mode])
                obj_r, obj_i = (window[slot, 0], window[slot, 1])
                wave_r = probe_r * obj_r - probe_i * obj_i
                wave_i = probe_r * obj_i + probe_i * obj_r
                waves.append(jnp.concatenate([wave_r, wave_i], axis=1))
            half = regroup(along_lanes(jnp.concatenate(waves, axis=0), turns[0]), length)
            spread = along_rows(half, turns[0])
            far[slot, pair] = spread
            square = spread * spread
            square = square[:, :length] + square[:, length:]
            square = square[:length] + square[length:]
            if pair == 0:
                power[slot] = square
            else:
                power[slot] += square
    for slot in range(slots):
        ratio = jnp.sqrt(intensity[slot].T / jnp.maximum(power[slot], 1.0)) - 1.0
        power[slot] = jnp.where(slot < live, ratio, 0.0)
    return coverage


def backward_slot(slot, pair, probes_of, turns, window, far, power, terms):
    length = power.shape[-1]
    factor = power[slot]
    factor = jnp.concatenate([factor, factor], axis=1)
    factor = jnp.concatenate([factor, factor], axis=0)
    half = regroup(along_lanes(far[slot, pair] * factor, turns[1]), length)
    change = along_rows(half, turns[1])
    obj_r, obj_i = (window[slot, 0], window[slot, 1])
    terms_r = jnp.zeros((length, length), jnp.float32)
    terms_i = jnp.zeros((length, length), jnp.float32)
    moved_r, moved_i = ([], [])
    for which in range(2):
        rows = slice(which * length, (which + 1) * length)
        change_r, change_i = (change[rows, :length], change[rows, length:])
        probe_r, probe_i = probes_of(2 * pair + which)
        terms_r += probe_r * change_r + probe_i * change_i
        terms_i += probe_r * change_i - probe_i * change_r
        moved_r.append(obj_r * change_r + obj_i * change_i)
        moved_i.append(obj_r * change_i - obj_i * change_r)
    if pair == 0:
        terms[slot, 0] = terms_r
        terms[slot, 1] = terms_i
    else:
        terms[slot, 0] += terms_r
        terms[slot, 1] += terms_i
    return moved_r, moved_i


def slots_kernel(
    places, counts, object_map, probes, intensity, turns, totals, sums, window, far, power, terms
):
    modes, length = (probes.shape[1], probes.shape[-1])
    tall = length // 8
    live = counts[0]
    totals[...] = jnp.zeros_like(totals)
    terms[0, 2] = lighting_of(probes)
    sums[2 * modes] = forward_slots(
        places, live, object_map, probes, intensity, turns, window, far, power
    )
    for pair in range(modes // 2):
        for slot in range(intensity.shape[0]):
            moved_r, moved_i = backward_slot(
                slot, pair, lambda k: (probes[0, k], probes[1, k]), turns, window, far, power, terms
            )
            for which in range(2):
                mode = 2 * pair + which
                if slot == 0:
                    sums[mode] = moved_r[which]
                    sums[modes + mode] = moved_i[which]
                else:
                    sums[mode] += moved_r[which]
                    sums[modes + mode] += moved_i[which]

    def place_slot(slot, carry):
        for plane in range(3):
            part = terms[slot, plane] if plane < 2 else terms[0, 2]
            add_placed(places, slot, part.reshape(tall, 8, length), totals, plane)
        return carry

    lax.fori_loop(0, live, place_slot, 0)


def accumulate(object_map, probes, places, counts, intensity, turns):
    _, modes, length, _ = probes.shape
    slots = intensity.shape[0]
    return pl.pallas_call(
        slots_kernel,
        out_shape=(
            jax.ShapeDtypeStruct((3,) + object_map.shape[1:], jnp.float32),
            jax.ShapeDtypeStruct((2 * modes + 1, length, length), jnp.float32),
        ),
        in_specs=[scalars, scalars] + [memory] * 4,
        out_specs=(memory, memory),
        scratch_shapes=[
            pltpu.VMEM((slots, 2, length, length), jnp.float32),
            pltpu.VMEM((slots, modes // 2, 2 * length, 2 * length), jnp.float32),
            pltpu.VMEM((slots, length, length), jnp.float32),
            pltpu.VMEM((slots, 3, length, length), jnp.float32),
        ],
        compiler_params=pltpu.CompilerParams(vmem_limit_bytes=36 * 1024 * 1024),
        name="slots",
    )(places, counts, object_map, probes, intensity, turns)


def outward_kernel(
    places, counts, object_map, probes, intensity, turns, window, far, power, coverage, lit, light
):
    length = probes.shape[-1]
    live = counts[0]
    lit[...] = jnp.zeros_like(lit)
    light[...] = lighting_of(probes).reshape(light.shape)
    coverage[...] = forward_slots(
        places, live, object_map, probes, intensity, turns, window, far, power
    )

    def place_slot(slot, carry):
        add_placed(places, slot, light[...], lit, 0)
        return carry

    lax.fori_loop(0, live, place_slot, 0)


def outward(object_map, probes, places, counts, intensity, turns):
    _, modes, length, _ = probes.shape
    slots = intensity.shape[0]
    shapes = (
        (slots, 2, length, length),
        (slots, modes // 2, 2 * length, 2 * length),
        (slots, length, length),
        (length, length),
        (1,) + object_map.shape[1:],
    )
    return pl.pallas_call(
        outward_kernel,
        out_shape=tuple(jax.ShapeDtypeStruct(shape, jnp.float32) for shape in shapes),
        in_specs=[scalars, scalars] + [memory] * 4,
        out_specs=(memory,) * 5,
        scratch_shapes=[pltpu.VMEM((length // 8, 8, length), jnp.float32)],
        compiler_params=pltpu.CompilerParams(vmem_limit_bytes=20 * 1024 * 1024),
        name="outward",
    )(places, counts, object_map, probes, intensity, turns)


def window_places(starts, rows, lanes, length, lead):
    rows_at = jnp.clip(starts[:, 0], 0, rows - length)
    cols_at = jnp.clip(starts[:, 1], 0, lanes - length)
    tile = jnp.minimum(rows_at // 8, (rows - length) // 8 - 1)
    shift = rows_at - 8 * tile
    back = (lanes + lead - cols_at) % lanes
    return jnp.stack([tile, back, shift, (8 - shift) % 8], axis=1)


def mixing(probes, probe_step):
    mix_r = jnp.sum(probes[0] * probe_step[0] + probes[1] * probe_step[1], axis=0)
    mix_i = jnp.sum(probes[0] * probe_step[1] - probes[1] * probe_step[0], axis=0)
    return (mix_r, mix_i)


def cross_term(object_map, change, starts, active, mix_r, mix_i):
    length = mix_r.shape[-1]
    anchor_index = jnp.int32(0)

    def cross_visit_slot(running, element):
        corner_at, weight = element
        corner = (anchor_index, corner_at[0], corner_at[1])
        object_win = lax.dynamic_slice(object_map, corner, (2, length, length))
        change_win = lax.dynamic_slice(change, corner, (2, length, length))
        aligned = change_win[0] * object_win[0] + change_win[1] * object_win[1]
        rotated = change_win[0] * object_win[1] - change_win[1] * object_win[0]
        return (running + weight * jnp.sum(aligned * mix_r - rotated * mix_i), None)

    running, _ = lax.scan(cross_visit_slot, jnp.zeros((), jnp.float32), (starts, active))
    return running


def solve_steps(object_curve, cross_curve, probe_curve, object_slope, probe_slope):
    object_diag = 1.1 * object_curve + 0.001
    probe_diag = 1.1 * probe_curve + 0.001
    determinant = object_diag * probe_diag - cross_curve * cross_curve
    object_rate = (probe_diag * object_slope - cross_curve * probe_slope) / determinant
    probe_rate = (object_diag * probe_slope - cross_curve * object_slope) / determinant
    return (object_rate, probe_rate)


def widen(planes, margin):
    return with_halo(planes, (("tx", 1), ("ty", 2)), margin)


def fold_rims(totals, margin, height, breadth):
    middle = totals[:, margin : margin + height, :]
    for direction in (1, -1):
        border = totals[:, margin + height :, :] if direction == 1 else totals[:, :margin, :]
        arrived = from_behind(border, "tx", direction)
        if direction == 1:
            middle = jnp.concatenate([middle + arrived, middle[:, margin:, :]], axis=1)
        else:
            middle = jnp.concatenate([middle[:, : height - margin, :], middle + arrived], axis=1)
    interior = middle[:, :, margin : margin + breadth]
    for direction in (1, -1):
        border = middle[:, :, margin + breadth :] if direction == 1 else middle[:, :, :margin]
        arrived = from_behind(border, "ty", direction)
        if direction == 1:
            interior = jnp.concatenate(
                [interior[:, :, :margin] + arrived, interior[:, :, margin:]], axis=2
            )
        else:
            interior = jnp.concatenate(
                [interior[:, :, : breadth - margin], interior[:, :, breadth - margin :] + arrived],
                axis=2,
            )
    return interior


def general(object_field, probe_modes, positions, counts, intensity):
    length = probe_modes.shape[-1]
    margin = length // 2
    height = object_field.shape[1]
    breadth = object_field.shape[2]
    turns = split_tables(length)
    modes = probe_modes.shape[1]
    anchor = jnp.stack(
        [lax.axis_index("tx") * height - margin, lax.axis_index("ty") * breadth - margin]
    )
    starts = positions - anchor[None, :]
    active = (jnp.arange(positions.shape[0], dtype=jnp.int32) < counts[0]).astype(jnp.float32)
    places = window_places(starts, height + 2 * margin, breadth + 2 * margin, length, 0)
    object_map = object_field
    probes = probe_modes
    extended = widen(object_map, margin)
    for repeat in range(ITERS):
        tiled = extended.reshape(2, -1, 8, extended.shape[-1])
        totals, sums = accumulate(tiled, probes, places, counts, intensity, turns)
        totals = totals.reshape((3,) + extended.shape[1:])
        interior = fold_rims(totals, margin, height, breadth)
        change = interior[:2] / jnp.maximum(interior[2], 1.0)
        object_part = jnp.sum((change[0] * change[0] + change[1] * change[1]) * interior[2])
        slope_part = jnp.sum(interior[:2] * change)
        wide_change = widen(change, margin)
        sums = lax.psum(sums, ("tx", "ty"))
        probe_total = sums[: 2 * modes].reshape(probes.shape)
        weight_total = sums[2 * modes]
        probe_step = probe_total / (weight_total + 1e-05)
        mix_r, mix_i = mixing(probes, probe_step)
        cross_part = cross_term(extended, wide_change, starts, active, mix_r, mix_i)
        object_curve, cross_curve, object_slope = lax.psum(
            (object_part, cross_part, slope_part), ("tx", "ty")
        )
        probe_curve = jnp.sum(
            (probe_step[0] * probe_step[0] + probe_step[1] * probe_step[1]) * weight_total
        )
        probe_slope = jnp.sum(probe_total * probe_step)
        object_rate, probe_rate = solve_steps(
            object_curve, cross_curve, probe_curve, object_slope, probe_slope
        )
        object_map = object_map + object_rate * change
        probes = probes + probe_rate * probe_step
        if repeat + 1 < ITERS:
            extended = extended + object_rate * wide_change
    return (object_map, probes)

outside = pl.BlockSpec(memory_space=pltpu.HBM)
OTHERS = [(i, j) for i in range(4) for j in range(4) if i or j]
AROUND = [(i, j) for i in (-1, 0, 1) for j in (-1, 0, 1) if i or j]
SIDES = [(i, j) for i in (-1, 0, 1) for j in (-1, 1)]


def everyone(row, col):
    return [{"tx": (row + i) % 4, "ty": (col + j) % 4} for i, j in OTHERS]


def greet(peers):
    barrier = pltpu.get_barrier_semaphore()
    for peer in peers:
        pl.semaphore_signal(barrier, 1, device_id=peer, device_id_type=pl.DeviceIdType.MESH)
    pl.semaphore_wait(barrier, len(peers))


class Copies:
    def __init__(self, send, arrive):
        self.send, self.arrive, self.count = (send, arrive, 0)
        self.unsent = []

    def slots(self, number):
        self.count += number
        return self.count - number

    def make(self, source, target, index, landing, peer):
        return pltpu.make_async_remote_copy(
            src_ref=source,
            dst_ref=target,
            send_sem=self.send.at[index],
            recv_sem=self.arrive.at[landing],
            device_id=peer,
            device_id_type=pl.DeviceIdType.MESH,
        )

    def start(self, source, target, peer):
        index = self.slots(1)
        copy = self.make(source, target, index, index, peer)
        copy.start()
        self.unsent.append(copy)
        return copy

    def group(self, items, view):
        index = self.slots(1)
        for source, target, peer in items:
            self.make(source, target, index, index, peer).start()
        whole = self.make(view, view, index, index, items[0][2])
        self.unsent.append(whole)
        return whole

    def finish(self):
        for copy in self.unsent:
            copy.wait_send()
        self.unsent = []


class Ring:
    def __init__(self, copies, row, col, source, target):
        self.copies, self.row, self.col = (copies, row, col)
        self.source, self.target = (source, target)
        self.base = copies.slots(len(AROUND))

    def each(self, what):
        for k, (i, j) in enumerate(AROUND):
            row, col = (self.row + i, self.col + j)
            inside = (row >= 0) & (row < 4) & (col >= 0) & (col < 4)
            pl.when(inside)(functools.partial(what, k, i, j, {"tx": row, "ty": col}))

    def outgoing(self, k, i, j, peer):
        landing = AROUND.index((-i, -j))
        return self.copies.make(
            self.source(i, j), self.target(-i, -j), self.base + k, self.base + landing, peer
        )

    def blank(self):
        for i, j in AROUND:
            row, col = (self.row + i, self.col + j)
            inside = (row >= 0) & (row < 4) & (col >= 0) & (col < 4)
            target = self.target(i, j)

            @pl.when(jnp.logical_not(inside))
            def _():
                target[...] = jnp.zeros(target.shape, jnp.float32)

    def start(self):
        self.each(lambda k, i, j, peer: self.outgoing(k, i, j, peer).start())

    def receive(self):
        def arrived(k, i, j, peer):
            index = self.base + k
            self.copies.make(self.source(i, j), self.target(i, j), index, index, peer).wait_recv()

        self.each(arrived)

    def finish(self):
        self.each(lambda k, i, j, peer: self.outgoing(k, i, j, peer).wait_send())


class Edges:
    def __init__(self, copies, row, col, axis, source, target):
        self.copies, self.axis = (copies, axis)
        self.source, self.target = (source, target)
        self.place = {"tx": row, "ty": col}
        self.base = copies.slots(2)

    def each(self, what, missing=False):
        for k, ahead in ((0, -1), (1, 1)):
            there = self.place[self.axis] + ahead
            inside = (there >= 0) & (there < 4)
            inside = jnp.logical_not(inside) if missing else inside
            peer = {**self.place, self.axis: there}
            pl.when(inside)(functools.partial(what, k, peer))

    def blank(self):
        def clear(k, peer):
            target = self.target(k)
            target[...] = jnp.zeros(target.shape, jnp.float32)

        self.each(clear, missing=True)

    def outgoing(self, k, peer):
        landing = 1 - k
        return self.copies.make(
            self.source(k), self.target(landing), self.base + k, self.base + landing, peer
        )

    def start(self):
        self.each(lambda k, peer: self.outgoing(k, peer).start())

    def receive(self):
        def arrived(k, peer):
            index = self.base + k
            self.copies.make(self.source(k), self.target(k), index, index, peer).wait_recv()

        self.each(arrived)

    def finish(self):
        self.each(lambda k, peer: self.outgoing(k, peer).wait_send())


def early_lanes(value):
    return lax.broadcasted_iota(jnp.int32, value.shape, value.ndim - 1) < value.shape[-1] // 2


def turned(value):
    return pltpu.roll(value, value.shape[-1] // 2, value.ndim - 1)


def pack_first(block):
    half = block.shape[1] // 2
    top, bottom = (block[:, :half], block[:, half:])
    return jnp.where(early_lanes(top), top, turned(bottom))


def pack_last(block):
    half = block.shape[1] // 2
    top, bottom = (block[:, :half], block[:, half:])
    return jnp.where(early_lanes(top), turned(top), bottom)


def unpack(first, last):
    early = early_lanes(first)
    top = jnp.where(early, first, turned(last))
    bottom = jnp.where(early, turned(first), last)
    return jnp.concatenate([top, bottom], axis=1)


def row_range(i, high):
    return slice((i + 1) * high, (i + 2) * high)


def halo_ring(copies, row, col, own, packed, above, beside):
    def source(i, j):
        return own if j == 0 else packed.at[(j + 1) // 2]

    def target(i, j):
        return above.at[(i + 1) // 2] if j == 0 else beside.at[SIDES.index((i, j))]

    return Ring(copies, row, col, source, target)


def spread_halo(own, above, beside, wide):
    high, broad = (own.shape[1], own.shape[-1])
    for i in (-1, 0, 1):
        rows = row_range(i, high)
        wide[:, rows, :, :broad] = own if i == 0 else above[(i + 1) // 2]
        wide[:, rows, :, broad:] = unpack(
            beside[SIDES.index((i, 1))], beside[SIDES.index((i, -1))]
        )


def widen_kernel(
    own_at, probes_at, turns_at, intensity_at, wide, probes, turns, intensity, own, whole, packed, above,
    beside, local, send, arrive,
):
    row, col = (lax.axis_index("tx"), lax.axis_index("ty"))
    fetches = [
        pltpu.make_async_copy(source, target, local.at[k])
        for k, (source, target) in enumerate(
            ((own_at, own), (probes_at, probes), (turns_at, turns), (intensity_at, intensity))
        )
    ]
    for fetch in fetches:
        fetch.start()
    copies = Copies(send, arrive)
    ring = halo_ring(copies, row, col, whole, packed, above, beside)
    ring.blank()
    fetches[0].wait()
    block = own[...].reshape(2, own.shape[1] // 8, 8, own.shape[2])
    whole[...] = block
    packed[0] = pack_first(block)
    packed[1] = pack_last(block)
    greet(everyone(row, col))
    ring.start()
    for fetch in fetches[1:]:
        fetch.wait()
    ring.receive()
    spread_halo(block, above, beside, wide)
    ring.finish()


def halo_scratch(high, broad):
    return [
        pltpu.VMEM((2, 2, high // 2, 8, broad), jnp.float32),
        pltpu.VMEM((2, 2, high, 8, broad), jnp.float32),
        pltpu.VMEM((6, 2, high // 2, 8, broad), jnp.float32),
    ]


def widen_tiles(own, probes, turns, intensity):
    two, height, broad = own.shape
    high = height // 8

    def like(value):
        return jax.ShapeDtypeStruct(value.shape, value.dtype)

    return pl.pallas_call(
        widen_kernel,
        out_shape=(
            jax.ShapeDtypeStruct((two, 3 * high, 8, 2 * broad), jnp.float32),
            like(probes),
            like(turns),
            like(intensity),
        ),
        in_specs=[outside] * 4,
        out_specs=(memory,) * 4,
        scratch_shapes=[
            pltpu.VMEM(own.shape, jnp.float32),
            pltpu.VMEM((two, high, 8, broad), jnp.float32),
        ]
        + halo_scratch(high, broad)
        + [
            pltpu.SemaphoreType.DMA((4,)),
            pltpu.SemaphoreType.DMA((8,)),
            pltpu.SemaphoreType.DMA((8,)),
        ],
        compiler_params=pltpu.CompilerParams(
            collective_id=0, has_side_effects=True, vmem_limit_bytes=51300 * 1024
        ),
        name="widen",
    )(own, probes, turns, intensity)


def in_rows(values, lanes):
    at = lax.broadcasted_iota(jnp.int32, (8, lanes), 0)
    result = jnp.zeros((8, lanes), jnp.float32)
    for place, value in enumerate(values):
        result = jnp.where(at == place, value, result)
    return result


def settle_kernel(
    last, places, weights, object_map, probes, turns, window, far, power, coverage, lit, *rest
):
    if last:
        got, change_own, rates_out = rest[:3]
    else:
        new_map, new_probes, got = rest[:3]
    rest = rest[3:]
    sums, r1, acc, r2, acca, r3 = (rest[4 * n : 4 * n + 4] for n in range(6))
    (
        terms, padded, totals, fold_out, fold_in, upright, over, column, near_out, near, wide,
        held, mix, mine, pair_in, ours, inbox, send, arrive,
    ) = rest[24:]
    row, col = (lax.axis_index("tx"), lax.axis_index("ty"))
    core, side = (col % 2, col // 2)
    rows, broad = (column.shape[1], column.shape[-1])
    high = rows // 3
    tall, length = (2 * high, power.shape[-1])
    slots = places.shape[0]
    modes = probes.shape[1]
    pairs = modes // 2
    blocks = probes.shape[2:]
    middle = slice(high, 2 * high)
    ends = (slice(0, high), slice(2 * high, 3 * high))
    peers = everyone(row, col)
    partner = {"tx": row, "ty": side * 2 + (1 - core)}
    across = {"tx": row, "ty": (1 - side) * 2 + core}
    along = [{"tx": (row + j) % 4, "ty": col} for j in (1, 2, 3)]
    places_of = [
        ((side + j) % 2, (row + i) % 4) for i in range(4) for j in range(2) if i or j
    ]
    chips = [{"tx": there, "ty": aside * 2 + core} for aside, there in places_of]
    copies = Copies(send, arrive)
    spot = (core, side, row)

    barrier = pltpu.get_barrier_semaphore()
    for peer in peers:
        pl.semaphore_signal(barrier, 1, device_id=peer, device_id_type=pl.DeviceIdType.MESH)

    def edges(axis, source, target):
        made = Edges(copies, row, col, axis, source, target)
        made.blank()
        return made

    fold_side = edges("ty", lambda k: fold_out.at[k], lambda k: fold_in.at[k])
    fold_over = edges("tx", lambda k: upright.at[:, ends[k]], lambda k: over.at[k])
    halo_over = edges("tx", lambda k: column.at[:, middle], lambda k: column.at[:, ends[k]])
    halo_side = edges("ty", lambda k: near_out.at[k], lambda k: near.at[k])
    padded[...] = jnp.zeros_like(padded)
    totals[:2] = jnp.zeros((2,) + totals.shape[1:], jnp.float32)
    totals[2] = lit[0]

    def probes_of(mode):
        return tuple(probes[part, mode].reshape(length, length) for part in range(2))

    def compute(pair):
        for slot in range(slots):
            moved_r, moved_i = backward_slot(
                slot, pair, probes_of, turns, window, far, power, terms
            )
            for n, value in enumerate(moved_r + moved_i):
                value = value.reshape(blocks)
                if slot == 0:
                    sums[pair][:, :, :, n] = value
                else:
                    sums[pair][:, :, :, n] += value

    shared = {}
    moving = {}

    def core_sum(n):
        moving[n] = copies.start(sums[n].at[1 - core], r1[n], partner)

    def outer_sum(n):
        moving[n].wait_recv()
        acc[n][...] = sums[n][core] + r1[n][...]
        moving[n] = copies.start(acc[n].at[1 - side], r2[n], across)

    def rows_sum(n):
        moving[n].wait_recv()
        acca[n][...] = acc[n][side] + r2[n][...]
        items = [(acca[n].at[peer["tx"]], r3[n].at[k], peer) for k, peer in enumerate(along)]
        moving[n] = copies.group(items, r3[n])

    def give(n, block, peer):
        moving[n] = copies.start(block, block, peer)

    def slab(n):
        moving[n].wait_recv()
        total = acca[n][row] + r3[n][0] + r3[n][1] + r3[n][2]
        if n == 0:
            shared["weight"] = total[4]
            total = total[:4]
        weight = shared["weight"]
        found = total / (weight + 1e-05)
        got[(n,) + spot] = found
        block = got.at[(n,) + spot]
        view = got.at[n, core, side, pl.ds(0, 3)]
        moving[n] = copies.group([(block, block, peer) for peer in along], view)
        some = slice(2 * n, 2 * n + 2)
        probe_r, probe_i = (probes[(0, some) + spot], probes[(1, some) + spot])
        for name, value in (
            ("mix_r", probe_r * found[:2] + probe_i * found[2:]),
            ("mix_i", probe_r * found[2:] - probe_i * found[:2]),
            ("curve", found * found * weight),
            ("slope", total * found),
        ):
            value = jnp.sum(value, axis=0)
            shared[name] = value if n == 0 else shared[name] + value

    def across_give(n):
        moving[n].wait_recv()
        give(n, got.at[n, core, side], across)

    def core_give(n):
        moving[n].wait_recv()
        give(n, got.at[n, core], partner)

    sums[0][:, :, :, 4] = coverage[...].reshape(blocks)
    compute(0)
    pl.semaphore_wait(barrier, len(peers))
    core_sum(0)
    compute(1)
    core_sum(1)
    outer_sum(0)
    compute(2)
    core_sum(2)
    outer_sum(1)
    compute(3)
    core_sum(3)
    outer_sum(2)
    rows_sum(0)

    for slot in range(slots):
        tile, back, shift = (places[slot, n] for n in range(3))
        onward = lax.rem(2 * broad - back, 2 * broad)
        for plane in range(2):
            keep = padded.at[slot % 2, plane]
            keep[high : high + tall + 1] = lower(terms[slot, plane].reshape(tall, 8, length), shift)
            part = padded[slot % 2, plane, pl.ds(high - tile, 3 * high)]
            totals[plane] += broaden(part, onward, 2 * broad)
    rim = totals[:, :, :, broad:]
    fold_out[0] = pack_last(rim)
    fold_out[1] = pack_first(rim)
    fold_side.start()
    outer_sum(3)
    rows_sum(1)
    rows_sum(2)
    slab(0)

    fold_side.receive()
    upright[...] = totals[:, :, :, :broad] + unpack(fold_in[0], fold_in[1])
    fold_over.start()
    rows_sum(3)
    slab(1)
    slab(2)
    slab(3)
    mix[spot + (0,)] = shared["mix_r"]
    mix[spot + (1,)] = shared["mix_i"]
    block = mix.at[spot]
    mixes = [copies.start(block, block, peer) for peer in chips]

    fold_over.receive()
    interior = upright[:, middle] + over[0] + over[1]
    moved = interior[:2] / jnp.maximum(interior[2], 1.0)
    column[:, middle] = moved
    halo_over.start()
    across_give(0)
    across_give(1)
    curve = jnp.sum((moved[0] * moved[0] + moved[1] * moved[1]) * interior[2])
    slope = jnp.sum(interior[:2] * moved)
    probe_curve = jnp.sum(shared["curve"])
    probe_slope = jnp.sum(shared["slope"])

    halo_over.receive()
    near_out[0] = pack_first(column[...])
    near_out[1] = pack_last(column[...])
    halo_side.start()
    across_give(2)
    across_give(3)
    core_give(0)
    wide[:, :, :, :broad] = column[...]

    halo_side.receive()
    wide[:, :, :, broad:] = unpack(near[1], near[0])
    held[0] = wide[0] * object_map[0] + wide[1] * object_map[1]
    held[1] = wide[0] * object_map[1] - wide[1] * object_map[0]
    gathered = []
    for plane in range(2):
        running = jnp.zeros((tall, 8, broad), jnp.float32)
        for slot in range(slots):
            running += weights[slot] * cut_window(places, slot, held, plane, length)
        gathered.append(running)
    for copy in mixes:
        copy.wait_recv()
    block = mix.at[core]
    mix_pass = copies.start(block, block, partner)
    core_give(1)
    core_give(3)
    mix_pass.wait_recv()
    mix_r, mix_i = (mix[:, :, :, n].reshape(tall, 8, broad) for n in range(2))
    cross = jnp.sum(gathered[0] * mix_r - gathered[1] * mix_i)
    mine[...] = in_rows((curve, slope, probe_curve, probe_slope, cross), broad)
    pair_sent = copies.start(mine, pair_in, partner)
    core_give(2)
    pair_sent.wait_recv()
    ours[...] = mine[...] + pair_in[...]
    scalars_sent = copies.group([(ours, inbox.at[k], peer) for k, peer in enumerate(chips)], inbox)
    copies.finish()
    for made in (fold_side, fold_over, halo_over, halo_side):
        made.finish()
    for n in range(pairs):
        moving[n].wait_recv()
    scalars_sent.wait_recv()
    sent = ours[...] + jnp.sum(inbox[...], axis=0)
    object_rate, probe_rate = solve_steps(
        sent[0:1], sent[4:5], sent[2:3], sent[1:2], sent[3:4]
    )
    object_rate = jnp.broadcast_to(object_rate, (8, broad))
    probe_rate = jnp.broadcast_to(probe_rate, (8, broad))
    if last:
        at = lax.broadcasted_iota(jnp.int32, (8, broad), 0)
        rates_out[...] = jnp.where(at == 0, object_rate, probe_rate)
        change_own[...] = column[:, middle]
    else:
        both = jnp.concatenate([object_rate, object_rate], axis=1)
        new_map[...] = object_map[...] + both * wide[...]
        for n in range(pairs):
            for part in range(2):
                for which in range(2):
                    at = (part, 2 * n + which)
                    stepped = got[n, :, :, :, 2 * part + which]
                    new_probes[at] = probes[at] + probe_rate * stepped


def settle(last, places, weights, object_map, probes, turns, spread):
    _, rows, _, lanes = object_map.shape
    modes, length = (probes.shape[1], probes.shape[-1])
    slots = places.shape[0]
    high, broad = (rows // 3, lanes // 2)
    f32 = jnp.float32
    grid = (2, 2, 4)
    step = jax.ShapeDtypeStruct((modes // 2,) + grid + (4, 8, length), f32)
    if last:
        out_shape = (
            step,
            jax.ShapeDtypeStruct((2, high, 8, broad), f32),
            jax.ShapeDtypeStruct((8, broad), f32),
        )
    else:
        out_shape = (
            jax.ShapeDtypeStruct(object_map.shape, f32),
            jax.ShapeDtypeStruct((2, modes) + grid + (8, length), f32),
            step,
        )
    scratch = [
        lead + (5 if pair == 0 else 4, 8, length)
        for lead in (grid, (2, 4), (2, 4), (4,), (4,), (3,))
        for pair in range(modes // 2)
    ] + [
        (slots, 2, length, length),
        (2, 2, 4 * high + 1, 8, length),
        (3, rows, 8, lanes),
        (2, 3, rows // 2, 8, broad),
        (2, 3, rows // 2, 8, broad),
        (3, rows, 8, broad),
        (2, 3, high, 8, broad),
        (2, rows, 8, broad),
        (2, 2, rows // 2, 8, broad),
        (2, 2, rows // 2, 8, broad),
        (2, rows, 8, lanes),
        (2, rows, 8, lanes),
        grid + (2, 8, length),
        (8, broad),
        (8, broad),
        (8, broad),
        (7, 8, broad),
    ]
    return pl.pallas_call(
        functools.partial(settle_kernel, last),
        out_shape=out_shape,
        in_specs=[scalars, scalars] + [memory] * 8,
        out_specs=(memory,) * 3,
        scratch_shapes=[pltpu.VMEM(shape, f32) for shape in scratch]
        + [pltpu.SemaphoreType.DMA((52,)), pltpu.SemaphoreType.DMA((52,))],
        compiler_params=pltpu.CompilerParams(
            collective_id=2 if last else 1,
            has_side_effects=True,
            vmem_limit_bytes=28 * 1024 * 1024,
        ),
        name="finish" if last else "settle",
    )(
        places,
        weights,
        object_map,
        probes.reshape((2, modes) + grid + (8, length)),
        turns,
        *spread,
    )


def apply_kernel(object_map, change, probes, step, rates, object_at, probes_at, tile, fresh, done):
    modes = probes.shape[1]
    high, broad = (change.shape[1], change.shape[3])
    object_rate = jnp.broadcast_to(rates[0:1], (8, broad))
    probe_rate = jnp.broadcast_to(rates[1:2], (8, broad))
    copies = []
    for part in range(2):
        for first in range(0, modes, 4):
            some = slice(first, first + 4)
            stepped = jnp.stack(
                [step[mode // 2, :, 2 * part + mode % 2] for mode in range(first, first + 4)]
            )
            moved = probes[part, some] + probe_rate * stepped
            fresh[part, some] = moved.reshape((4,) + fresh.shape[2:])
            block = (part, pl.ds(first, 4))
            copies.append(
                pltpu.make_async_copy(fresh.at[block], probes_at.at[block], done.at[len(copies)])
            )
            copies[-1].start()
    moved = object_map[:, high : 2 * high, :, :broad] + object_rate * change[...]
    tile[...] = moved.reshape(tile.shape)
    copies.append(pltpu.make_async_copy(tile, object_at, done.at[len(copies)]))
    copies[-1].start()
    for copy in copies:
        copy.wait()


def apply(object_map, change, probes, step, rates):
    _, high, _, broad = change.shape
    modes, length = (probes.shape[1], probes.shape[-1])
    shapes = ((2, 8 * high, broad), (2, modes, length, length))
    blocks = (2, modes, length // 8, 8, length)
    return pl.pallas_call(
        apply_kernel,
        out_shape=tuple(jax.ShapeDtypeStruct(shape, jnp.float32) for shape in shapes),
        in_specs=[memory] * 5,
        out_specs=(outside,) * 2,
        scratch_shapes=[pltpu.VMEM(shape, jnp.float32) for shape in shapes]
        + [pltpu.SemaphoreType.DMA((modes // 2 + 1,))],
        compiler_params=pltpu.CompilerParams(vmem_limit_bytes=8 * 1024 * 1024),
        name="apply",
    )(
        object_map,
        change,
        probes.reshape(blocks),
        step.reshape((modes // 2, length // 8, 4, 8, length)),
        rates,
    )


def direct(object_field, probe_modes, positions, counts, intensity):
    two, modes, length, _ = probe_modes.shape
    margin = length // 2
    _, height, breadth = object_field.shape
    anchor = jnp.stack(
        [lax.axis_index("tx") * height - margin, lax.axis_index("ty") * breadth - margin]
    )
    starts = positions - anchor[None, :]
    lanes = 2 * breadth
    places = window_places(starts, height + 2 * margin, lanes, length, margin)
    weights = (jnp.arange(positions.shape[0], dtype=jnp.int32) < counts[0]).astype(jnp.float32)
    object_map, probes, turns, measured = widen_tiles(
        object_field,
        probe_modes,
        jnp.asarray(split_tables(length)),
        intensity,
    )
    for repeat in range(ITERS):
        spread = outward(object_map, probes, places, counts, measured, turns)
        last = repeat + 1 == ITERS
        settled = settle(last, places, weights, object_map, probes, turns, spread)
        if not last:
            object_map, probes, _ = settled
            probes = probes.reshape(probe_modes.shape)
    step, change, rates = settled
    return apply(object_map, change, probes, step, rates)


def shards(object_field, probe_modes, positions, counts, intensity):
    _, height, breadth = object_field.shape
    length = probe_modes.shape[-1]
    grid = (lax.axis_size("tx"), lax.axis_size("ty"))
    arguments = (object_field, probe_modes, positions, counts, intensity)
    if grid == (4, 4) and length == 128 and (2 * height, breadth) == (length, length):
        return direct(*arguments)
    return general(*arguments)


def solution(mesh):
    return jax.shard_map(
        shards,
        mesh=mesh,
        in_specs=(
            P("groups", "tx", "ty"),
            P("groups", None, None, None),
            P(("groups", "tx", "ty"), None),
            P(("groups", "tx", "ty")),
            P(("groups", "tx", "ty"), None, None),
        ),
        out_specs=(P("groups", "tx", "ty"), P("groups", None, None, None)),
        check_vma=False,
    )
```

```python
import functools

import jax
import jax.numpy as jnp
import ml_dtypes
import numpy as np
from jax import lax
from jax.experimental import pallas as pl
from jax.experimental.pallas import tpu as pltpu
from jax.sharding import PartitionSpec as P

ITERS = 2
memory = pl.BlockSpec(memory_space=pltpu.VMEM)
scalars = pl.BlockSpec(memory_space=pltpu.SMEM)


def with_halo(value, sides, width):
    for axis, dim in sides:
        size, length = (lax.axis_size(axis), value.shape[dim])
        up = [(i, (i + 1) % size) for i in range(size - 1)]
        down = [(j, i) for i, j in up]
        last = lax.slice_in_dim(value, length - width, length, axis=dim)
        first = lax.slice_in_dim(value, 0, width, axis=dim)
        before = lax.ppermute(last, axis, up)
        after = lax.ppermute(first, axis, down)
        value = jnp.concatenate([before, value, after], axis=dim)
    return value


def from_behind(block, axis, distance):
    devices = range(lax.axis_size(axis))
    route = [(i - distance, i) for i in devices if i - distance in devices]
    return lax.ppermute(block, axis, route)


def split_tables(length):
    indices = np.arange(length)
    angles = (indices[:, None] * indices[None, :] % length) * (2.0 * np.pi / length)
    cos_table = np.cos(angles) / np.sqrt(length)
    sin_table = np.sin(angles) / np.sqrt(length)
    forward = np.block([[cos_table, -sin_table], [sin_table, cos_table]])
    inverse = np.block([[cos_table, sin_table], [-sin_table, cos_table]])

    def stacked(table):
        coarse = table.astype(np.float32).astype(ml_dtypes.bfloat16)
        fine = (table - coarse.astype(np.float64)).astype(ml_dtypes.bfloat16)
        return np.concatenate([coarse, coarse, fine], axis=0)

    return np.stack([stacked(forward), stacked(inverse)])


def halves(value, axis):
    coarse = value.astype(jnp.bfloat16)
    fine = (value - coarse.astype(jnp.float32)).astype(jnp.bfloat16)
    return jnp.concatenate([coarse, fine, coarse], axis=axis)


def along_lanes(value, table):
    return jnp.dot(halves(value, 1), table, preferred_element_type=jnp.float32)


def along_rows(value, table):
    dims = (((0,), (0,)), ((), ()))
    return lax.dot_general(halves(value, 0), table, dims, preferred_element_type=jnp.float32)


def regroup(value, length):
    top, bottom = (value[:length], value[length:])
    return jnp.concatenate(
        [
            jnp.concatenate([top[:, :length], bottom[:, :length]], axis=1),
            jnp.concatenate([top[:, length:], bottom[:, length:]], axis=1),
        ],
        axis=0,
    )


def cut_window(places, slot, maps, plane, length):
    tall = length // 8
    tile, back, shift, upward = (places[slot, n] for n in range(4))
    sublane = lax.broadcasted_iota(jnp.int32, (tall, 8, length), 1)
    part = maps[plane, pl.ds(tile, tall + 1)]
    part = pltpu.roll(part, back, 2)[:, :, :length]
    part = pltpu.roll(part, upward, 1)
    return jnp.where(sublane + shift < 8, part[:tall], part[1:])


def lower(part, shift):
    tall, _, length = part.shape
    sublane = lax.broadcasted_iota(jnp.int32, (tall + 1, 8, length), 1)
    blank = jnp.zeros((1, 8, length), jnp.float32)
    part = pltpu.roll(part, lax.rem(shift, 8), 1)
    return jnp.where(
        sublane >= shift,
        jnp.concatenate([part, blank], axis=0),
        jnp.concatenate([blank, part], axis=0),
    )


def broaden(part, onward, breadth):
    margin = jnp.zeros(part.shape[:2] + (breadth - part.shape[2],), jnp.float32)
    return pltpu.roll(jnp.concatenate([part, margin], axis=2), onward, 2)


def add_placed(places, slot, part, totals, plane):
    breadth = totals.shape[-1]
    tile, back, shift = (places[slot, n] for n in range(3))
    onward = lax.rem(breadth - back, breadth)
    wide = broaden(lower(part, shift), onward, breadth)
    totals[plane, pl.ds(tile, wide.shape[0])] += wide


def lighting_of(probes):
    length = probes.shape[-1]
    lighting = jnp.zeros((length, length), jnp.float32)
    for mode in range(probes.shape[1]):
        lighting += probes[0, mode] * probes[0, mode] + probes[1, mode] * probes[1, mode]
    return lighting


def forward_slots(places, live, object_map, probes, intensity, turns, window, far, power):
    modes, length = (probes.shape[1], probes.shape[-1])
    slots = intensity.shape[0]
    coverage = jnp.zeros((length, length), jnp.float32)
    for slot in range(slots):
        for plane in range(2):
            part = cut_window(places, slot, object_map, plane, length)
            window[slot, plane] = part.reshape(length, length)
        lit = window[slot, 0] * window[slot, 0] + window[slot, 1] * window[slot, 1]
        coverage += jnp.where(slot < live, lit, 0.0)
    for pair in range(modes // 2):
        for slot in range(slots):
            waves = []
            for mode in (2 * pair, 2 * pair + 1):
                probe_r, probe_i = (probes[0, mode], probes[1, mode])
                obj_r, obj_i = (window[slot, 0], window[slot, 1])
                wave_r = probe_r * obj_r - probe_i * obj_i
                wave_i = probe_r * obj_i + probe_i * obj_r
                waves.append(jnp.concatenate([wave_r, wave_i], axis=1))
            half = regroup(along_lanes(jnp.concatenate(waves, axis=0), turns[0]), length)
            spread = along_rows(half, turns[0])
            far[slot, pair] = spread
            square = spread * spread
            square = square[:, :length] + square[:, length:]
            square = square[:length] + square[length:]
            if pair == 0:
                power[slot] = square
            else:
                power[slot] += square
    for slot in range(slots):
        ratio = jnp.sqrt(intensity[slot].T / jnp.maximum(power[slot], 1.0)) - 1.0
        power[slot] = jnp.where(slot < live, ratio, 0.0)
    return coverage


def backward_slot(slot, pair, probes_of, turns, window, far, power, terms):
    length = power.shape[-1]
    factor = power[slot]
    factor = jnp.concatenate([factor, factor], axis=1)
    factor = jnp.concatenate([factor, factor], axis=0)
    half = regroup(along_lanes(far[slot, pair] * factor, turns[1]), length)
    change = along_rows(half, turns[1])
    obj_r, obj_i = (window[slot, 0], window[slot, 1])
    terms_r = jnp.zeros((length, length), jnp.float32)
    terms_i = jnp.zeros((length, length), jnp.float32)
    moved_r, moved_i = ([], [])
    for which in range(2):
        rows = slice(which * length, (which + 1) * length)
        change_r, change_i = (change[rows, :length], change[rows, length:])
        probe_r, probe_i = probes_of(2 * pair + which)
        terms_r += probe_r * change_r + probe_i * change_i
        terms_i += probe_r * change_i - probe_i * change_r
        moved_r.append(obj_r * change_r + obj_i * change_i)
        moved_i.append(obj_r * change_i - obj_i * change_r)
    if pair == 0:
        terms[slot, 0] = terms_r
        terms[slot, 1] = terms_i
    else:
        terms[slot, 0] += terms_r
        terms[slot, 1] += terms_i
    return moved_r, moved_i


def slots_kernel(
    places, counts, object_map, probes, intensity, turns, totals, sums, window, far, power, terms
):
    modes, length = (probes.shape[1], probes.shape[-1])
    tall = length // 8
    live = counts[0]
    totals[...] = jnp.zeros_like(totals)
    terms[0, 2] = lighting_of(probes)
    sums[2 * modes] = forward_slots(
        places, live, object_map, probes, intensity, turns, window, far, power
    )
    for pair in range(modes // 2):
        for slot in range(intensity.shape[0]):
            moved_r, moved_i = backward_slot(
                slot, pair, lambda k: (probes[0, k], probes[1, k]), turns, window, far, power, terms
            )
            for which in range(2):
                mode = 2 * pair + which
                if slot == 0:
                    sums[mode] = moved_r[which]
                    sums[modes + mode] = moved_i[which]
                else:
                    sums[mode] += moved_r[which]
                    sums[modes + mode] += moved_i[which]

    def place_slot(slot, carry):
        for plane in range(3):
            part = terms[slot, plane] if plane < 2 else terms[0, 2]
            add_placed(places, slot, part.reshape(tall, 8, length), totals, plane)
        return carry

    lax.fori_loop(0, live, place_slot, 0)


def accumulate(object_map, probes, places, counts, intensity, turns):
    _, modes, length, _ = probes.shape
    slots = intensity.shape[0]
    return pl.pallas_call(
        slots_kernel,
        out_shape=(
            jax.ShapeDtypeStruct((3,) + object_map.shape[1:], jnp.float32),
            jax.ShapeDtypeStruct((2 * modes + 1, length, length), jnp.float32),
        ),
        in_specs=[scalars, scalars] + [memory] * 4,
        out_specs=(memory, memory),
        scratch_shapes=[
            pltpu.VMEM((slots, 2, length, length), jnp.float32),
            pltpu.VMEM((slots, modes // 2, 2 * length, 2 * length), jnp.float32),
            pltpu.VMEM((slots, length, length), jnp.float32),
            pltpu.VMEM((slots, 3, length, length), jnp.float32),
        ],
        compiler_params=pltpu.CompilerParams(vmem_limit_bytes=36 * 1024 * 1024),
        name="slots",
    )(places, counts, object_map, probes, intensity, turns)


def outward_kernel(
    places, counts, object_map, probes, intensity, turns, window, far, power, coverage, lit, light
):
    length = probes.shape[-1]
    live = counts[0]
    lit[...] = jnp.zeros_like(lit)
    light[...] = lighting_of(probes).reshape(light.shape)
    coverage[...] = forward_slots(
        places, live, object_map, probes, intensity, turns, window, far, power
    )

    def place_slot(slot, carry):
        add_placed(places, slot, light[...], lit, 0)
        return carry

    lax.fori_loop(0, live, place_slot, 0)


def outward(object_map, probes, places, counts, intensity, turns):
    _, modes, length, _ = probes.shape
    slots = intensity.shape[0]
    shapes = (
        (slots, 2, length, length),
        (slots, modes // 2, 2 * length, 2 * length),
        (slots, length, length),
        (length, length),
        (1,) + object_map.shape[1:],
    )
    return pl.pallas_call(
        outward_kernel,
        out_shape=tuple(jax.ShapeDtypeStruct(shape, jnp.float32) for shape in shapes),
        in_specs=[scalars, scalars] + [memory] * 4,
        out_specs=(memory,) * 5,
        scratch_shapes=[pltpu.VMEM((length // 8, 8, length), jnp.float32)],
        compiler_params=pltpu.CompilerParams(vmem_limit_bytes=20 * 1024 * 1024),
        name="outward",
    )(places, counts, object_map, probes, intensity, turns)


def window_places(starts, rows, lanes, length, lead):
    rows_at = jnp.clip(starts[:, 0], 0, rows - length)
    cols_at = jnp.clip(starts[:, 1], 0, lanes - length)
    tile = jnp.minimum(rows_at // 8, (rows - length) // 8 - 1)
    shift = rows_at - 8 * tile
    back = (lanes + lead - cols_at) % lanes
    return jnp.stack([tile, back, shift, (8 - shift) % 8], axis=1)


def mixing(probes, probe_step):
    mix_r = jnp.sum(probes[0] * probe_step[0] + probes[1] * probe_step[1], axis=0)
    mix_i = jnp.sum(probes[0] * probe_step[1] - probes[1] * probe_step[0], axis=0)
    return (mix_r, mix_i)


def cross_term(object_map, change, starts, active, mix_r, mix_i):
    length = mix_r.shape[-1]
    anchor_index = jnp.int32(0)

    def cross_visit_slot(running, element):
        corner_at, weight = element
        corner = (anchor_index, corner_at[0], corner_at[1])
        object_win = lax.dynamic_slice(object_map, corner, (2, length, length))
        change_win = lax.dynamic_slice(change, corner, (2, length, length))
        aligned = change_win[0] * object_win[0] + change_win[1] * object_win[1]
        rotated = change_win[0] * object_win[1] - change_win[1] * object_win[0]
        return (running + weight * jnp.sum(aligned * mix_r - rotated * mix_i), None)

    running, _ = lax.scan(cross_visit_slot, jnp.zeros((), jnp.float32), (starts, active))
    return running


def solve_steps(object_curve, cross_curve, probe_curve, object_slope, probe_slope):
    object_diag = 1.1 * object_curve + 0.001
    probe_diag = 1.1 * probe_curve + 0.001
    determinant = object_diag * probe_diag - cross_curve * cross_curve
    object_rate = (probe_diag * object_slope - cross_curve * probe_slope) / determinant
    probe_rate = (object_diag * probe_slope - cross_curve * object_slope) / determinant
    return (object_rate, probe_rate)


def widen(planes, margin):
    return with_halo(planes, (("tx", 1), ("ty", 2)), margin)


def fold_rims(totals, margin, height, breadth):
    middle = totals[:, margin : margin + height, :]
    for direction in (1, -1):
        border = totals[:, margin + height :, :] if direction == 1 else totals[:, :margin, :]
        arrived = from_behind(border, "tx", direction)
        if direction == 1:
            middle = jnp.concatenate([middle + arrived, middle[:, margin:, :]], axis=1)
        else:
            middle = jnp.concatenate([middle[:, : height - margin, :], middle + arrived], axis=1)
    interior = middle[:, :, margin : margin + breadth]
    for direction in (1, -1):
        border = middle[:, :, margin + breadth :] if direction == 1 else middle[:, :, :margin]
        arrived = from_behind(border, "ty", direction)
        if direction == 1:
            interior = jnp.concatenate(
                [interior[:, :, :margin] + arrived, interior[:, :, margin:]], axis=2
            )
        else:
            interior = jnp.concatenate(
                [interior[:, :, : breadth - margin], interior[:, :, breadth - margin :] + arrived],
                axis=2,
            )
    return interior


def general(object_field, probe_modes, positions, counts, intensity):
    length = probe_modes.shape[-1]
    margin = length // 2
    height = object_field.shape[1]
    breadth = object_field.shape[2]
    turns = split_tables(length)
    modes = probe_modes.shape[1]
    anchor = jnp.stack(
        [lax.axis_index("tx") * height - margin, lax.axis_index("ty") * breadth - margin]
    )
    starts = positions - anchor[None, :]
    active = (jnp.arange(positions.shape[0], dtype=jnp.int32) < counts[0]).astype(jnp.float32)
    places = window_places(starts, height + 2 * margin, breadth + 2 * margin, length, 0)
    object_map = object_field
    probes = probe_modes
    extended = widen(object_map, margin)
    for repeat in range(ITERS):
        tiled = extended.reshape(2, -1, 8, extended.shape[-1])
        totals, sums = accumulate(tiled, probes, places, counts, intensity, turns)
        totals = totals.reshape((3,) + extended.shape[1:])
        interior = fold_rims(totals, margin, height, breadth)
        change = interior[:2] / jnp.maximum(interior[2], 1.0)
        object_part = jnp.sum((change[0] * change[0] + change[1] * change[1]) * interior[2])
        slope_part = jnp.sum(interior[:2] * change)
        wide_change = widen(change, margin)
        sums = lax.psum(sums, ("tx", "ty"))
        probe_total = sums[: 2 * modes].reshape(probes.shape)
        weight_total = sums[2 * modes]
        probe_step = probe_total / (weight_total + 1e-05)
        mix_r, mix_i = mixing(probes, probe_step)
        cross_part = cross_term(extended, wide_change, starts, active, mix_r, mix_i)
        object_curve, cross_curve, object_slope = lax.psum(
            (object_part, cross_part, slope_part), ("tx", "ty")
        )
        probe_curve = jnp.sum(
            (probe_step[0] * probe_step[0] + probe_step[1] * probe_step[1]) * weight_total
        )
        probe_slope = jnp.sum(probe_total * probe_step)
        object_rate, probe_rate = solve_steps(
            object_curve, cross_curve, probe_curve, object_slope, probe_slope
        )
        object_map = object_map + object_rate * change
        probes = probes + probe_rate * probe_step
        if repeat + 1 < ITERS:
            extended = extended + object_rate * wide_change
    return (object_map, probes)

outside = pl.BlockSpec(memory_space=pltpu.HBM)
OTHERS = [(i, j) for i in range(4) for j in range(4) if i or j]
AROUND = [(i, j) for i in (-1, 0, 1) for j in (-1, 0, 1) if i or j]
SIDES = [(i, j) for i in (-1, 0, 1) for j in (-1, 1)]


def everyone(row, col):
    return [{"tx": (row + i) % 4, "ty": (col + j) % 4} for i, j in OTHERS]


def greet(peers):
    barrier = pltpu.get_barrier_semaphore()
    for peer in peers:
        pl.semaphore_signal(barrier, 1, device_id=peer, device_id_type=pl.DeviceIdType.MESH)
    pl.semaphore_wait(barrier, len(peers))


class Copies:
    def __init__(self, send, arrive):
        self.send, self.arrive, self.count = (send, arrive, 0)
        self.unsent = []

    def slots(self, number):
        self.count += number
        return self.count - number

    def make(self, source, target, index, landing, peer):
        return pltpu.make_async_remote_copy(
            src_ref=source,
            dst_ref=target,
            send_sem=self.send.at[index],
            recv_sem=self.arrive.at[landing],
            device_id=peer,
            device_id_type=pl.DeviceIdType.MESH,
        )

    def start(self, source, target, peer):
        index = self.slots(1)
        copy = self.make(source, target, index, index, peer)
        copy.start()
        self.unsent.append(copy)
        return copy

    def group(self, items, view):
        index = self.slots(1)
        for source, target, peer in items:
            self.make(source, target, index, index, peer).start()
        whole = self.make(view, view, index, index, items[0][2])
        self.unsent.append(whole)
        return whole

    def finish(self):
        for copy in self.unsent:
            copy.wait_send()
        self.unsent = []


class Ring:
    def __init__(self, copies, row, col, source, target):
        self.copies, self.row, self.col = (copies, row, col)
        self.source, self.target = (source, target)
        self.base = copies.slots(len(AROUND))

    def each(self, what):
        for k, (i, j) in enumerate(AROUND):
            row, col = (self.row + i, self.col + j)
            inside = (row >= 0) & (row < 4) & (col >= 0) & (col < 4)
            pl.when(inside)(functools.partial(what, k, i, j, {"tx": row, "ty": col}))

    def outgoing(self, k, i, j, peer):
        landing = AROUND.index((-i, -j))
        return self.copies.make(
            self.source(i, j), self.target(-i, -j), self.base + k, self.base + landing, peer
        )

    def blank(self):
        for i, j in AROUND:
            row, col = (self.row + i, self.col + j)
            inside = (row >= 0) & (row < 4) & (col >= 0) & (col < 4)
            target = self.target(i, j)

            @pl.when(jnp.logical_not(inside))
            def _():
                target[...] = jnp.zeros(target.shape, jnp.float32)

    def start(self):
        self.each(lambda k, i, j, peer: self.outgoing(k, i, j, peer).start())

    def receive(self):
        def arrived(k, i, j, peer):
            index = self.base + k
            self.copies.make(self.source(i, j), self.target(i, j), index, index, peer).wait_recv()

        self.each(arrived)

    def finish(self):
        self.each(lambda k, i, j, peer: self.outgoing(k, i, j, peer).wait_send())


class Edges:
    def __init__(self, copies, row, col, axis, source, target):
        self.copies, self.axis = (copies, axis)
        self.source, self.target = (source, target)
        self.place = {"tx": row, "ty": col}
        self.base = copies.slots(2)

    def each(self, what, missing=False):
        for k, ahead in ((0, -1), (1, 1)):
            there = self.place[self.axis] + ahead
            inside = (there >= 0) & (there < 4)
            inside = jnp.logical_not(inside) if missing else inside
            peer = {**self.place, self.axis: there}
            pl.when(inside)(functools.partial(what, k, peer))

    def blank(self):
        def clear(k, peer):
            target = self.target(k)
            target[...] = jnp.zeros(target.shape, jnp.float32)

        self.each(clear, missing=True)

    def outgoing(self, k, peer):
        landing = 1 - k
        return self.copies.make(
            self.source(k), self.target(landing), self.base + k, self.base + landing, peer
        )

    def start(self):
        self.each(lambda k, peer: self.outgoing(k, peer).start())

    def receive(self):
        def arrived(k, peer):
            index = self.base + k
            self.copies.make(self.source(k), self.target(k), index, index, peer).wait_recv()

        self.each(arrived)

    def finish(self):
        self.each(lambda k, peer: self.outgoing(k, peer).wait_send())


def early_lanes(value):
    return lax.broadcasted_iota(jnp.int32, value.shape, value.ndim - 1) < value.shape[-1] // 2


def turned(value):
    return pltpu.roll(value, value.shape[-1] // 2, value.ndim - 1)


def pack_first(block):
    half = block.shape[1] // 2
    top, bottom = (block[:, :half], block[:, half:])
    return jnp.where(early_lanes(top), top, turned(bottom))


def pack_last(block):
    half = block.shape[1] // 2
    top, bottom = (block[:, :half], block[:, half:])
    return jnp.where(early_lanes(top), turned(top), bottom)


def unpack(first, last):
    early = early_lanes(first)
    top = jnp.where(early, first, turned(last))
    bottom = jnp.where(early, turned(first), last)
    return jnp.concatenate([top, bottom], axis=1)


def row_range(i, high):
    return slice((i + 1) * high, (i + 2) * high)


def halo_ring(copies, row, col, own, packed, above, beside):
    def source(i, j):
        return own if j == 0 else packed.at[(j + 1) // 2]

    def target(i, j):
        return above.at[(i + 1) // 2] if j == 0 else beside.at[SIDES.index((i, j))]

    return Ring(copies, row, col, source, target)


def spread_halo(own, above, beside, wide):
    high, broad = (own.shape[1], own.shape[-1])
    for i in (-1, 0, 1):
        rows = row_range(i, high)
        wide[:, rows, :, :broad] = own if i == 0 else above[(i + 1) // 2]
        wide[:, rows, :, broad:] = unpack(
            beside[SIDES.index((i, 1))], beside[SIDES.index((i, -1))]
        )


def widen_kernel(
    own_at, probes_at, turns_at, intensity_at, wide, probes, turns, intensity, own, whole, packed, above,
    beside, local, send, arrive,
):
    row, col = (lax.axis_index("tx"), lax.axis_index("ty"))
    fetches = [
        pltpu.make_async_copy(source, target, local.at[k])
        for k, (source, target) in enumerate(
            ((own_at, own), (probes_at, probes), (turns_at, turns), (intensity_at, intensity))
        )
    ]
    for fetch in fetches:
        fetch.start()
    copies = Copies(send, arrive)
    ring = halo_ring(copies, row, col, whole, packed, above, beside)
    ring.blank()
    fetches[0].wait()
    block = own[...].reshape(2, own.shape[1] // 8, 8, own.shape[2])
    whole[...] = block
    packed[0] = pack_first(block)
    packed[1] = pack_last(block)
    greet(everyone(row, col))
    ring.start()
    for fetch in fetches[1:]:
        fetch.wait()
    ring.receive()
    spread_halo(block, above, beside, wide)
    ring.finish()


def halo_scratch(high, broad):
    return [
        pltpu.VMEM((2, 2, high // 2, 8, broad), jnp.float32),
        pltpu.VMEM((2, 2, high, 8, broad), jnp.float32),
        pltpu.VMEM((6, 2, high // 2, 8, broad), jnp.float32),
    ]


def widen_tiles(own, probes, turns, intensity):
    two, height, broad = own.shape
    high = height // 8

    def like(value):
        return jax.ShapeDtypeStruct(value.shape, value.dtype)

    return pl.pallas_call(
        widen_kernel,
        out_shape=(
            jax.ShapeDtypeStruct((two, 3 * high, 8, 2 * broad), jnp.float32),
            like(probes),
            like(turns),
            like(intensity),
        ),
        in_specs=[outside] * 4,
        out_specs=(memory,) * 4,
        scratch_shapes=[
            pltpu.VMEM(own.shape, jnp.float32),
            pltpu.VMEM((two, high, 8, broad), jnp.float32),
        ]
        + halo_scratch(high, broad)
        + [
            pltpu.SemaphoreType.DMA((4,)),
            pltpu.SemaphoreType.DMA((8,)),
            pltpu.SemaphoreType.DMA((8,)),
        ],
        compiler_params=pltpu.CompilerParams(
            collective_id=0, has_side_effects=True, vmem_limit_bytes=51300 * 1024
        ),
        name="widen",
    )(own, probes, turns, intensity)


def in_rows(values, lanes):
    at = lax.broadcasted_iota(jnp.int32, (8, lanes), 0)
    result = jnp.zeros((8, lanes), jnp.float32)
    for place, value in enumerate(values):
        result = jnp.where(at == place, value, result)
    return result


def settle_kernel(
    last, places, weights, object_map, probes, turns, window, far, power, coverage, lit, *rest
):
    if last:
        got, change_own, rates_out = rest[:3]
    else:
        new_map, new_probes, got = rest[:3]
    (
        sums, terms, padded, totals, fold_out, fold_in, upright, over, column, near_out, near, r1,
        acc, r2, acca, r3, accb, r4, wide, held, mix, mine, pair_in, ours, inbox, send, arrive,
    ) = rest[3:]
    row, col = (lax.axis_index("tx"), lax.axis_index("ty"))
    core, side, upper, lower_bit = (col % 2, col // 2, row // 2, row % 2)
    rows, broad = (column.shape[1], column.shape[-1])
    high = rows // 3
    tall, length = (2 * high, power.shape[-1])
    slots = places.shape[0]
    modes = probes.shape[1]
    pairs = modes // 2
    blocks = got.shape[1:]
    middle = slice(high, 2 * high)
    ends = (slice(0, high), slice(2 * high, 3 * high))
    peers = everyone(row, col)
    partner = {"tx": row, "ty": side * 2 + (1 - core)}
    across = {"tx": row, "ty": (1 - side) * 2 + core}
    beside = {"tx": row + 1 - 2 * lower_bit, "ty": col}
    beyond = {"tx": (row + 2) % 4, "ty": col}
    chips = [
        {"tx": (row + i) % 4, "ty": ((side + j) % 2) * 2 + core}
        for i in range(4)
        for j in range(2)
        if i or j
    ]
    copies = Copies(send, arrive)
    spot = (core, side, upper, lower_bit)

    barrier = pltpu.get_barrier_semaphore()
    for peer in peers:
        pl.semaphore_signal(barrier, 1, device_id=peer, device_id_type=pl.DeviceIdType.MESH)

    def edges(axis, source, target):
        made = Edges(copies, row, col, axis, source, target)
        made.blank()
        return made

    fold_side = edges("ty", lambda k: fold_out.at[k], lambda k: fold_in.at[k])
    fold_over = edges("tx", lambda k: upright.at[:, ends[k]], lambda k: over.at[k])
    halo_over = edges("tx", lambda k: column.at[:, middle], lambda k: column.at[:, ends[k]])
    halo_side = edges("ty", lambda k: near_out.at[k], lambda k: near.at[k])
    padded[...] = jnp.zeros_like(padded)
    totals[:2] = jnp.zeros((2,) + totals.shape[1:], jnp.float32)
    totals[2] = lit[0]

    def probes_of(mode):
        return tuple(probes[part, mode].reshape(length, length) for part in range(2))

    def compute(pair):
        base = 1 + 4 * pair
        for slot in range(slots):
            moved_r, moved_i = backward_slot(
                slot, pair, probes_of, turns, window, far, power, terms
            )
            for n, value in enumerate(moved_r + moved_i):
                value = value.reshape(blocks)
                if slot == 0:
                    sums[base + n] = value
                else:
                    sums[base + n] += value

    def chunk(n):
        return slice(1 + 4 * n if n else 0, 5 + 4 * n)

    def planes(n):
        return slice(4 * n, 4 * n + 4)

    shared = {}
    moving = {}

    def core_sum(n):
        part = chunk(n)
        moving[n] = copies.start(sums.at[part, 1 - core], r1.at[part], partner)

    def across_sum(n):
        part = chunk(n)
        moving[n].wait_recv()
        acc[part] = sums[part, core] + r1[part]
        moving[n] = copies.start(acc.at[part, 1 - side], r2.at[part], across)

    def beside_sum(n):
        part = chunk(n)
        moving[n].wait_recv()
        acca[part] = acc[part, side] + r2[part]
        moving[n] = copies.start(acca.at[part, :, 1 - lower_bit], r3.at[part], beside)

    def beyond_sum(n):
        part = chunk(n)
        moving[n].wait_recv()
        accb[part] = acca[part, :, lower_bit] + r3[part]
        moving[n] = copies.start(accb.at[part, 1 - upper], r4.at[part], beyond)

    def give(n, block, peer):
        moving[n] = copies.start(block, block, peer)

    def slab(n):
        part = chunk(n)
        moving[n].wait_recv()
        total = accb[part, upper] + r4[part]
        if n == 0:
            shared["weight"] = total[0]
            total = total[1:]
        weight = shared["weight"]
        found = total / (weight + 1e-05)
        got[(planes(n),) + spot] = found
        give(n, got.at[(planes(n),) + spot], beyond)
        some = slice(2 * n, 2 * n + 2)
        probe_r, probe_i = (probes[(0, some) + spot], probes[(1, some) + spot])
        for name, value in (
            ("mix_r", probe_r * found[:2] + probe_i * found[2:]),
            ("mix_i", probe_r * found[2:] - probe_i * found[:2]),
            ("curve", found * found * weight),
            ("slope", total * found),
        ):
            value = jnp.sum(value, axis=0)
            shared[name] = value if n == 0 else shared[name] + value

    def beside_give(n):
        moving[n].wait_recv()
        give(n, got.at[planes(n), core, side, :, lower_bit], beside)

    def across_give(n):
        moving[n].wait_recv()
        give(n, got.at[planes(n), core, side], across)

    def core_give(n):
        moving[n].wait_recv()
        give(n, got.at[planes(n), core], partner)

    sums[0] = coverage[...].reshape(blocks)
    compute(0)
    pl.semaphore_wait(barrier, len(peers))
    core_sum(0)
    compute(1)
    core_sum(1)
    across_sum(0)
    compute(2)
    core_sum(2)
    across_sum(1)
    compute(3)
    core_sum(3)
    across_sum(2)
    beside_sum(0)

    for slot in range(slots):
        tile, back, shift = (places[slot, n] for n in range(3))
        onward = lax.rem(2 * broad - back, 2 * broad)
        for plane in range(2):
            keep = padded.at[slot % 2, plane]
            keep[high : high + tall + 1] = lower(terms[slot, plane].reshape(tall, 8, length), shift)
            part = padded[slot % 2, plane, pl.ds(high - tile, 3 * high)]
            totals[plane] += broaden(part, onward, 2 * broad)
    rim = totals[:, :, :, broad:]
    fold_out[0] = pack_last(rim)
    fold_out[1] = pack_first(rim)
    fold_side.start()
    across_sum(3)
    beside_sum(1)
    beyond_sum(0)
    beside_sum(2)

    fold_side.receive()
    upright[...] = totals[:, :, :, :broad] + unpack(fold_in[0], fold_in[1])
    fold_over.start()
    beyond_sum(1)
    beside_sum(3)
    slab(0)
    beyond_sum(2)
    slab(1)
    beyond_sum(3)

    fold_over.receive()
    interior = upright[:, middle] + over[0] + over[1]
    moved = interior[:2] / jnp.maximum(interior[2], 1.0)
    column[:, middle] = moved
    halo_over.start()
    beside_give(0)
    slab(2)
    slab(3)
    mix[(0,) + spot] = shared["mix_r"]
    mix[(1,) + spot] = shared["mix_i"]
    block = mix.at[(slice(None),) + spot]
    mixes = [copies.start(block, block, peer) for peer in chips]
    beside_give(1)
    curve = jnp.sum((moved[0] * moved[0] + moved[1] * moved[1]) * interior[2])
    slope = jnp.sum(interior[:2] * moved)
    probe_curve = jnp.sum(shared["curve"])
    probe_slope = jnp.sum(shared["slope"])

    halo_over.receive()
    near_out[0] = pack_first(column[...])
    near_out[1] = pack_last(column[...])
    halo_side.start()
    across_give(0)
    beside_give(2)
    across_give(1)
    beside_give(3)
    wide[:, :, :, :broad] = column[...]

    halo_side.receive()
    wide[:, :, :, broad:] = unpack(near[1], near[0])
    held[0] = wide[0] * object_map[0] + wide[1] * object_map[1]
    held[1] = wide[0] * object_map[1] - wide[1] * object_map[0]
    gathered = []
    for plane in range(2):
        running = jnp.zeros((tall, 8, broad), jnp.float32)
        for slot in range(slots):
            running += weights[slot] * cut_window(places, slot, held, plane, length)
        gathered.append(running)
    for copy in mixes:
        copy.wait_recv()
    block = mix.at[:, core]
    mix_pass = copies.start(block, block, partner)
    core_give(0)
    across_give(2)
    across_give(3)
    mix_pass.wait_recv()
    mix_all = mix[...].reshape(2, tall, 8, broad)
    cross = jnp.sum(gathered[0] * mix_all[0] - gathered[1] * mix_all[1])
    mine[...] = in_rows((curve, slope, probe_curve, probe_slope, cross), broad)
    pair_sent = copies.start(mine, pair_in, partner)
    core_give(1)
    pair_sent.wait_recv()
    ours[...] = mine[...] + pair_in[...]
    scalars_sent = copies.group([(ours, inbox.at[k], peer) for k, peer in enumerate(chips)], inbox)
    core_give(2)
    core_give(3)
    copies.finish()
    for made in (fold_side, fold_over, halo_over, halo_side):
        made.finish()
    for n in range(pairs):
        moving[n].wait_recv()
    scalars_sent.wait_recv()
    sent = ours[...] + jnp.sum(inbox[...], axis=0)
    object_rate, probe_rate = solve_steps(
        sent[0:1], sent[4:5], sent[2:3], sent[1:2], sent[3:4]
    )
    object_rate = jnp.broadcast_to(object_rate, (8, broad))
    probe_rate = jnp.broadcast_to(probe_rate, (8, broad))
    if last:
        at = lax.broadcasted_iota(jnp.int32, (8, broad), 0)
        rates_out[...] = jnp.where(at == 0, object_rate, probe_rate)
        change_own[...] = column[:, middle]
    else:
        both = jnp.concatenate([object_rate, object_rate], axis=1)
        new_map[...] = object_map[...] + both * wide[...]
        for n in range(pairs):
            some = slice(2 * n, 2 * n + 2)
            for part in range(2):
                first = 4 * n + 2 * part
                new_probes[part, some] = probes[part, some] + probe_rate * got[first : first + 2]


def settle(last, places, weights, object_map, probes, turns, spread):
    _, rows, _, lanes = object_map.shape
    modes, length = (probes.shape[1], probes.shape[-1])
    slots = places.shape[0]
    planes = 2 * modes
    high, broad = (rows // 3, lanes // 2)
    f32 = jnp.float32
    grid = (2, 2, 2, 2)
    step = jax.ShapeDtypeStruct((planes,) + grid + (8, length), f32)
    if last:
        out_shape = (
            step,
            jax.ShapeDtypeStruct((2, high, 8, broad), f32),
            jax.ShapeDtypeStruct((8, broad), f32),
        )
    else:
        out_shape = (
            jax.ShapeDtypeStruct(object_map.shape, f32),
            jax.ShapeDtypeStruct((2, modes) + grid + (8, length), f32),
            step,
        )
    scratch = [
        (planes + 1,) + grid + (8, length),
        (slots, 2, length, length),
        (2, 2, 4 * high + 1, 8, length),
        (3, rows, 8, lanes),
        (2, 3, rows // 2, 8, broad),
        (2, 3, rows // 2, 8, broad),
        (3, rows, 8, broad),
        (2, 3, high, 8, broad),
        (2, rows, 8, broad),
        (2, 2, rows // 2, 8, broad),
        (2, 2, rows // 2, 8, broad),
        (planes + 1, 2, 2, 2, 8, length),
        (planes + 1, 2, 2, 2, 8, length),
        (planes + 1, 2, 2, 8, length),
        (planes + 1, 2, 2, 8, length),
        (planes + 1, 2, 8, length),
        (planes + 1, 2, 8, length),
        (planes + 1, 8, length),
        (2, rows, 8, lanes),
        (2, rows, 8, lanes),
        (2,) + grid + (8, length),
        (8, broad),
        (8, broad),
        (8, broad),
        (7, 8, broad),
    ]
    return pl.pallas_call(
        functools.partial(settle_kernel, last),
        out_shape=out_shape,
        in_specs=[scalars, scalars] + [memory] * 8,
        out_specs=(memory,) * 3,
        scratch_shapes=[pltpu.VMEM(shape, f32) for shape in scratch]
        + [pltpu.SemaphoreType.DMA((52,)), pltpu.SemaphoreType.DMA((52,))],
        compiler_params=pltpu.CompilerParams(
            collective_id=2 if last else 1,
            has_side_effects=True,
            vmem_limit_bytes=28 * 1024 * 1024,
        ),
        name="finish" if last else "settle",
    )(
        places,
        weights,
        object_map,
        probes.reshape((2, modes) + grid + (8, length)),
        turns,
        *spread,
    )


def apply_kernel(object_map, change, probes, step, rates, object_at, probes_at, tile, fresh, done):
    modes = probes.shape[1]
    high, broad = (change.shape[1], change.shape[3])
    object_rate = jnp.broadcast_to(rates[0:1], (8, broad))
    probe_rate = jnp.broadcast_to(rates[1:2], (8, broad))
    copies = []
    for part in range(2):
        for first in range(0, modes, 4):
            some = slice(first, first + 4)
            base = 2 * (first + part)
            stepped = jnp.concatenate(
                [step[base : base + 2], step[base + 4 : base + 6]], axis=0
            )
            moved = probes[part, some] + probe_rate * stepped
            fresh[part, some] = moved.reshape((4,) + fresh.shape[2:])
            block = (part, pl.ds(first, 4))
            copies.append(
                pltpu.make_async_copy(fresh.at[block], probes_at.at[block], done.at[len(copies)])
            )
            copies[-1].start()
    moved = object_map[:, high : 2 * high, :, :broad] + object_rate * change[...]
    tile[...] = moved.reshape(tile.shape)
    copies.append(pltpu.make_async_copy(tile, object_at, done.at[len(copies)]))
    copies[-1].start()
    for copy in copies:
        copy.wait()


def apply(object_map, change, probes, step, rates):
    _, high, _, broad = change.shape
    modes, length = (probes.shape[1], probes.shape[-1])
    shapes = ((2, 8 * high, broad), (2, modes, length, length))
    blocks = (2, modes, length // 8, 8, length)
    return pl.pallas_call(
        apply_kernel,
        out_shape=tuple(jax.ShapeDtypeStruct(shape, jnp.float32) for shape in shapes),
        in_specs=[memory] * 5,
        out_specs=(outside,) * 2,
        scratch_shapes=[pltpu.VMEM(shape, jnp.float32) for shape in shapes]
        + [pltpu.SemaphoreType.DMA((modes // 2 + 1,))],
        compiler_params=pltpu.CompilerParams(vmem_limit_bytes=8 * 1024 * 1024),
        name="apply",
    )(
        object_map,
        change,
        probes.reshape(blocks),
        step.reshape((2 * modes,) + blocks[2:]),
        rates,
    )


def direct(object_field, probe_modes, positions, counts, intensity):
    two, modes, length, _ = probe_modes.shape
    margin = length // 2
    _, height, breadth = object_field.shape
    anchor = jnp.stack(
        [lax.axis_index("tx") * height - margin, lax.axis_index("ty") * breadth - margin]
    )
    starts = positions - anchor[None, :]
    lanes = 2 * breadth
    places = window_places(starts, height + 2 * margin, lanes, length, margin)
    weights = (jnp.arange(positions.shape[0], dtype=jnp.int32) < counts[0]).astype(jnp.float32)
    object_map, probes, turns, measured = widen_tiles(
        object_field,
        probe_modes,
        jnp.asarray(split_tables(length)),
        intensity,
    )
    for repeat in range(ITERS):
        spread = outward(object_map, probes, places, counts, measured, turns)
        last = repeat + 1 == ITERS
        settled = settle(last, places, weights, object_map, probes, turns, spread)
        if not last:
            object_map, probes, _ = settled
            probes = probes.reshape(probe_modes.shape)
    step, change, rates = settled
    return apply(object_map, change, probes, step, rates)


def shards(object_field, probe_modes, positions, counts, intensity):
    _, height, breadth = object_field.shape
    length = probe_modes.shape[-1]
    grid = (lax.axis_size("tx"), lax.axis_size("ty"))
    arguments = (object_field, probe_modes, positions, counts, intensity)
    if grid == (4, 4) and length == 128 and (2 * height, breadth) == (length, length):
        return direct(*arguments)
    return general(*arguments)


def solution(mesh):
    return jax.shard_map(
        shards,
        mesh=mesh,
        in_specs=(
            P("groups", "tx", "ty"),
            P("groups", None, None, None),
            P(("groups", "tx", "ty"), None),
            P(("groups", "tx", "ty")),
            P(("groups", "tx", "ty"), None, None),
        ),
        out_specs=(P("groups", "tx", "ty"), P("groups", None, None, None)),
        check_vma=False,
    )
```

```python
import functools

import jax
import jax.numpy as jnp
import ml_dtypes
import numpy as np
from jax import lax
from jax.experimental import pallas as pl
from jax.experimental.pallas import tpu as pltpu
from jax.sharding import PartitionSpec as P

ITERS = 2
memory = pl.BlockSpec(memory_space=pltpu.VMEM)
scalars = pl.BlockSpec(memory_space=pltpu.SMEM)


def with_halo(value, sides, width):
    for axis, dim in sides:
        size, length = (lax.axis_size(axis), value.shape[dim])
        up = [(i, (i + 1) % size) for i in range(size - 1)]
        down = [(j, i) for i, j in up]
        last = lax.slice_in_dim(value, length - width, length, axis=dim)
        first = lax.slice_in_dim(value, 0, width, axis=dim)
        before = lax.ppermute(last, axis, up)
        after = lax.ppermute(first, axis, down)
        value = jnp.concatenate([before, value, after], axis=dim)
    return value


def from_behind(block, axis, distance):
    devices = range(lax.axis_size(axis))
    route = [(i - distance, i) for i in devices if i - distance in devices]
    return lax.ppermute(block, axis, route)


def split_tables(length):
    indices = np.arange(length)
    angles = (indices[:, None] * indices[None, :] % length) * (2.0 * np.pi / length)
    cos_table = np.cos(angles) / np.sqrt(length)
    sin_table = np.sin(angles) / np.sqrt(length)
    forward = np.block([[cos_table, -sin_table], [sin_table, cos_table]])
    inverse = np.block([[cos_table, sin_table], [-sin_table, cos_table]])

    def stacked(table):
        coarse = table.astype(np.float32).astype(ml_dtypes.bfloat16)
        fine = (table - coarse.astype(np.float64)).astype(ml_dtypes.bfloat16)
        return np.concatenate([coarse, coarse, fine], axis=0)

    return np.stack([stacked(forward), stacked(inverse)])


def halves(value, axis):
    coarse = value.astype(jnp.bfloat16)
    fine = (value - coarse.astype(jnp.float32)).astype(jnp.bfloat16)
    return jnp.concatenate([coarse, fine, coarse], axis=axis)


def along_lanes(value, table):
    return jnp.dot(halves(value, 1), table, preferred_element_type=jnp.float32)


def along_rows(value, table):
    dims = (((0,), (0,)), ((), ()))
    return lax.dot_general(halves(value, 0), table, dims, preferred_element_type=jnp.float32)


def regroup(value, length):
    top, bottom = (value[:length], value[length:])
    return jnp.concatenate(
        [
            jnp.concatenate([top[:, :length], bottom[:, :length]], axis=1),
            jnp.concatenate([top[:, length:], bottom[:, length:]], axis=1),
        ],
        axis=0,
    )


def cut_window(places, slot, maps, plane, length):
    tall = length // 8
    tile, back, shift, upward = (places[slot, n] for n in range(4))
    sublane = lax.broadcasted_iota(jnp.int32, (tall, 8, length), 1)
    part = maps[plane, pl.ds(tile, tall + 1)]
    part = pltpu.roll(part, back, 2)[:, :, :length]
    part = pltpu.roll(part, upward, 1)
    return jnp.where(sublane + shift < 8, part[:tall], part[1:])


def lower(part, shift):
    tall, _, length = part.shape
    sublane = lax.broadcasted_iota(jnp.int32, (tall + 1, 8, length), 1)
    blank = jnp.zeros((1, 8, length), jnp.float32)
    part = pltpu.roll(part, lax.rem(shift, 8), 1)
    return jnp.where(
        sublane >= shift,
        jnp.concatenate([part, blank], axis=0),
        jnp.concatenate([blank, part], axis=0),
    )


def broaden(part, onward, breadth):
    margin = jnp.zeros(part.shape[:2] + (breadth - part.shape[2],), jnp.float32)
    return pltpu.roll(jnp.concatenate([part, margin], axis=2), onward, 2)


def add_placed(places, slot, part, totals, plane):
    breadth = totals.shape[-1]
    tile, back, shift = (places[slot, n] for n in range(3))
    onward = lax.rem(breadth - back, breadth)
    wide = broaden(lower(part, shift), onward, breadth)
    totals[plane, pl.ds(tile, wide.shape[0])] += wide


def lighting_of(probes):
    length = probes.shape[-1]
    lighting = jnp.zeros((length, length), jnp.float32)
    for mode in range(probes.shape[1]):
        lighting += probes[0, mode] * probes[0, mode] + probes[1, mode] * probes[1, mode]
    return lighting


def forward_slots(places, live, object_map, probes, intensity, turns, window, far, power):
    modes, length = (probes.shape[1], probes.shape[-1])
    slots = intensity.shape[0]
    coverage = jnp.zeros((length, length), jnp.float32)
    for slot in range(slots):
        for plane in range(2):
            part = cut_window(places, slot, object_map, plane, length)
            window[slot, plane] = part.reshape(length, length)
        lit = window[slot, 0] * window[slot, 0] + window[slot, 1] * window[slot, 1]
        coverage += jnp.where(slot < live, lit, 0.0)
    for pair in range(modes // 2):
        for slot in range(slots):
            waves = []
            for mode in (2 * pair, 2 * pair + 1):
                probe_r, probe_i = (probes[0, mode], probes[1, mode])
                obj_r, obj_i = (window[slot, 0], window[slot, 1])
                wave_r = probe_r * obj_r - probe_i * obj_i
                wave_i = probe_r * obj_i + probe_i * obj_r
                waves.append(jnp.concatenate([wave_r, wave_i], axis=1))
            half = regroup(along_lanes(jnp.concatenate(waves, axis=0), turns[0]), length)
            spread = along_rows(half, turns[0])
            far[slot, pair] = spread
            square = spread * spread
            square = square[:, :length] + square[:, length:]
            square = square[:length] + square[length:]
            if pair == 0:
                power[slot] = square
            else:
                power[slot] += square
    for slot in range(slots):
        ratio = jnp.sqrt(intensity[slot].T / jnp.maximum(power[slot], 1.0)) - 1.0
        power[slot] = jnp.where(slot < live, ratio, 0.0)
    return coverage


def backward_slot(slot, pair, probes_of, turns, window, far, power, terms):
    length = power.shape[-1]
    factor = power[slot]
    factor = jnp.concatenate([factor, factor], axis=1)
    factor = jnp.concatenate([factor, factor], axis=0)
    half = regroup(along_lanes(far[slot, pair] * factor, turns[1]), length)
    change = along_rows(half, turns[1])
    obj_r, obj_i = (window[slot, 0], window[slot, 1])
    terms_r = jnp.zeros((length, length), jnp.float32)
    terms_i = jnp.zeros((length, length), jnp.float32)
    moved_r, moved_i = ([], [])
    for which in range(2):
        rows = slice(which * length, (which + 1) * length)
        change_r, change_i = (change[rows, :length], change[rows, length:])
        probe_r, probe_i = probes_of(2 * pair + which)
        terms_r += probe_r * change_r + probe_i * change_i
        terms_i += probe_r * change_i - probe_i * change_r
        moved_r.append(obj_r * change_r + obj_i * change_i)
        moved_i.append(obj_r * change_i - obj_i * change_r)
    if pair == 0:
        terms[slot, 0] = terms_r
        terms[slot, 1] = terms_i
    else:
        terms[slot, 0] += terms_r
        terms[slot, 1] += terms_i
    return moved_r, moved_i


def slots_kernel(
    places, counts, object_map, probes, intensity, turns, totals, sums, window, far, power, terms
):
    modes, length = (probes.shape[1], probes.shape[-1])
    tall = length // 8
    live = counts[0]
    totals[...] = jnp.zeros_like(totals)
    terms[0, 2] = lighting_of(probes)
    sums[2 * modes] = forward_slots(
        places, live, object_map, probes, intensity, turns, window, far, power
    )
    for pair in range(modes // 2):
        for slot in range(intensity.shape[0]):
            moved_r, moved_i = backward_slot(
                slot, pair, lambda k: (probes[0, k], probes[1, k]), turns, window, far, power, terms
            )
            for which in range(2):
                mode = 2 * pair + which
                if slot == 0:
                    sums[mode] = moved_r[which]
                    sums[modes + mode] = moved_i[which]
                else:
                    sums[mode] += moved_r[which]
                    sums[modes + mode] += moved_i[which]

    def place_slot(slot, carry):
        for plane in range(3):
            part = terms[slot, plane] if plane < 2 else terms[0, 2]
            add_placed(places, slot, part.reshape(tall, 8, length), totals, plane)
        return carry

    lax.fori_loop(0, live, place_slot, 0)


def accumulate(object_map, probes, places, counts, intensity, turns):
    _, modes, length, _ = probes.shape
    slots = intensity.shape[0]
    return pl.pallas_call(
        slots_kernel,
        out_shape=(
            jax.ShapeDtypeStruct((3,) + object_map.shape[1:], jnp.float32),
            jax.ShapeDtypeStruct((2 * modes + 1, length, length), jnp.float32),
        ),
        in_specs=[scalars, scalars] + [memory] * 4,
        out_specs=(memory, memory),
        scratch_shapes=[
            pltpu.VMEM((slots, 2, length, length), jnp.float32),
            pltpu.VMEM((slots, modes // 2, 2 * length, 2 * length), jnp.float32),
            pltpu.VMEM((slots, length, length), jnp.float32),
            pltpu.VMEM((slots, 3, length, length), jnp.float32),
        ],
        compiler_params=pltpu.CompilerParams(vmem_limit_bytes=36 * 1024 * 1024),
        name="slots",
    )(places, counts, object_map, probes, intensity, turns)


def outward_kernel(
    places, counts, object_map, probes, intensity, turns, window, far, power, coverage, lit, light
):
    length = probes.shape[-1]
    live = counts[0]
    lit[...] = jnp.zeros_like(lit)
    light[...] = lighting_of(probes).reshape(light.shape)
    coverage[...] = forward_slots(
        places, live, object_map, probes, intensity, turns, window, far, power
    )

    def place_slot(slot, carry):
        add_placed(places, slot, light[...], lit, 0)
        return carry

    lax.fori_loop(0, live, place_slot, 0)


def outward(object_map, probes, places, counts, intensity, turns):
    _, modes, length, _ = probes.shape
    slots = intensity.shape[0]
    shapes = (
        (slots, 2, length, length),
        (slots, modes // 2, 2 * length, 2 * length),
        (slots, length, length),
        (length, length),
        (1,) + object_map.shape[1:],
    )
    return pl.pallas_call(
        outward_kernel,
        out_shape=tuple(jax.ShapeDtypeStruct(shape, jnp.float32) for shape in shapes),
        in_specs=[scalars, scalars] + [memory] * 4,
        out_specs=(memory,) * 5,
        scratch_shapes=[pltpu.VMEM((length // 8, 8, length), jnp.float32)],
        compiler_params=pltpu.CompilerParams(vmem_limit_bytes=20 * 1024 * 1024),
        name="outward",
    )(places, counts, object_map, probes, intensity, turns)


def window_places(starts, rows, lanes, length, lead):
    rows_at = jnp.clip(starts[:, 0], 0, rows - length)
    cols_at = jnp.clip(starts[:, 1], 0, lanes - length)
    tile = jnp.minimum(rows_at // 8, (rows - length) // 8 - 1)
    shift = rows_at - 8 * tile
    back = (lanes + lead - cols_at) % lanes
    return jnp.stack([tile, back, shift, (8 - shift) % 8], axis=1)


def mixing(probes, probe_step):
    mix_r = jnp.sum(probes[0] * probe_step[0] + probes[1] * probe_step[1], axis=0)
    mix_i = jnp.sum(probes[0] * probe_step[1] - probes[1] * probe_step[0], axis=0)
    return (mix_r, mix_i)


def cross_term(object_map, change, starts, active, mix_r, mix_i):
    length = mix_r.shape[-1]
    anchor_index = jnp.int32(0)

    def cross_visit_slot(running, element):
        corner_at, weight = element
        corner = (anchor_index, corner_at[0], corner_at[1])
        object_win = lax.dynamic_slice(object_map, corner, (2, length, length))
        change_win = lax.dynamic_slice(change, corner, (2, length, length))
        aligned = change_win[0] * object_win[0] + change_win[1] * object_win[1]
        rotated = change_win[0] * object_win[1] - change_win[1] * object_win[0]
        return (running + weight * jnp.sum(aligned * mix_r - rotated * mix_i), None)

    running, _ = lax.scan(cross_visit_slot, jnp.zeros((), jnp.float32), (starts, active))
    return running


def solve_steps(object_curve, cross_curve, probe_curve, object_slope, probe_slope):
    object_diag = 1.1 * object_curve + 0.001
    probe_diag = 1.1 * probe_curve + 0.001
    determinant = object_diag * probe_diag - cross_curve * cross_curve
    object_rate = (probe_diag * object_slope - cross_curve * probe_slope) / determinant
    probe_rate = (object_diag * probe_slope - cross_curve * object_slope) / determinant
    return (object_rate, probe_rate)


def widen(planes, margin):
    return with_halo(planes, (("tx", 1), ("ty", 2)), margin)


def fold_rims(totals, margin, height, breadth):
    middle = totals[:, margin : margin + height, :]
    for direction in (1, -1):
        border = totals[:, margin + height :, :] if direction == 1 else totals[:, :margin, :]
        arrived = from_behind(border, "tx", direction)
        if direction == 1:
            middle = jnp.concatenate([middle + arrived, middle[:, margin:, :]], axis=1)
        else:
            middle = jnp.concatenate([middle[:, : height - margin, :], middle + arrived], axis=1)
    interior = middle[:, :, margin : margin + breadth]
    for direction in (1, -1):
        border = middle[:, :, margin + breadth :] if direction == 1 else middle[:, :, :margin]
        arrived = from_behind(border, "ty", direction)
        if direction == 1:
            interior = jnp.concatenate(
                [interior[:, :, :margin] + arrived, interior[:, :, margin:]], axis=2
            )
        else:
            interior = jnp.concatenate(
                [interior[:, :, : breadth - margin], interior[:, :, breadth - margin :] + arrived],
                axis=2,
            )
    return interior


def general(object_field, probe_modes, positions, counts, intensity):
    length = probe_modes.shape[-1]
    margin = length // 2
    height = object_field.shape[1]
    breadth = object_field.shape[2]
    turns = split_tables(length)
    modes = probe_modes.shape[1]
    anchor = jnp.stack(
        [lax.axis_index("tx") * height - margin, lax.axis_index("ty") * breadth - margin]
    )
    starts = positions - anchor[None, :]
    active = (jnp.arange(positions.shape[0], dtype=jnp.int32) < counts[0]).astype(jnp.float32)
    places = window_places(starts, height + 2 * margin, breadth + 2 * margin, length, 0)
    object_map = object_field
    probes = probe_modes
    extended = widen(object_map, margin)
    for repeat in range(ITERS):
        tiled = extended.reshape(2, -1, 8, extended.shape[-1])
        totals, sums = accumulate(tiled, probes, places, counts, intensity, turns)
        totals = totals.reshape((3,) + extended.shape[1:])
        interior = fold_rims(totals, margin, height, breadth)
        change = interior[:2] / jnp.maximum(interior[2], 1.0)
        object_part = jnp.sum((change[0] * change[0] + change[1] * change[1]) * interior[2])
        slope_part = jnp.sum(interior[:2] * change)
        wide_change = widen(change, margin)
        sums = lax.psum(sums, ("tx", "ty"))
        probe_total = sums[: 2 * modes].reshape(probes.shape)
        weight_total = sums[2 * modes]
        probe_step = probe_total / (weight_total + 1e-05)
        mix_r, mix_i = mixing(probes, probe_step)
        cross_part = cross_term(extended, wide_change, starts, active, mix_r, mix_i)
        object_curve, cross_curve, object_slope = lax.psum(
            (object_part, cross_part, slope_part), ("tx", "ty")
        )
        probe_curve = jnp.sum(
            (probe_step[0] * probe_step[0] + probe_step[1] * probe_step[1]) * weight_total
        )
        probe_slope = jnp.sum(probe_total * probe_step)
        object_rate, probe_rate = solve_steps(
            object_curve, cross_curve, probe_curve, object_slope, probe_slope
        )
        object_map = object_map + object_rate * change
        probes = probes + probe_rate * probe_step
        if repeat + 1 < ITERS:
            extended = extended + object_rate * wide_change
    return (object_map, probes)

outside = pl.BlockSpec(memory_space=pltpu.HBM)
OTHERS = [(i, j) for i in range(4) for j in range(4) if i or j]
AROUND = [(i, j) for i in (-1, 0, 1) for j in (-1, 0, 1) if i or j]
SIDES = [(i, j) for i in (-1, 0, 1) for j in (-1, 1)]


def everyone(row, col):
    return [{"tx": (row + i) % 4, "ty": (col + j) % 4} for i, j in OTHERS]


def greet(peers):
    barrier = pltpu.get_barrier_semaphore()
    for peer in peers:
        pl.semaphore_signal(barrier, 1, device_id=peer, device_id_type=pl.DeviceIdType.MESH)
    pl.semaphore_wait(barrier, len(peers))


class Copies:
    def __init__(self, send, arrive):
        self.send, self.arrive, self.count = (send, arrive, 0)
        self.unsent = []

    def slots(self, number):
        self.count += number
        return self.count - number

    def make(self, source, target, index, landing, peer):
        return pltpu.make_async_remote_copy(
            src_ref=source,
            dst_ref=target,
            send_sem=self.send.at[index],
            recv_sem=self.arrive.at[landing],
            device_id=peer,
            device_id_type=pl.DeviceIdType.MESH,
        )

    def start(self, source, target, peer):
        index = self.slots(1)
        copy = self.make(source, target, index, index, peer)
        copy.start()
        self.unsent.append(copy)
        return copy

    def group(self, items, view):
        index = self.slots(1)
        for source, target, peer in items:
            self.make(source, target, index, index, peer).start()
        whole = self.make(view, view, index, index, items[0][2])
        self.unsent.append(whole)
        return whole

    def finish(self):
        for copy in self.unsent:
            copy.wait_send()
        self.unsent = []


class Ring:
    def __init__(self, copies, row, col, source, target):
        self.copies, self.row, self.col = (copies, row, col)
        self.source, self.target = (source, target)
        self.base = copies.slots(len(AROUND))

    def each(self, what):
        for k, (i, j) in enumerate(AROUND):
            row, col = (self.row + i, self.col + j)
            inside = (row >= 0) & (row < 4) & (col >= 0) & (col < 4)
            pl.when(inside)(functools.partial(what, k, i, j, {"tx": row, "ty": col}))

    def outgoing(self, k, i, j, peer):
        landing = AROUND.index((-i, -j))
        return self.copies.make(
            self.source(i, j), self.target(-i, -j), self.base + k, self.base + landing, peer
        )

    def blank(self):
        for i, j in AROUND:
            row, col = (self.row + i, self.col + j)
            inside = (row >= 0) & (row < 4) & (col >= 0) & (col < 4)
            target = self.target(i, j)

            @pl.when(jnp.logical_not(inside))
            def _():
                target[...] = jnp.zeros(target.shape, jnp.float32)

    def start(self):
        self.each(lambda k, i, j, peer: self.outgoing(k, i, j, peer).start())

    def receive(self):
        def arrived(k, i, j, peer):
            index = self.base + k
            self.copies.make(self.source(i, j), self.target(i, j), index, index, peer).wait_recv()

        self.each(arrived)

    def finish(self):
        self.each(lambda k, i, j, peer: self.outgoing(k, i, j, peer).wait_send())


class Edges:
    def __init__(self, copies, row, col, axis, source, target):
        self.copies, self.axis = (copies, axis)
        self.source, self.target = (source, target)
        self.place = {"tx": row, "ty": col}
        self.base = copies.slots(2)

    def each(self, what, missing=False):
        for k, ahead in ((0, -1), (1, 1)):
            there = self.place[self.axis] + ahead
            inside = (there >= 0) & (there < 4)
            inside = jnp.logical_not(inside) if missing else inside
            peer = {**self.place, self.axis: there}
            pl.when(inside)(functools.partial(what, k, peer))

    def blank(self):
        def clear(k, peer):
            target = self.target(k)
            target[...] = jnp.zeros(target.shape, jnp.float32)

        self.each(clear, missing=True)

    def outgoing(self, k, peer):
        landing = 1 - k
        return self.copies.make(
            self.source(k), self.target(landing), self.base + k, self.base + landing, peer
        )

    def start(self):
        self.each(lambda k, peer: self.outgoing(k, peer).start())

    def receive(self):
        def arrived(k, peer):
            index = self.base + k
            self.copies.make(self.source(k), self.target(k), index, index, peer).wait_recv()

        self.each(arrived)

    def finish(self):
        self.each(lambda k, peer: self.outgoing(k, peer).wait_send())


def early_lanes(value):
    return lax.broadcasted_iota(jnp.int32, value.shape, value.ndim - 1) < value.shape[-1] // 2


def turned(value):
    return pltpu.roll(value, value.shape[-1] // 2, value.ndim - 1)


def pack_first(block):
    half = block.shape[1] // 2
    top, bottom = (block[:, :half], block[:, half:])
    return jnp.where(early_lanes(top), top, turned(bottom))


def pack_last(block):
    half = block.shape[1] // 2
    top, bottom = (block[:, :half], block[:, half:])
    return jnp.where(early_lanes(top), turned(top), bottom)


def unpack(first, last):
    early = early_lanes(first)
    top = jnp.where(early, first, turned(last))
    bottom = jnp.where(early, turned(first), last)
    return jnp.concatenate([top, bottom], axis=1)


def row_range(i, high):
    return slice((i + 1) * high, (i + 2) * high)


def halo_ring(copies, row, col, own, packed, above, beside):
    def source(i, j):
        return own if j == 0 else packed.at[(j + 1) // 2]

    def target(i, j):
        return above.at[(i + 1) // 2] if j == 0 else beside.at[SIDES.index((i, j))]

    return Ring(copies, row, col, source, target)


def spread_halo(own, above, beside, wide):
    high, broad = (own.shape[1], own.shape[-1])
    for i in (-1, 0, 1):
        rows = row_range(i, high)
        wide[:, rows, :, :broad] = own if i == 0 else above[(i + 1) // 2]
        wide[:, rows, :, broad:] = unpack(
            beside[SIDES.index((i, 1))], beside[SIDES.index((i, -1))]
        )


def widen_kernel(
    own_at, probes_at, turns_at, intensity_at, wide, probes, turns, intensity, own, whole, packed, above,
    beside, local, send, arrive,
):
    row, col = (lax.axis_index("tx"), lax.axis_index("ty"))
    peers = everyone(row, col)
    barrier = pltpu.get_barrier_semaphore()
    for peer in peers:
        pl.semaphore_signal(barrier, 1, device_id=peer, device_id_type=pl.DeviceIdType.MESH)
    fetches = [
        pltpu.make_async_copy(source, target, local.at[k])
        for k, (source, target) in enumerate(
            ((own_at, own), (probes_at, probes), (turns_at, turns), (intensity_at, intensity))
        )
    ]
    for fetch in fetches:
        fetch.start()
    copies = Copies(send, arrive)
    ring = halo_ring(copies, row, col, whole, packed, above, beside)
    ring.blank()
    fetches[0].wait()
    block = own[...].reshape(2, own.shape[1] // 8, 8, own.shape[2])
    whole[...] = block
    packed[0] = pack_first(block)
    packed[1] = pack_last(block)
    pl.semaphore_wait(barrier, len(peers))
    ring.start()
    for fetch in fetches[1:]:
        fetch.wait()
    ring.receive()
    spread_halo(block, above, beside, wide)
    ring.finish()


def halo_scratch(high, broad):
    return [
        pltpu.VMEM((2, 2, high // 2, 8, broad), jnp.float32),
        pltpu.VMEM((2, 2, high, 8, broad), jnp.float32),
        pltpu.VMEM((6, 2, high // 2, 8, broad), jnp.float32),
    ]


def widen_tiles(own, probes, turns, intensity):
    two, height, broad = own.shape
    high = height // 8

    def like(value):
        return jax.ShapeDtypeStruct(value.shape, value.dtype)

    return pl.pallas_call(
        widen_kernel,
        out_shape=(
            jax.ShapeDtypeStruct((two, 3 * high, 8, 2 * broad), jnp.float32),
            like(probes),
            like(turns),
            like(intensity),
        ),
        in_specs=[outside] * 4,
        out_specs=(memory,) * 4,
        scratch_shapes=[
            pltpu.VMEM(own.shape, jnp.float32),
            pltpu.VMEM((two, high, 8, broad), jnp.float32),
        ]
        + halo_scratch(high, broad)
        + [
            pltpu.SemaphoreType.DMA((4,)),
            pltpu.SemaphoreType.DMA((8,)),
            pltpu.SemaphoreType.DMA((8,)),
        ],
        compiler_params=pltpu.CompilerParams(
            collective_id=0, has_side_effects=True, vmem_limit_bytes=51300 * 1024
        ),
        name="widen",
    )(own, probes, turns, intensity)


def in_rows(values, lanes):
    at = lax.broadcasted_iota(jnp.int32, (8, lanes), 0)
    result = jnp.zeros((8, lanes), jnp.float32)
    for place, value in enumerate(values):
        result = jnp.where(at == place, value, result)
    return result


def settle_kernel(
    last, places, weights, object_map, probes, turns, window, far, power, coverage, lit, *rest
):
    if last:
        got, change_own, rates_out = rest[:3]
    else:
        new_map, new_probes, got = rest[:3]
    (
        sums, terms, padded, totals, fold_out, fold_in, upright, over, column, near_out, near, r1,
        acc, r2, acca, r3, accb, r4, wide, held, mix, mine, pair_in, ours, inbox, send, arrive,
    ) = rest[3:]
    row, col = (lax.axis_index("tx"), lax.axis_index("ty"))
    core, side, upper, lower_bit = (col % 2, col // 2, row // 2, row % 2)
    rows, broad = (column.shape[1], column.shape[-1])
    high = rows // 3
    tall, length = (2 * high, power.shape[-1])
    slots = places.shape[0]
    modes = probes.shape[1]
    pairs = modes // 2
    blocks = got.shape[1:]
    middle = slice(high, 2 * high)
    ends = (slice(0, high), slice(2 * high, 3 * high))
    peers = everyone(row, col)
    partner = {"tx": row, "ty": side * 2 + (1 - core)}
    across = {"tx": row, "ty": (1 - side) * 2 + core}
    beside = {"tx": row + 1 - 2 * lower_bit, "ty": col}
    beyond = {"tx": (row + 2) % 4, "ty": col}
    chips = [
        {"tx": (row + i) % 4, "ty": ((side + j) % 2) * 2 + core}
        for i in range(4)
        for j in range(2)
        if i or j
    ]
    copies = Copies(send, arrive)
    spot = (core, side, upper, lower_bit)

    barrier = pltpu.get_barrier_semaphore()
    for peer in peers:
        pl.semaphore_signal(barrier, 1, device_id=peer, device_id_type=pl.DeviceIdType.MESH)

    def edges(axis, source, target):
        made = Edges(copies, row, col, axis, source, target)
        made.blank()
        return made

    fold_side = edges("ty", lambda k: fold_out.at[k], lambda k: fold_in.at[k])
    fold_over = edges("tx", lambda k: upright.at[:, ends[k]], lambda k: over.at[k])
    halo_over = edges("tx", lambda k: column.at[:, middle], lambda k: column.at[:, ends[k]])
    halo_side = edges("ty", lambda k: near_out.at[k], lambda k: near.at[k])
    padded[...] = jnp.zeros_like(padded)
    totals[:2] = jnp.zeros((2,) + totals.shape[1:], jnp.float32)
    totals[2] = lit[0]

    def probes_of(mode):
        return tuple(probes[part, mode].reshape(length, length) for part in range(2))

    def compute(pair):
        base = 1 + 4 * pair
        for slot in range(slots):
            moved_r, moved_i = backward_slot(
                slot, pair, probes_of, turns, window, far, power, terms
            )
            for n, value in enumerate(moved_r + moved_i):
                value = value.reshape(blocks)
                if slot == 0:
                    sums[base + n] = value
                else:
                    sums[base + n] += value

    def chunk(n):
        return slice(1 + 4 * n if n else 0, 5 + 4 * n)

    def planes(n):
        return slice(4 * n, 4 * n + 4)

    shared = {}
    moving = {}

    def core_sum(n):
        part = chunk(n)
        moving[n] = copies.start(sums.at[part, 1 - core], r1.at[part], partner)

    def across_sum(n):
        part = chunk(n)
        moving[n].wait_recv()
        acc[part] = sums[part, core] + r1[part]
        moving[n] = copies.start(acc.at[part, 1 - side], r2.at[part], across)

    def beside_sum(n):
        part = chunk(n)
        moving[n].wait_recv()
        acca[part] = acc[part, side] + r2[part]
        moving[n] = copies.start(acca.at[part, :, 1 - lower_bit], r3.at[part], beside)

    def beyond_sum(n):
        part = chunk(n)
        moving[n].wait_recv()
        accb[part] = acca[part, :, lower_bit] + r3[part]
        moving[n] = copies.start(accb.at[part, 1 - upper], r4.at[part], beyond)

    def give(n, block, peer):
        moving[n] = copies.start(block, block, peer)

    def slab(n):
        part = chunk(n)
        moving[n].wait_recv()
        total = accb[part, upper] + r4[part]
        if n == 0:
            shared["weight"] = total[0]
            total = total[1:]
        weight = shared["weight"]
        found = total / (weight + 1e-05)
        got[(planes(n),) + spot] = found
        give(n, got.at[(planes(n),) + spot], beyond)
        some = slice(2 * n, 2 * n + 2)
        probe_r, probe_i = (probes[(0, some) + spot], probes[(1, some) + spot])
        for name, value in (
            ("mix_r", probe_r * found[:2] + probe_i * found[2:]),
            ("mix_i", probe_r * found[2:] - probe_i * found[:2]),
            ("curve", found * found * weight),
            ("slope", total * found),
        ):
            value = jnp.sum(value, axis=0)
            shared[name] = value if n == 0 else shared[name] + value

    def beside_give(n):
        moving[n].wait_recv()
        give(n, got.at[planes(n), core, side, :, lower_bit], beside)

    def across_give(n):
        moving[n].wait_recv()
        give(n, got.at[planes(n), core, side], across)

    def core_give(n):
        moving[n].wait_recv()
        give(n, got.at[planes(n), core], partner)

    sums[0] = coverage[...].reshape(blocks)
    compute(0)
    pl.semaphore_wait(barrier, len(peers))
    core_sum(0)
    compute(1)
    core_sum(1)
    across_sum(0)
    compute(2)
    core_sum(2)
    across_sum(1)
    compute(3)
    core_sum(3)
    across_sum(2)
    beside_sum(0)

    for slot in range(slots):
        tile, back, shift = (places[slot, n] for n in range(3))
        onward = lax.rem(2 * broad - back, 2 * broad)
        for plane in range(2):
            keep = padded.at[slot % 2, plane]
            keep[high : high + tall + 1] = lower(terms[slot, plane].reshape(tall, 8, length), shift)
            part = padded[slot % 2, plane, pl.ds(high - tile, 3 * high)]
            totals[plane] += broaden(part, onward, 2 * broad)
    rim = totals[:, :, :, broad:]
    fold_out[0] = pack_last(rim)
    fold_out[1] = pack_first(rim)
    fold_side.start()
    across_sum(3)
    beside_sum(1)
    beyond_sum(0)
    beside_sum(2)

    fold_side.receive()
    upright[...] = totals[:, :, :, :broad] + unpack(fold_in[0], fold_in[1])
    fold_over.start()
    beyond_sum(1)
    beside_sum(3)
    slab(0)
    beyond_sum(2)
    slab(1)
    beyond_sum(3)

    fold_over.receive()
    interior = upright[:, middle] + over[0] + over[1]
    moved = interior[:2] / jnp.maximum(interior[2], 1.0)
    column[:, middle] = moved
    halo_over.start()
    beside_give(0)
    slab(2)
    slab(3)
    mix[(0,) + spot] = shared["mix_r"]
    mix[(1,) + spot] = shared["mix_i"]
    block = mix.at[(slice(None),) + spot]
    mixes = [copies.start(block, block, peer) for peer in chips]
    beside_give(1)
    curve = jnp.sum((moved[0] * moved[0] + moved[1] * moved[1]) * interior[2])
    slope = jnp.sum(interior[:2] * moved)
    probe_curve = jnp.sum(shared["curve"])
    probe_slope = jnp.sum(shared["slope"])

    halo_over.receive()
    near_out[0] = pack_first(column[...])
    near_out[1] = pack_last(column[...])
    halo_side.start()
    across_give(0)
    beside_give(2)
    across_give(1)
    beside_give(3)
    wide[:, :, :, :broad] = column[...]

    halo_side.receive()
    wide[:, :, :, broad:] = unpack(near[1], near[0])
    held[0] = wide[0] * object_map[0] + wide[1] * object_map[1]
    held[1] = wide[0] * object_map[1] - wide[1] * object_map[0]
    gathered = []
    for plane in range(2):
        running = jnp.zeros((tall, 8, broad), jnp.float32)
        for slot in range(slots):
            running += weights[slot] * cut_window(places, slot, held, plane, length)
        gathered.append(running)
    for copy in mixes:
        copy.wait_recv()
    block = mix.at[:, core]
    mix_pass = copies.start(block, block, partner)
    core_give(0)
    across_give(2)
    across_give(3)
    mix_pass.wait_recv()
    mix_all = mix[...].reshape(2, tall, 8, broad)
    cross = jnp.sum(gathered[0] * mix_all[0] - gathered[1] * mix_all[1])
    mine[...] = in_rows((curve, slope, probe_curve, probe_slope, cross), broad)
    pair_sent = copies.start(mine, pair_in, partner)
    core_give(1)
    pair_sent.wait_recv()
    ours[...] = mine[...] + pair_in[...]
    scalars_sent = copies.group([(ours, inbox.at[k], peer) for k, peer in enumerate(chips)], inbox)
    core_give(2)
    core_give(3)
    copies.finish()
    for made in (fold_side, fold_over, halo_over, halo_side):
        made.finish()
    for n in range(pairs):
        moving[n].wait_recv()
    scalars_sent.wait_recv()
    sent = ours[...] + jnp.sum(inbox[...], axis=0)
    object_rate, probe_rate = solve_steps(
        sent[0:1], sent[4:5], sent[2:3], sent[1:2], sent[3:4]
    )
    object_rate = jnp.broadcast_to(object_rate, (8, broad))
    probe_rate = jnp.broadcast_to(probe_rate, (8, broad))
    if last:
        at = lax.broadcasted_iota(jnp.int32, (8, broad), 0)
        rates_out[...] = jnp.where(at == 0, object_rate, probe_rate)
        change_own[...] = column[:, middle]
    else:
        both = jnp.concatenate([object_rate, object_rate], axis=1)
        new_map[...] = object_map[...] + both * wide[...]
        for n in range(pairs):
            some = slice(2 * n, 2 * n + 2)
            for part in range(2):
                first = 4 * n + 2 * part
                new_probes[part, some] = probes[part, some] + probe_rate * got[first : first + 2]


def settle(last, places, weights, object_map, probes, turns, spread):
    _, rows, _, lanes = object_map.shape
    modes, length = (probes.shape[1], probes.shape[-1])
    slots = places.shape[0]
    planes = 2 * modes
    high, broad = (rows // 3, lanes // 2)
    f32 = jnp.float32
    grid = (2, 2, 2, 2)
    step = jax.ShapeDtypeStruct((planes,) + grid + (8, length), f32)
    if last:
        out_shape = (
            step,
            jax.ShapeDtypeStruct((2, high, 8, broad), f32),
            jax.ShapeDtypeStruct((8, broad), f32),
        )
    else:
        out_shape = (
            jax.ShapeDtypeStruct(object_map.shape, f32),
            jax.ShapeDtypeStruct((2, modes) + grid + (8, length), f32),
            step,
        )
    scratch = [
        (planes + 1,) + grid + (8, length),
        (slots, 2, length, length),
        (2, 2, 4 * high + 1, 8, length),
        (3, rows, 8, lanes),
        (2, 3, rows // 2, 8, broad),
        (2, 3, rows // 2, 8, broad),
        (3, rows, 8, broad),
        (2, 3, high, 8, broad),
        (2, rows, 8, broad),
        (2, 2, rows // 2, 8, broad),
        (2, 2, rows // 2, 8, broad),
        (planes + 1, 2, 2, 2, 8, length),
        (planes + 1, 2, 2, 2, 8, length),
        (planes + 1, 2, 2, 8, length),
        (planes + 1, 2, 2, 8, length),
        (planes + 1, 2, 8, length),
        (planes + 1, 2, 8, length),
        (planes + 1, 8, length),
        (2, rows, 8, lanes),
        (2, rows, 8, lanes),
        (2,) + grid + (8, length),
        (8, broad),
        (8, broad),
        (8, broad),
        (7, 8, broad),
    ]
    return pl.pallas_call(
        functools.partial(settle_kernel, last),
        out_shape=out_shape,
        in_specs=[scalars, scalars] + [memory] * 8,
        out_specs=(memory,) * 3,
        scratch_shapes=[pltpu.VMEM(shape, f32) for shape in scratch]
        + [pltpu.SemaphoreType.DMA((52,)), pltpu.SemaphoreType.DMA((52,))],
        compiler_params=pltpu.CompilerParams(
            collective_id=2 if last else 1,
            has_side_effects=True,
            vmem_limit_bytes=28 * 1024 * 1024,
        ),
        name="finish" if last else "settle",
    )(
        places,
        weights,
        object_map,
        probes.reshape((2, modes) + grid + (8, length)),
        turns,
        *spread,
    )


def apply_kernel(object_map, change, probes, step, rates, object_at, probes_at, tile, fresh, done):
    modes = probes.shape[1]
    high, broad = (change.shape[1], change.shape[3])
    object_rate = jnp.broadcast_to(rates[0:1], (8, broad))
    probe_rate = jnp.broadcast_to(rates[1:2], (8, broad))
    copies = []
    for part in range(2):
        for first in range(0, modes, 4):
            some = slice(first, first + 4)
            base = 2 * (first + part)
            stepped = jnp.concatenate(
                [step[base : base + 2], step[base + 4 : base + 6]], axis=0
            )
            moved = probes[part, some] + probe_rate * stepped
            fresh[part, some] = moved.reshape((4,) + fresh.shape[2:])
            block = (part, pl.ds(first, 4))
            copies.append(
                pltpu.make_async_copy(fresh.at[block], probes_at.at[block], done.at[len(copies)])
            )
            copies[-1].start()
    moved = object_map[:, high : 2 * high, :, :broad] + object_rate * change[...]
    tile[...] = moved.reshape(tile.shape)
    copies.append(pltpu.make_async_copy(tile, object_at, done.at[len(copies)]))
    copies[-1].start()
    for copy in copies:
        copy.wait()


def apply(object_map, change, probes, step, rates):
    _, high, _, broad = change.shape
    modes, length = (probes.shape[1], probes.shape[-1])
    shapes = ((2, 8 * high, broad), (2, modes, length, length))
    blocks = (2, modes, length // 8, 8, length)
    return pl.pallas_call(
        apply_kernel,
        out_shape=tuple(jax.ShapeDtypeStruct(shape, jnp.float32) for shape in shapes),
        in_specs=[memory] * 5,
        out_specs=(outside,) * 2,
        scratch_shapes=[pltpu.VMEM(shape, jnp.float32) for shape in shapes]
        + [pltpu.SemaphoreType.DMA((modes // 2 + 1,))],
        compiler_params=pltpu.CompilerParams(vmem_limit_bytes=8 * 1024 * 1024),
        name="apply",
    )(
        object_map,
        change,
        probes.reshape(blocks),
        step.reshape((2 * modes,) + blocks[2:]),
        rates,
    )


def direct(object_field, probe_modes, positions, counts, intensity):
    two, modes, length, _ = probe_modes.shape
    margin = length // 2
    _, height, breadth = object_field.shape
    anchor = jnp.stack(
        [lax.axis_index("tx") * height - margin, lax.axis_index("ty") * breadth - margin]
    )
    starts = positions - anchor[None, :]
    lanes = 2 * breadth
    places = window_places(starts, height + 2 * margin, lanes, length, margin)
    weights = (jnp.arange(positions.shape[0], dtype=jnp.int32) < counts[0]).astype(jnp.float32)
    object_map, probes, turns, measured = widen_tiles(
        object_field,
        probe_modes,
        jnp.asarray(split_tables(length)),
        intensity,
    )
    for repeat in range(ITERS):
        spread = outward(object_map, probes, places, counts, measured, turns)
        last = repeat + 1 == ITERS
        settled = settle(last, places, weights, object_map, probes, turns, spread)
        if not last:
            object_map, probes, _ = settled
            probes = probes.reshape(probe_modes.shape)
    step, change, rates = settled
    return apply(object_map, change, probes, step, rates)


def shards(object_field, probe_modes, positions, counts, intensity):
    _, height, breadth = object_field.shape
    length = probe_modes.shape[-1]
    grid = (lax.axis_size("tx"), lax.axis_size("ty"))
    arguments = (object_field, probe_modes, positions, counts, intensity)
    if grid == (4, 4) and length == 128 and (2 * height, breadth) == (length, length):
        return direct(*arguments)
    return general(*arguments)


def solution(mesh):
    return jax.shard_map(
        shards,
        mesh=mesh,
        in_specs=(
            P("groups", "tx", "ty"),
            P("groups", None, None, None),
            P(("groups", "tx", "ty"), None),
            P(("groups", "tx", "ty")),
            P(("groups", "tx", "ty"), None, None),
        ),
        out_specs=(P("groups", "tx", "ty"), P("groups", None, None, None)),
        check_vma=False,
    )
```
